32 devices in a mesh: dp: 4 (over x, core), seq: 4 (over z), mp: 2 (over y).
Axes of the slice: x: 2, y: 2, z: 4, core: 2. Of those that a mesh axis runs over, the one named last changes fastest.
Arguments:
- block_input: bfloat16 [2, 4096, 1536], P(None, ('dp', 'seq', 'mp')), may hold values from -6 to 6
- segment: int32 [2, 4, 1024], P(None, 'dp'), may hold values from 0 to 3, never falling along the last dimension, each value on 1 to 512 neighbouring positions
- norm1_gain: float32 [1536], replicated, may hold values from 0.5 to 1.5
- w_qkv: bfloat16 [1536, 3, 1536], P(None, None, 'mp'), may hold values from -0.15625 to 0.15625
- conv_kernel: float32 [16, 6, 11], P('mp'), may hold values from -1.5 to 1.5
- head_mix: float32 [16, 2], P('mp'), may hold values from 0.25 to 1
- out_gain: float32 [1536], P('mp'), may hold values from 0.5 to 1.5
- w_out: bfloat16 [1536, 1536], P('mp'), may hold values from -0.15625 to 0.15625
- norm2_gain: float32 [1536], replicated, may hold values from 0.5 to 1.5
- w_in: bfloat16 [1536, 2, 4096], P(None, None, 'mp'), may hold values from -0.15625 to 0.15625
- w_down: bfloat16 [4096, 1536], P('mp'), may hold values from -0.125 to 0.125
- grad_y: bfloat16 [2, 4096, 1536], P(None, ('dp', 'seq', 'mp')), may hold values from -6 to 6
Outputs:
- block_output: bfloat16 [2, 4096, 1536], P(None, ('dp', 'seq', 'mp'))
- grad_x: float32 [2, 4096, 1536], P(None, ('dp', 'seq', 'mp'))
- grad_norm1: float32 [1536], replicated
- grad_qkv: float32 [1536, 3, 1536], P(None, None, 'mp')
- grad_kernel: float32 [16, 6, 11], P('mp')
- grad_mix: float32 [16, 2], P('mp')
- grad_out_gain: float32 [1536], P('mp')
- grad_out: float32 [1536, 1536], P('mp')
- grad_norm2: float32 [1536], replicated
- grad_in: float32 [1536, 2, 4096], P(None, None, 'mp')
- grad_down: float32 [4096, 1536], P('mp')
The draws below stay inside these ranges and needn't reach their ends.
Inputs may be any that keep to these rules, and one draw needn't show every extreme that they name: `segment`: ids never fall along a group, each document spans 1 to 512 tokens, and one spans exactly 512.
All inputs are finite; a program needn't handle non-finite values.
Results may differ from the reference program's by a relative error of at most 0.024.
Values may be sent and summed in bfloat16 or wider, within the bound.
A program may use at most 320 MiB of HBM per device.

```python
import math
import jax
import jax.numpy as jnp
import numpy as np
from jax import lax

D = 1536
HEADS = 16
HEAD = 96
FF = 4096
QTAPS = 6
KTAPS = 11
GROUPS_DEV = 2
GROUP = 1024
TOKENS = 4096
DOCS = 4
LONGEST = 512
N_DP = 4


def level_of(stream_key, dims, cuts, smallest, top_value):
    gain = 1.0
    for axis_at, shards_of in cuts:
        steps = jax.random.uniform(jax.random.fold_in(jax.random.fold_in(stream_key, 6), axis_at), (shards_of,), jnp.float32, smallest / len(cuts), top_value / len(cuts))
        gain = gain * jnp.repeat(jnp.exp(steps), dims[axis_at] // shards_of).reshape((-1,) + (1,) * (len(dims) - 1 - axis_at))
    return gain


def profile(count, total, most, skew):
    portions = [(1 << 20) // math.isqrt(rank ** skew) + 1 for rank in range(2, count + 1)]
    spare, holding = total - most - (count - 1), [1] * (count - 1)
    while spare > 0:
        free = [i for i in range(count - 1) if holding[i] < most]
        pool, remaining = sum([portions[i] for i in free]), spare
        for i in free:
            more = min(most - holding[i], max(1, remaining * portions[i] // pool), spare)
            holding[i] = holding[i] + more
            spare = spare - more
    return np.array([most] + holding)


def uneven_parts(key, count, total, bound, skew):
    if count == 2:
        one = jax.random.randint(key, (), max(1, total - bound), min(bound, total - 1) + 1)
        return jnp.stack([one, total - one])
    tallies = jnp.asarray(profile(count, total, bound, skew), jnp.int32)
    pairs = (count - 1) // 2
    donor, receiver = tallies[1:1 + 2 * pairs:2], tallies[2:2 + 2 * pairs:2]
    room = jnp.minimum(donor - 1, bound - receiver)
    moved = jax.random.randint(jax.random.fold_in(key, 1), (pairs,), 0, 1 << 20) % (room + 1)
    tallies = tallies.at[1:1 + 2 * pairs:2].set(donor - moved).at[2:2 + 2 * pairs:2].set(receiver + moved)
    return tallies[jax.random.permutation(jax.random.fold_in(key, 2), count)]


def centred(rng, dims, spread, most, shards=(), kind=jnp.bfloat16):
    array = spread * jax.random.normal(rng, dims, jnp.float32)
    if shards:
        array = array * level_of(rng, dims, shards, -0.22, 0.18)
    return jnp.clip(array, -most, most).astype(kind)


def setup_inputs(seed: int = 0) -> dict:
    key_of = jax.random.split(jax.random.key(seed), 13)
    block_input = centred(key_of[0], (GROUPS_DEV, TOKENS, D), 1.0, 6.0, ((1, 32),))
    segment = jax.vmap(lambda own: jnp.searchsorted(jnp.cumsum(uneven_parts(own, DOCS, GROUP, LONGEST, 2)), jnp.arange(GROUP), side="right"))(jax.random.split(key_of[1], GROUPS_DEV * N_DP)).reshape((GROUPS_DEV, N_DP, GROUP)).astype(jnp.int32)
    norm1_gain = jnp.clip(1.0 + 0.1 * jax.random.normal(key_of[2], (D,), jnp.float32), 0.5, 1.5)
    w_qkv = centred(key_of[3], (D, 3, D), D ** -0.5, 0.15625, ((2, 2),))
    conv_kernel = centred(key_of[4], (HEADS, QTAPS, KTAPS), 0.25, 1.5, ((0, 2),), jnp.float32)
    head_mix = jnp.clip(0.25 + 0.75 * jax.random.uniform(key_of[5], (HEADS, 2), jnp.float32) ** level_of(key_of[5], (HEADS, 2), ((0, 2),), -0.2, 0.2), 0.25, 1.0)
    out_gain = jnp.clip(1.0 + 0.1 * jax.random.normal(key_of[6], (D,), jnp.float32), 0.5, 1.5)
    w_out = centred(key_of[7], (D, D), D ** -0.5, 0.15625, ((0, 2),))
    norm2_gain = jnp.clip(1.0 + 0.1 * jax.random.normal(key_of[8], (D,), jnp.float32), 0.5, 1.5)
    w_in = centred(key_of[9], (D, 2, FF), D ** -0.5, 0.15625, ((2, 2),))
    w_down = centred(key_of[10], (FF, D), (FF // 2) ** -0.5, 0.125, ((0, 2),))
    grad_y = centred(key_of[11], (GROUPS_DEV, TOKENS, D), 1.0, 6.0, ((1, 32),))
    return dict(block_input=block_input, segment=segment, norm1_gain=norm1_gain, w_qkv=w_qkv, conv_kernel=conv_kernel, head_mix=head_mix, out_gain=out_gain, w_out=w_out, norm2_gain=norm2_gain, w_in=w_in, w_down=w_down, grad_y=grad_y)


epsilon = 1e-05
block_limit = 512
highest = lax.Precision.HIGHEST

@jax.custom_vjp
def low(v):
    return lax.optimization_barrier(v.astype(jnp.bfloat16)).astype(jnp.float32)

@jax.custom_vjp
def low_back(v):
    return v

def low_keep(v):
    return (low(v), None)

def low_pass(kept, grad):
    return (grad,)

def back_keep(v):
    return (v, None)

def back_low(kept, grad):
    return (low(grad),)
low.defvjp(low_keep, low_pass)
low_back.defvjp(back_keep, back_low)

def rounded_both(values):
    return low_back(low(values))

def normalize(values):
    return values * lax.rsqrt(lax.optimization_barrier(jnp.mean(values * values, axis=-1, keepdims=True)) + epsilon)

def convolve(maps, kernel, out_rows, width):
    rim_rows = QTAPS - 1
    half_keys = KTAPS // 2
    padded = jnp.pad(maps, ((0, 0), (0, 0), (half_keys, half_keys)))
    running = jnp.zeros((maps.shape[0], out_rows, width), jnp.float32)
    for query_tap in range(QTAPS):
        for key_tap in range(KTAPS):
            window = padded[:, rim_rows - query_tap:rim_rows - query_tap + out_rows, KTAPS - 1 - key_tap:KTAPS - 1 - key_tap + width]
            running = running + kernel[:, query_tap, key_tap][:, None, None] * window
    return running

def mix_heads(probs, mixing):
    groups = probs.shape[0] // 2
    pairs = probs.reshape((groups, 2) + probs.shape[1:])
    mix_three = mixing.reshape(groups, 2, 2)
    mixed = mix_three[:, :, 0, None, None] * pairs[:, 0:1] + mix_three[:, :, 1, None, None] * pairs[:, 1:2]
    return mixed.reshape(probs.shape)

def attention_group(queries, keys, values, seg_ids, kernel, mixing):
    rim_rows = QTAPS - 1
    block_rows = min(block_limit, GROUP)
    block_count = GROUP // block_rows
    query_pad = jnp.concatenate([jnp.zeros((rim_rows, D), jnp.float32), queries])
    seg_pad = jnp.concatenate([jnp.zeros((rim_rows,), jnp.int32), seg_ids])
    key_heads = keys.reshape(GROUP, HEADS, HEAD)
    value_heads = values.reshape(GROUP, HEADS, HEAD)
    key_pos = jnp.arange(GROUP, dtype=jnp.int32)

    def one_block(block_index):
        first_row = (block_index * block_rows).astype(jnp.int32)
        query_ext = lax.dynamic_slice_in_dim(query_pad, first_row, block_rows + rim_rows, 0).reshape(block_rows + rim_rows, HEADS, HEAD)
        ext_seg = lax.dynamic_slice_in_dim(seg_pad, first_row, block_rows + rim_rows, 0)
        ext_pos = first_row - rim_rows + jnp.arange(block_rows + rim_rows, dtype=jnp.int32)
        valid = (key_pos[None, :] <= ext_pos[:, None]) & (ext_pos[:, None] >= 0) & (seg_ids[None, :] == ext_seg[:, None])
        scores = low_back(jnp.einsum('rhd,khd->hrk', query_ext, key_heads, precision=highest) * HEAD ** (-0.5))
        maps = jnp.where(valid[None], scores, 0.0)
        logits = jnp.where(valid[None, rim_rows:], convolve(maps, kernel, block_rows, GROUP), -jnp.inf)
        row_max = lax.optimization_barrier(jnp.max(logits, axis=-1, keepdims=True))
        powers = jnp.exp(logits - row_max)
        probs = powers / lax.optimization_barrier(jnp.sum(powers, axis=-1, keepdims=True))
        mixed = low(mix_heads(probs, mixing))
        return jnp.einsum('hrk,khd->rhd', mixed, value_heads, precision=highest)
    outputs = lax.map(jax.checkpoint(one_block), jnp.arange(block_count, dtype=jnp.int32))
    return outputs.reshape(GROUP, HEADS, HEAD)

def block_layer(rows_in, seg_ids, gain_one, weight_qkv, kernel, mixing, gain_head, weight_out, gain_two, weight_in, weight_down):
    normed_one = low(normalize(rows_in) * gain_one)
    projected = jnp.einsum('rd,dtc->rtc', normed_one, weight_qkv, precision=highest)
    queries = rounded_both(projected[:, 0])
    keys = rounded_both(projected[:, 1])
    values = rounded_both(projected[:, 2])
    attended = low_back(attention_group(queries, keys, values, seg_ids, kernel, mixing))
    grouped = normalize(attended) * gain_head.reshape(HEADS, HEAD)
    mixed_out = low(grouped.reshape(GROUP, D))
    branch = low_back(jnp.dot(mixed_out, weight_out, precision=highest))
    resid = rows_in + branch
    normed_two = low(normalize(resid) * gain_two)
    gate_up = jnp.einsum('rd,dtf->rtf', normed_two, weight_in, precision=highest)
    gate = low_back(gate_up[:, 0])
    upward = low_back(gate_up[:, 1])
    hidden = low(jax.nn.silu(gate) * upward)
    return resid + low_back(jnp.dot(hidden, weight_down, precision=highest))

def reference(block_input, segment, norm1_gain, w_qkv, conv_kernel, head_mix, out_gain, w_out, norm2_gain, w_in, w_down, grad_y):
    params = (block_input.astype(jnp.float32), norm1_gain, w_qkv.astype(jnp.float32), conv_kernel, head_mix, out_gain, w_out.astype(jnp.float32), norm2_gain, w_in.astype(jnp.float32), w_down.astype(jnp.float32))
    seg_all = segment.reshape(GROUPS_DEV * N_DP, GROUP)

    def forward(rows_all, gain_one, weight_qkv, kernel, mixing, gain_head, weight_out, gain_two, weight_in, weight_down):
        groups_in = rows_all.reshape(GROUPS_DEV * N_DP, GROUP, D)

        def step(carry, item):
            group_rows, seg_ids = item
            result = block_layer(group_rows, seg_ids, gain_one, weight_qkv, kernel, mixing, gain_head, weight_out, gain_two, weight_in, weight_down)
            return (carry, result)
        unused, outputs = lax.scan(step, jnp.zeros((), jnp.float32), (groups_in, seg_all))
        return outputs.reshape(GROUPS_DEV, N_DP * GROUP, D)
    output, pullback = jax.vjp(forward, *params)
    grads = pullback(grad_y.astype(jnp.float32))
    return (output.astype(jnp.bfloat16), grads[0], grads[1], grads[2], grads[3], grads[4], grads[5], grads[6], grads[7], grads[8], grads[9])
```

```python
import functools
import math

import jax
import jax.numpy as jnp
from jax import lax
from jax.experimental import pallas as pl
from jax.experimental.pallas import tpu as pltpu
from jax.sharding import PartitionSpec as P

QTAPS = 6
KTAPS = 11
LONGEST = 512
RIM = QTAPS - 1
HALF = KTAPS // 2
TILE = 256
OWN = TILE - 2 * HALF
LANES = 16

epsilon = 1e-05
VMEM_LIMIT = 58 * 1024 * 1024


def from_behind(value, axis, steps):
    count = lax.axis_size(axis)
    first, last = (max(0, -steps), min(count, count - steps))
    return lax.ppermute(value, axis, [(source, source + steps) for source in range(first, last)])


def inverse_rms(values):
    return lax.rsqrt(jnp.mean(values * values, axis=-1, keepdims=True) + epsilon)


def norm_back(upstream, normed, inverse, gain):
    scaled = upstream * gain
    return inverse * (scaled - normed * jnp.mean(scaled * normed, axis=-1, keepdims=True))


def tile_widths(window):
    widths, left = [], window
    while left > 0:
        width = TILE
        while width > 128 and left <= width // 2 - 2 * HALF:
            width //= 2
        widths.append(width)
        left -= width - 2 * HALF
    return widths


def tile_starts(window):
    starts, at = [], 0
    for width in tile_widths(window):
        starts.append(at)
        at += width - 2 * HALF
    return starts


def spread_keys(array, axis, fill=0):
    window = array.shape[axis]
    widths, starts = tile_widths(window), tile_starts(window)
    pads = [(0, 0)] * array.ndim
    pads[axis] = (HALF, starts[-1] + widths[-1] - HALF - window)
    padded = jnp.pad(array, pads, constant_values=fill)
    return jnp.concatenate(
        [lax.slice_in_dim(padded, s, s + w, axis=axis) for s, w in zip(starts, widths)], axis=axis
    )


def collect_keys(array, axis, window):
    widths, starts = tile_widths(window), tile_starts(window)
    length = starts[-1] + widths[-1]
    total, at = 0.0, 0
    for s, w in zip(starts, widths):
        pads = [(0, 0)] * array.ndim
        pads[axis] = (s, length - s - w)
        total = total + jnp.pad(lax.slice_in_dim(array, at, at + w, axis=axis), pads)
        at += w
    return lax.slice_in_dim(total, HALF, HALF + window, axis=axis)


def own_columns(window):
    own = []
    for s, w in zip(tile_starts(window), tile_widths(window)):
        own += [HALF <= c < w - HALF and s + c - HALF < window for c in range(w)]
    return own


def spread_rows(rim, rows):
    steps = rows.shape[0] // LANES
    rest = rows.shape[1:]
    ahead = jnp.zeros((steps - RIM,) + rest, rows.dtype)
    blocks = jnp.concatenate([ahead, rim.astype(rows.dtype), rows]).reshape((LANES + 1, steps) + rest)
    ext = jnp.concatenate([blocks[:LANES, steps - RIM :], blocks[1:]], axis=1)
    return jnp.swapaxes(ext, 0, 1).reshape(((steps + RIM) * LANES,) + rest)


def spread_plain(rows):
    steps = rows.shape[0] // LANES
    rest = rows.shape[1:]
    return jnp.swapaxes(rows.reshape((LANES, steps) + rest), 0, 1).reshape(rows.shape)


def collect_plain(rows):
    steps = rows.shape[0] // LANES
    rest = rows.shape[1:]
    return jnp.swapaxes(rows.reshape((steps, LANES) + rest), 0, 1).reshape(rows.shape)


def collect_rows(ext):
    steps = ext.shape[0] // LANES - RIM
    rest = ext.shape[1:]
    blocks = jnp.swapaxes(ext.reshape((steps + RIM, LANES) + rest), 0, 1)
    early, main = blocks[:, :RIM], blocks[:, RIM:]
    main = main.reshape((LANES * steps,) + rest)
    shifted = jnp.pad(early[1:], [(0, 1), (steps - RIM, 0)] + [(0, 0)] * len(rest))
    return early[0], main + shifted.reshape((LANES * steps,) + rest)


def taps_kernel(fwd_ref, bwd_ref, t_ref, tt_ref):
    for source, target in ((fwd_ref, t_ref), (bwd_ref, tt_ref)):
        for a in range(QTAPS):
            row = jnp.broadcast_to(source[0, a : a + 1, :], (TILE, TILE))
            turned = pltpu.roll(row, 0, 1, stride=1, stride_axis=0)
            target[0, a * TILE : (a + 1) * TILE, :] = turned.astype(jnp.bfloat16)


def band_matrices(conv_kernel, scale):
    heads = conv_kernel.shape[0]
    taps = conv_kernel * scale
    gap = jnp.zeros((heads, QTAPS, TILE - KTAPS), jnp.float32)
    fwd = jnp.concatenate([taps[:, :, HALF:], gap, taps[:, :, :HALF]], axis=2)
    flipped = taps[:, :, ::-1]
    bwd = jnp.concatenate([flipped[:, :, HALF:], gap, flipped[:, :, :HALF]], axis=2)
    big = jax.ShapeDtypeStruct((heads, QTAPS * TILE, TILE), jnp.bfloat16)
    small_spec = pl.BlockSpec((1, QTAPS, TILE), lambda h: (h, 0, 0))
    big_spec = pl.BlockSpec((1, QTAPS * TILE, TILE), lambda h: (h, 0, 0))
    return pl.pallas_call(
        taps_kernel,
        grid=(heads,),
        in_specs=[small_spec, small_spec],
        out_specs=[big_spec, big_spec],
        out_shape=[big, big],
        compiler_params=pltpu.CompilerParams(vmem_limit_bytes=VMEM_LIMIT),
        name="band_matrices",
    )(fwd, bwd)


def band(ref, h, w):
    if w == TILE:
        return ref[h]
    return jnp.concatenate([ref[h, a * TILE : a * TILE + w, :w] for a in range(QTAPS)], axis=0)


CONTRACT_LAST = (((1,), (1,)), ((), ()))
CONTRACT_FIRST = (((0,), (0,)), ((), ()))


def dot(lhs, rhs, dims=(((1,), (0,)), ((), ()))):
    return lax.dot_general(lhs, rhs, dims, preferred_element_type=jnp.float32)


def attend_kernel(widths, q_ref, k_ref, v_ref, t_ref, mask_ref, bias_ref, mix_ref, p_ref, m_ref, att_ref, logit_ref, mixed_ref):
    rows = p_ref.shape[1]
    chunk = min(rows, 64)
    pair = pl.program_id(0)
    for h in range(2):
        at = 0
        for w in widths:
            s = dot(q_ref[h], k_ref[h, at : at + w, :], CONTRACT_LAST)
            m_ref[h, :, at : at + w] = s.astype(jnp.bfloat16) * mask_ref[:, at : at + w]
            at += w
        at = 0
        for w in widths:
            lhs = jnp.concatenate(
                [m_ref[h, (RIM - a) * LANES : (RIM - a) * LANES + rows, at : at + w] for a in range(QTAPS)], axis=1
            )
            logit_ref[:, at : at + w] = dot(lhs, band(t_ref, h, w)) + bias_ref[:, at : at + w]
            at += w
        for r in range(0, rows, chunk):
            logits = logit_ref[r : r + chunk, :]
            powers = jnp.exp(logits - jnp.max(logits, axis=-1, keepdims=True))
            p_ref[h, r : r + chunk, :] = powers / jnp.sum(powers, axis=-1, keepdims=True)
    for o in range(2):
        w0, w1 = mix_ref[2 * pair + o, 0], mix_ref[2 * pair + o, 1]
        for r in range(0, rows, chunk):
            mixed_ref[r : r + chunk, :] = (
                w0 * p_ref[0, r : r + chunk, :] + w1 * p_ref[1, r : r + chunk, :]
            ).astype(jnp.bfloat16)
        att_ref[o] = dot(mixed_ref[...], v_ref[o])


def attend(q, k, v, t, mask, bias, head_mix, widths):
    groups, heads, ext, size = q.shape
    rows, cols = bias.shape[1:]
    two = lambda a, b: pl.BlockSpec((None, 2, a, b), lambda g, n: (n, g, 0, 0))
    whole = lambda a, b: pl.BlockSpec((None, a, b), lambda g, n: (n, 0, 0))
    return pl.pallas_call(
        functools.partial(attend_kernel, widths),
        grid=(heads // 2, groups),
        in_specs=[
            two(ext, size),
            two(cols, size),
            two(cols, size),
            pl.BlockSpec((2, QTAPS * TILE, TILE), lambda g, n: (g, 0, 0)),
            whole(ext, cols),
            whole(rows, cols),
            pl.BlockSpec(memory_space=pltpu.SMEM),
        ],
        out_specs=[two(rows, cols), two(ext, cols), two(rows, size)],
        out_shape=[
            jax.ShapeDtypeStruct((groups, heads, rows, cols), jnp.float32),
            jax.ShapeDtypeStruct((groups, heads, ext, cols), jnp.bfloat16),
            jax.ShapeDtypeStruct((groups, heads, rows, size), jnp.float32),
        ],
        scratch_shapes=[pltpu.VMEM((rows, cols), jnp.float32), pltpu.VMEM((rows, cols), jnp.bfloat16)],
        compiler_params=pltpu.CompilerParams(vmem_limit_bytes=VMEM_LIMIT),
        cost_estimate=pl.CostEstimate(
            flops=2 * groups * heads * rows * cols * (QTAPS * TILE + 3 * size),
            bytes_accessed=groups * heads * cols * (4 * rows + 2 * ext) + heads * QTAPS * TILE * TILE * 2,
            transcendentals=groups * heads * rows * cols,
        ),
        name="attend",
    )(q, k, v, t, mask, bias, head_mix)


def attend_back_kernel(
    widths, ga_ref, p_ref, m_ref, q_ref, k_ref, v_ref, tt_ref, mask_ref, mix_ref,
    gq_ref, gk_ref, gv_ref, tap_ref, gmix_ref,
    gpm_ref, mixed_ref, gc_ref, gs_ref,
):
    rows, cols = p_ref.shape[1], p_ref.shape[2]
    ext = q_ref.shape[1]
    chunk = min(rows, 64)
    pair = pl.program_id(0)
    rim = RIM * LANES
    mix = [[mix_ref[2 * pair + o, t] for t in range(2)] for o in range(2)]
    for o in range(2):
        for r in range(0, rows, chunk):
            mixed_ref[r : r + chunk, :] = (
                mix[o][0] * p_ref[0, r : r + chunk, :] + mix[o][1] * p_ref[1, r : r + chunk, :]
            ).astype(jnp.bfloat16)
        gv_ref[o] = dot(ga_ref[o], mixed_ref[...], CONTRACT_FIRST)
        gpm_ref[o] = dot(ga_ref[o], v_ref[o], CONTRACT_LAST)
    gc_ref[:, :rim, :] = jnp.zeros((2, rim, cols), jnp.bfloat16)
    gc_ref[:, rim + rows :, :] = jnp.zeros((2, rim, cols), jnp.bfloat16)
    sums = [[jnp.zeros((1, 1), jnp.float32) for t in range(2)] for o in range(2)]
    for r in range(0, rows, chunk):
        for t in range(2):
            probs = p_ref[t, r : r + chunk, :]
            ups = [gpm_ref[o, r : r + chunk, :] for o in range(2)]
            dots = [jnp.sum(probs * up, axis=-1, keepdims=True) for up in ups]
            for o in range(2):
                sums[o][t] = sums[o][t] + jnp.sum(dots[o], axis=0, keepdims=True)
            down = mix[0][t] * dots[0] + mix[1][t] * dots[1]
            grad = probs * (mix[0][t] * ups[0] + mix[1][t] * ups[1] - down)
            gc_ref[t, rim + r : rim + r + chunk, :] = grad.astype(jnp.bfloat16)

    @pl.when(pl.program_id(1) == 0)
    def _():
        gmix_ref[...] = jnp.zeros(gmix_ref.shape, jnp.float32)
        tap_ref[...] = jnp.zeros(tap_ref.shape, jnp.float32)

    for o in range(2):
        for t in range(2):
            gmix_ref[0, 2 * o + t : 2 * o + t + 1, :] += jnp.broadcast_to(sums[o][t], (1, 128))
    for h in range(2):
        at = 0
        for w in widths:
            lhs = jnp.concatenate(
                [gc_ref[h, a * LANES : a * LANES + ext, at : at + w] for a in range(QTAPS)], axis=1
            )
            back = dot(lhs, band(tt_ref, h, w))
            gs_ref[:, at : at + w] = back.astype(jnp.bfloat16) * mask_ref[:, at : at + w]
            at += w
        gq_ref[h] = dot(gs_ref[...], k_ref[h])
        gk_ref[h] = dot(q_ref[h], gs_ref[...], CONTRACT_FIRST)
        for width in sorted(set(widths)):
            spans, at = [], 0
            for w in widths:
                if w == width:
                    spans.append(at)
                at += w
            turned = jnp.concatenate(
                [gc_ref[h, rim : rim + rows, at : at + width].T for at in spans], axis=1
            )
            for a in range(QTAPS):
                low = (RIM - a) * LANES
                maps = jnp.concatenate([m_ref[h, low : low + rows, at : at + width] for at in spans], axis=0)
                cross = dot(turned, maps)
                total = cross[:8]
                for r in range(8, width, 8):
                    total = total + pltpu.roll(cross[r : r + 8], width - r, 1)
                tap_ref[h, a, :, :128] += total[:, :128]
                tap_ref[h, a, :, 128:] += total[:, width - 128 :]


def attend_back(ga, p, m, q, k, v, tt, mask, head_mix, widths):
    groups, heads, ext, size = q.shape
    rows, cols = p.shape[2:]
    two = lambda a, b: pl.BlockSpec((None, 2, a, b), lambda g, n: (n, g, 0, 0))
    whole = lambda a, b: pl.BlockSpec((None, a, b), lambda g, n: (n, 0, 0))
    return pl.pallas_call(
        functools.partial(attend_back_kernel, widths),
        grid=(heads // 2, groups),
        in_specs=[
            two(rows, size),
            two(rows, cols),
            two(ext, cols),
            two(ext, size),
            two(cols, size),
            two(cols, size),
            pl.BlockSpec((2, QTAPS * TILE, TILE), lambda g, n: (g, 0, 0)),
            whole(ext, cols),
            pl.BlockSpec(memory_space=pltpu.SMEM),
        ],
        out_specs=[
            two(ext, size),
            two(size, cols),
            two(size, cols),
            pl.BlockSpec((2, QTAPS, 8, TILE), lambda g, n: (g, 0, 0, 0)),
            pl.BlockSpec((1, 8, 128), lambda g, n: (g, 0, 0)),
        ],
        out_shape=[
            jax.ShapeDtypeStruct((groups, heads, ext, size), jnp.float32),
            jax.ShapeDtypeStruct((groups, heads, size, cols), jnp.float32),
            jax.ShapeDtypeStruct((groups, heads, size, cols), jnp.float32),
            jax.ShapeDtypeStruct((heads, QTAPS, 8, TILE), jnp.float32),
            jax.ShapeDtypeStruct((heads // 2, 8, 128), jnp.float32),
        ],
        scratch_shapes=[
            pltpu.VMEM((2, rows, cols), jnp.float32),
            pltpu.VMEM((rows, cols), jnp.bfloat16),
            pltpu.VMEM((2, rows + 2 * RIM * LANES, cols), jnp.bfloat16),
            pltpu.VMEM((ext, cols), jnp.bfloat16),
        ],
        compiler_params=pltpu.CompilerParams(vmem_limit_bytes=VMEM_LIMIT),
        cost_estimate=pl.CostEstimate(
            flops=2 * groups * heads * rows * cols * (2 * QTAPS * TILE + 5 * size),
            bytes_accessed=groups * heads * cols * (4 * rows + 2 * ext) + heads * QTAPS * TILE * TILE * 2,
            transcendentals=0,
        ),
        name="attend_back",
    )(ga, p, m, q, k, v, tt, mask, head_mix)


def gather_rows(array):
    if lax.axis_size("mp") != 2:
        return lax.all_gather(array, "mp", axis=1, tiled=True)
    other = lax.ppermute(array, "mp", [(0, 1), (1, 0)])
    first = lax.axis_index("mp") == 0
    return jnp.concatenate([jnp.where(first, array, other), jnp.where(first, other, array)], axis=1)


def scatter_rows(array):
    count = lax.axis_size("mp")
    own = array.shape[1] // count
    if count != 2:
        return lax.psum_scatter(array, "mp", scatter_dimension=1, tiled=True).astype(jnp.float32)
    first = lax.axis_index("mp") == 0
    head, tail = array[:, :own], array[:, own:]
    arrived = lax.ppermute(jnp.where(first, tail, head), "mp", [(0, 1), (1, 0)])
    return jnp.where(first, head, tail).astype(jnp.float32) + arrived.astype(jnp.float32)


def matmul(spec, lhs, rhs):
    return jnp.einsum(spec, lhs, rhs, preferred_element_type=jnp.float32)


def to_heads(array, heads):
    groups, rows, width = array.shape
    return jnp.swapaxes(array.reshape(groups, rows, heads, width // heads), 1, 2)


def from_heads(array):
    groups, heads, rows, size = array.shape
    return jnp.swapaxes(array, 1, 2).reshape(groups, rows, heads * size)


def shards(
    block_input,
    segment,
    norm1_gain,
    w_qkv,
    conv_kernel,
    head_mix,
    out_gain,
    w_out,
    norm2_gain,
    w_in,
    w_down,
    grad_y,
):
    mp_count = lax.axis_size("mp")
    seq_count = lax.axis_size("seq")
    groups, own_rows, model = block_input.shape
    stretch = own_rows * mp_count
    rows = groups * stretch
    heads = conv_kernel.shape[0]
    local_width = w_qkv.shape[2]
    size = local_width // heads
    score_scale = size ** (-0.5)
    behind = min(-(-(LONGEST - 1) // stretch), seq_count - 1)
    window = (behind + 1) * stretch
    widths = tile_widths(window)
    flat = lambda array: array.reshape((rows,) + array.shape[2:])
    grouped = lambda array: array.reshape((groups, stretch) + array.shape[1:])

    seq_start = lax.axis_index("seq") * stretch
    ids = segment[:, 0]
    padded_ids = jnp.pad(ids, ((0, 0), (window - stretch, 0)), constant_values=-1)
    key_ids = lax.dynamic_slice_in_dim(padded_ids, seq_start, window, 1)
    key_pos = seq_start - (window - stretch) + jnp.arange(window, dtype=jnp.int32)
    ext_ids = jnp.pad(ids, ((0, 0), (RIM, 0)), constant_values=-2)
    ext_ids = lax.dynamic_slice_in_dim(ext_ids, seq_start, stretch + RIM, 1)
    ext_pos = seq_start - RIM + jnp.arange(stretch + RIM, dtype=jnp.int32)
    row_ids = jax.vmap(lambda v: spread_rows(v[:RIM], v[RIM:]))(ext_ids)
    row_pos = spread_rows(ext_pos[:RIM], ext_pos[RIM:])
    col_ids = spread_keys(key_ids, 1, -1)
    col_pos = spread_keys(key_pos, 0, 1 << 20)
    valid = (col_pos[None, None, :] <= row_pos[None, :, None]) & (
        row_ids[:, :, None] == col_ids[:, None, :]
    )
    own_cols = jnp.asarray(own_columns(window))
    mask = valid.astype(jnp.bfloat16)
    bias = jnp.where(valid[:, RIM * LANES :] & own_cols[None, None, :], 0.0, -jnp.inf)
    taps, taps_back = band_matrices(conv_kernel, score_scale)

    input_float = block_input.astype(jnp.float32)
    inverse_one = inverse_rms(input_float)
    normed_one = input_float * inverse_one
    h1 = flat(gather_rows((normed_one * norm1_gain).astype(jnp.bfloat16)))
    projected = matmul("rd,dtc->trc", h1, w_qkv).astype(jnp.bfloat16)
    queries = grouped(projected[0])
    kv = projected[1:].reshape(2, groups, stretch, local_width)
    kv_parts = [from_behind(kv, "seq", step) for step in range(behind, 0, -1)] + [kv]
    kv_all = jnp.concatenate(kv_parts, axis=2)
    query_rim = from_behind(queries[:, stretch - RIM :], "seq", 1)
    q_heads = to_heads(jax.vmap(spread_rows)(query_rim, queries), heads)
    kv_spread = spread_keys(kv_all, 2)
    k_heads, v_heads = to_heads(kv_spread[0], heads), to_heads(kv_spread[1], heads)
    probs, maps, att = attend(q_heads, k_heads, v_heads, taps, mask, bias, head_mix, widths)
    inverse_head = inverse_rms(att)
    normed_head = att * inverse_head
    gain_heads = out_gain.reshape(1, heads, 1, size)
    mixed_out = from_heads((normed_head * gain_heads).astype(jnp.bfloat16))
    mixed_out = flat(jax.vmap(collect_plain)(mixed_out))
    branch = scatter_rows(grouped(matmul("rc,cd->rd", mixed_out, w_out).astype(jnp.bfloat16)))
    resid = input_float + branch
    inverse_two = inverse_rms(resid)
    normed_two = resid * inverse_two
    h2 = flat(gather_rows((normed_two * norm2_gain).astype(jnp.bfloat16)))
    gate_up = matmul("rd,dtf->trf", h2, w_in)
    gate, upward = gate_up[0], gate_up[1]
    sigma = jax.nn.sigmoid(gate)
    silu_gate = gate * sigma
    hidden = (silu_gate * upward).astype(jnp.bfloat16)
    mlp_out = scatter_rows(grouped(matmul("rf,fd->rd", hidden, w_down).astype(jnp.bfloat16)))
    output = (resid + mlp_out).astype(jnp.bfloat16)

    grad_float = grad_y.astype(jnp.float32)
    grad_full = flat(gather_rows(grad_y))
    part_down = matmul("rf,rd->fd", hidden, grad_full)
    grad_hidden = matmul("rd,fd->rf", grad_full, w_down)
    grad_gate = grad_hidden * upward * sigma * (1.0 + gate * (1.0 - sigma))
    grad_up = grad_hidden * silu_gate
    grad_gate_up = jnp.stack([grad_gate, grad_up]).astype(jnp.bfloat16)
    part_in = matmul("rd,trf->dtf", h2, grad_gate_up)
    grad_h2 = scatter_rows(grouped(matmul("trf,dtf->rd", grad_gate_up, w_in).astype(jnp.bfloat16)))
    part_gain_two = jnp.sum(grad_h2 * normed_two, axis=(0, 1))
    grad_resid = grad_float + norm_back(grad_h2, normed_two, inverse_two, norm2_gain)

    branch_grad = flat(gather_rows(grad_resid.astype(jnp.bfloat16)))
    part_out = matmul("rc,rd->cd", mixed_out, branch_grad)
    grad_mixed = grouped(matmul("rd,cd->rc", branch_grad, w_out))
    grad_mixed = to_heads(jax.vmap(spread_plain)(grad_mixed), heads)
    part_gain_out = jnp.sum(grad_mixed * normed_head, axis=(0, 2)).reshape(local_width)
    grad_att = norm_back(grad_mixed, normed_head, inverse_head, gain_heads).astype(jnp.bfloat16)
    gq, gk, gv, tap_sums, mix_sums = attend_back(
        grad_att, probs, maps, q_heads, k_heads, v_heads, taps_back, mask, head_mix, widths
    )
    bands = jnp.concatenate([tap_sums[..., TILE - HALF :], tap_sums[..., : HALF + 8]], axis=3)
    part_kernel = score_scale * sum(bands[:, :, i, i : i + KTAPS] for i in range(8))[..., ::-1]
    part_mix = mix_sums[:, :4, 0].reshape(heads, 2)
    rim_grad, grad_queries = jax.vmap(collect_rows)(from_heads(gq))
    rim_back = from_behind(rim_grad, "seq", -1)
    grad_queries = grad_queries.at[:, stretch - RIM :].add(rim_back)
    gkv = collect_keys(jnp.stack([gk, gv]), 4, window)
    gkv = jnp.transpose(gkv, (0, 1, 4, 2, 3)).reshape(2, groups, window, local_width)
    grad_kv = gkv[:, :, window - stretch :]
    for step in range(1, behind + 1):
        at = window - (step + 1) * stretch
        sent = gkv[:, :, at : at + stretch].astype(jnp.bfloat16)
        grad_kv = grad_kv + from_behind(sent, "seq", -step).astype(jnp.float32)
    grad_project = jnp.concatenate(
        [flat(grad_queries)[None], grad_kv.reshape(2, rows, local_width)]
    ).astype(jnp.bfloat16)
    part_qkv = matmul("rd,trc->dtc", h1, grad_project)
    grad_h1 = scatter_rows(grouped(matmul("trc,dtc->rd", grad_project, w_qkv).astype(jnp.bfloat16)))
    part_gain_one = jnp.sum(grad_h1 * normed_one, axis=(0, 1))
    grad_input = grad_resid + norm_back(grad_h1, normed_one, inverse_one, norm1_gain)

    total = lambda part: lax.psum(part.astype(jnp.bfloat16), ("dp", "seq")).astype(jnp.float32)
    grad_norm_one, grad_norm_two = lax.psum((part_gain_one, part_gain_two), ("dp", "seq", "mp"))
    return (
        output,
        grad_input,
        grad_norm_one,
        total(part_qkv),
        total(part_kernel),
        total(part_mix),
        total(part_gain_out),
        total(part_out),
        grad_norm_two,
        total(part_in),
        total(part_down),
    )


def solution(mesh):
    placed = (
        P(None, ("dp", "seq", "mp"), None),
        P(None, "dp", None),
        P(),
        P(None, None, "mp"),
        P("mp", None, None),
        P("mp", None),
        P("mp"),
        P("mp", None),
        P(),
        P(None, None, "mp"),
        P("mp", None),
        P(None, ("dp", "seq", "mp"), None),
    )
    return jax.shard_map(
        shards,
        mesh=mesh,
        in_specs=placed,
        out_specs=(
            P(None, ("dp", "seq", "mp"), None),
            P(None, ("dp", "seq", "mp"), None),
            P(),
            P(None, None, "mp"),
            P("mp", None, None),
            P("mp", None),
            P("mp"),
            P("mp", None),
            P(),
            P(None, None, "mp"),
            P("mp", None),
        ),
        check_vma=False,
    )
```

```python
import functools
import math

import jax
import jax.numpy as jnp
from jax import lax
from jax.experimental import pallas as pl
from jax.experimental.pallas import tpu as pltpu
from jax.sharding import PartitionSpec as P

QTAPS = 6
KTAPS = 11
LONGEST = 512
RIM = QTAPS - 1
HALF = KTAPS // 2
TILE = 256
OWN = TILE - 2 * HALF
LANES = 16

epsilon = 1e-05
VMEM_LIMIT = 58 * 1024 * 1024


def from_behind(value, axis, steps):
    count = lax.axis_size(axis)
    first, last = (max(0, -steps), min(count, count - steps))
    return lax.ppermute(value, axis, [(source, source + steps) for source in range(first, last)])


def inverse_rms(values):
    return lax.rsqrt(jnp.mean(values * values, axis=-1, keepdims=True) + epsilon)


def norm_back(upstream, normed, inverse, gain):
    scaled = upstream * gain
    return inverse * (scaled - normed * jnp.mean(scaled * normed, axis=-1, keepdims=True))


def tile_widths(window):
    widths, left = [], window
    while left > 0:
        width = TILE
        while width > 128 and left <= width // 2 - 2 * HALF:
            width //= 2
        widths.append(width)
        left -= width - 2 * HALF
    return widths


def tile_starts(window):
    starts, at = [], 0
    for width in tile_widths(window):
        starts.append(at)
        at += width - 2 * HALF
    return starts


def spread_keys(array, axis, fill=0):
    window = array.shape[axis]
    widths, starts = tile_widths(window), tile_starts(window)
    pads = [(0, 0)] * array.ndim
    pads[axis] = (HALF, starts[-1] + widths[-1] - HALF - window)
    padded = jnp.pad(array, pads, constant_values=fill)
    return jnp.concatenate(
        [lax.slice_in_dim(padded, s, s + w, axis=axis) for s, w in zip(starts, widths)], axis=axis
    )


def collect_keys(array, axis, window):
    widths, starts = tile_widths(window), tile_starts(window)
    length = starts[-1] + widths[-1]
    total, at = 0.0, 0
    for s, w in zip(starts, widths):
        pads = [(0, 0)] * array.ndim
        pads[axis] = (s, length - s - w)
        total = total + jnp.pad(lax.slice_in_dim(array, at, at + w, axis=axis), pads)
        at += w
    return lax.slice_in_dim(total, HALF, HALF + window, axis=axis)


def own_columns(window):
    own = []
    for s, w in zip(tile_starts(window), tile_widths(window)):
        own += [HALF <= c < w - HALF and s + c - HALF < window for c in range(w)]
    return own


def spread_rows(rim, rows):
    steps = rows.shape[0] // LANES
    rest = rows.shape[1:]
    ahead = jnp.zeros((steps - RIM,) + rest, rows.dtype)
    blocks = jnp.concatenate([ahead, rim.astype(rows.dtype), rows]).reshape((LANES + 1, steps) + rest)
    ext = jnp.concatenate([blocks[:LANES, steps - RIM :], blocks[1:]], axis=1)
    return jnp.swapaxes(ext, 0, 1).reshape(((steps + RIM) * LANES,) + rest)


def spread_plain(rows):
    steps = rows.shape[0] // LANES
    rest = rows.shape[1:]
    return jnp.swapaxes(rows.reshape((LANES, steps) + rest), 0, 1).reshape(rows.shape)


def collect_plain(rows):
    steps = rows.shape[0] // LANES
    rest = rows.shape[1:]
    return jnp.swapaxes(rows.reshape((steps, LANES) + rest), 0, 1).reshape(rows.shape)


def collect_rows(ext):
    steps = ext.shape[0] // LANES - RIM
    rest = ext.shape[1:]
    blocks = jnp.swapaxes(ext.reshape((steps + RIM, LANES) + rest), 0, 1)
    early, main = blocks[:, :RIM], blocks[:, RIM:]
    main = main.reshape((LANES * steps,) + rest)
    shifted = jnp.pad(early[1:], [(0, 1), (steps - RIM, 0)] + [(0, 0)] * len(rest))
    return early[0], main + shifted.reshape((LANES * steps,) + rest)


def taps_kernel(fwd_ref, bwd_ref, t_ref, tt_ref):
    for source, target in ((fwd_ref, t_ref), (bwd_ref, tt_ref)):
        for a in range(QTAPS):
            row = jnp.broadcast_to(source[0, a : a + 1, :], (TILE, TILE))
            turned = pltpu.roll(row, 0, 1, stride=1, stride_axis=0)
            target[0, a * TILE : (a + 1) * TILE, :] = turned.astype(jnp.bfloat16)


def band_matrices(conv_kernel, scale):
    heads = conv_kernel.shape[0]
    taps = conv_kernel * scale
    gap = jnp.zeros((heads, QTAPS, TILE - KTAPS), jnp.float32)
    fwd = jnp.concatenate([taps[:, :, HALF:], gap, taps[:, :, :HALF]], axis=2)
    flipped = taps[:, :, ::-1]
    bwd = jnp.concatenate([flipped[:, :, HALF:], gap, flipped[:, :, :HALF]], axis=2)
    big = jax.ShapeDtypeStruct((heads, QTAPS * TILE, TILE), jnp.bfloat16)
    small_spec = pl.BlockSpec((1, QTAPS, TILE), lambda h: (h, 0, 0))
    big_spec = pl.BlockSpec((1, QTAPS * TILE, TILE), lambda h: (h, 0, 0))
    return pl.pallas_call(
        taps_kernel,
        grid=(heads,),
        in_specs=[small_spec, small_spec],
        out_specs=[big_spec, big_spec],
        out_shape=[big, big],
        compiler_params=pltpu.CompilerParams(vmem_limit_bytes=VMEM_LIMIT),
        name="band_matrices",
    )(fwd, bwd)


def band(ref, h, w):
    if w == TILE:
        return ref[h]
    return jnp.concatenate([ref[h, a * TILE : a * TILE + w, :w] for a in range(QTAPS)], axis=0)


CONTRACT_LAST = (((1,), (1,)), ((), ()))
CONTRACT_FIRST = (((0,), (0,)), ((), ()))


def dot(lhs, rhs, dims=(((1,), (0,)), ((), ()))):
    return lax.dot_general(lhs, rhs, dims, preferred_element_type=jnp.float32)


def attend_kernel(widths, q_ref, k_ref, v_ref, t_ref, mask_ref, bias_ref, mix_ref, p_ref, m_ref, att_ref, logit_ref, mixed_ref):
    rows = p_ref.shape[1]
    chunk = min(rows, 64)
    pair = pl.program_id(0)
    for h in range(2):
        at = 0
        for w in widths:
            s = dot(q_ref[h], k_ref[h, at : at + w, :], CONTRACT_LAST)
            m_ref[h, :, at : at + w] = s.astype(jnp.bfloat16) * mask_ref[:, at : at + w]
            at += w
        at = 0
        for w in widths:
            lhs = jnp.concatenate(
                [m_ref[h, (RIM - a) * LANES : (RIM - a) * LANES + rows, at : at + w] for a in range(QTAPS)], axis=1
            )
            logit_ref[:, at : at + w] = dot(lhs, band(t_ref, h, w)) + bias_ref[:, at : at + w]
            at += w
        for r in range(0, rows, chunk):
            logits = logit_ref[r : r + chunk, :]
            powers = jnp.exp(logits - jnp.max(logits, axis=-1, keepdims=True))
            p_ref[h, r : r + chunk, :] = powers / jnp.sum(powers, axis=-1, keepdims=True)
    for o in range(2):
        w0, w1 = mix_ref[2 * pair + o, 0], mix_ref[2 * pair + o, 1]
        for r in range(0, rows, chunk):
            mixed_ref[r : r + chunk, :] = (
                w0 * p_ref[0, r : r + chunk, :] + w1 * p_ref[1, r : r + chunk, :]
            ).astype(jnp.bfloat16)
        att_ref[o] = dot(mixed_ref[...], v_ref[o])


def attend(q, k, v, t, mask, bias, head_mix, widths):
    groups, heads, ext, size = q.shape
    rows, cols = bias.shape[1:]
    two = lambda a, b: pl.BlockSpec((None, 2, a, b), lambda g, n: (n, g, 0, 0))
    whole = lambda a, b: pl.BlockSpec((None, a, b), lambda g, n: (n, 0, 0))
    return pl.pallas_call(
        functools.partial(attend_kernel, widths),
        grid=(heads // 2, groups),
        in_specs=[
            two(ext, size),
            two(cols, size),
            two(cols, size),
            pl.BlockSpec((2, QTAPS * TILE, TILE), lambda g, n: (g, 0, 0)),
            whole(ext, cols),
            whole(rows, cols),
            pl.BlockSpec(memory_space=pltpu.SMEM),
        ],
        out_specs=[two(rows, cols), two(ext, cols), two(rows, size)],
        out_shape=[
            jax.ShapeDtypeStruct((groups, heads, rows, cols), jnp.float32),
            jax.ShapeDtypeStruct((groups, heads, ext, cols), jnp.bfloat16),
            jax.ShapeDtypeStruct((groups, heads, rows, size), jnp.float32),
        ],
        scratch_shapes=[pltpu.VMEM((rows, cols), jnp.float32), pltpu.VMEM((rows, cols), jnp.bfloat16)],
        compiler_params=pltpu.CompilerParams(vmem_limit_bytes=VMEM_LIMIT),
        cost_estimate=pl.CostEstimate(
            flops=2 * groups * heads * rows * cols * (QTAPS * TILE + 3 * size),
            bytes_accessed=groups * heads * cols * (4 * rows + 2 * ext) + heads * QTAPS * TILE * TILE * 2,
            transcendentals=groups * heads * rows * cols,
        ),
        name="attend",
    )(q, k, v, t, mask, bias, head_mix)


def attend_back_kernel(
    widths, ga_ref, p_ref, m_ref, q_ref, k_ref, v_ref, tt_ref, mask_ref, mix_ref,
    gq_ref, gk_ref, gv_ref, tap_ref, gmix_ref,
    gpm_ref, mixed_ref, gc_ref, gs_ref,
):
    rows, cols = p_ref.shape[1], p_ref.shape[2]
    ext = q_ref.shape[1]
    chunk = min(rows, 64)
    pair = pl.program_id(0)
    rim = RIM * LANES
    mix = [[mix_ref[2 * pair + o, t] for t in range(2)] for o in range(2)]
    for o in range(2):
        for r in range(0, rows, chunk):
            mixed_ref[r : r + chunk, :] = (
                mix[o][0] * p_ref[0, r : r + chunk, :] + mix[o][1] * p_ref[1, r : r + chunk, :]
            ).astype(jnp.bfloat16)
        gv_ref[o] = dot(ga_ref[o], mixed_ref[...], CONTRACT_FIRST)
        gpm_ref[o] = dot(ga_ref[o], v_ref[o], CONTRACT_LAST)
    gc_ref[:, :rim, :] = jnp.zeros((2, rim, cols), jnp.bfloat16)
    gc_ref[:, rim + rows :, :] = jnp.zeros((2, rim, cols), jnp.bfloat16)
    sums = [[jnp.zeros((1, 1), jnp.float32) for t in range(2)] for o in range(2)]
    for r in range(0, rows, chunk):
        for t in range(2):
            probs = p_ref[t, r : r + chunk, :]
            ups = [gpm_ref[o, r : r + chunk, :] for o in range(2)]
            dots = [jnp.sum(probs * up, axis=-1, keepdims=True) for up in ups]
            for o in range(2):
                sums[o][t] = sums[o][t] + jnp.sum(dots[o], axis=0, keepdims=True)
            down = mix[0][t] * dots[0] + mix[1][t] * dots[1]
            grad = probs * (mix[0][t] * ups[0] + mix[1][t] * ups[1] - down)
            gc_ref[t, rim + r : rim + r + chunk, :] = grad.astype(jnp.bfloat16)

    @pl.when(pl.program_id(1) == 0)
    def _():
        gmix_ref[...] = jnp.zeros(gmix_ref.shape, jnp.float32)
        tap_ref[...] = jnp.zeros(tap_ref.shape, jnp.float32)

    for o in range(2):
        for t in range(2):
            gmix_ref[0, 2 * o + t : 2 * o + t + 1, :] += jnp.broadcast_to(sums[o][t], (1, 128))
    for h in range(2):
        at = 0
        for w in widths:
            lhs = jnp.concatenate(
                [gc_ref[h, a * LANES : a * LANES + ext, at : at + w] for a in range(QTAPS)], axis=1
            )
            back = dot(lhs, band(tt_ref, h, w))
            gs_ref[:, at : at + w] = back.astype(jnp.bfloat16) * mask_ref[:, at : at + w]
            at += w
        gq_ref[h] = dot(gs_ref[...], k_ref[h])
        gk_ref[h] = dot(q_ref[h], gs_ref[...], CONTRACT_FIRST)
        for width in sorted(set(widths)):
            spans, at = [], 0
            for w in widths:
                if w == width:
                    spans.append(at)
                at += w
            turned = jnp.concatenate(
                [gc_ref[h, rim : rim + rows, at : at + width].T for at in spans], axis=1
            )
            for a in range(QTAPS):
                low = (RIM - a) * LANES
                maps = jnp.concatenate([m_ref[h, low : low + rows, at : at + width] for at in spans], axis=0)
                cross = dot(turned, maps)
                total = cross[:8]
                for r in range(8, width, 8):
                    total = total + pltpu.roll(cross[r : r + 8], width - r, 1)
                tap_ref[h, a, :, :128] += total[:, :128]
                tap_ref[h, a, :, 128:] += total[:, width - 128 :]


def attend_back(ga, p, m, q, k, v, tt, mask, head_mix, widths):
    groups, heads, ext, size = q.shape
    rows, cols = p.shape[2:]
    two = lambda a, b: pl.BlockSpec((None, 2, a, b), lambda g, n: (n, g, 0, 0))
    whole = lambda a, b: pl.BlockSpec((None, a, b), lambda g, n: (n, 0, 0))
    return pl.pallas_call(
        functools.partial(attend_back_kernel, widths),
        grid=(heads // 2, groups),
        in_specs=[
            two(rows, size),
            two(rows, cols),
            two(ext, cols),
            two(ext, size),
            two(cols, size),
            two(cols, size),
            pl.BlockSpec((2, QTAPS * TILE, TILE), lambda g, n: (g, 0, 0)),
            whole(ext, cols),
            pl.BlockSpec(memory_space=pltpu.SMEM),
        ],
        out_specs=[
            two(ext, size),
            two(size, cols),
            two(size, cols),
            pl.BlockSpec((2, QTAPS, 8, TILE), lambda g, n: (g, 0, 0, 0)),
            pl.BlockSpec((1, 8, 128), lambda g, n: (g, 0, 0)),
        ],
        out_shape=[
            jax.ShapeDtypeStruct((groups, heads, ext, size), jnp.float32),
            jax.ShapeDtypeStruct((groups, heads, size, cols), jnp.float32),
            jax.ShapeDtypeStruct((groups, heads, size, cols), jnp.float32),
            jax.ShapeDtypeStruct((heads, QTAPS, 8, TILE), jnp.float32),
            jax.ShapeDtypeStruct((heads // 2, 8, 128), jnp.float32),
        ],
        scratch_shapes=[
            pltpu.VMEM((2, rows, cols), jnp.float32),
            pltpu.VMEM((rows, cols), jnp.bfloat16),
            pltpu.VMEM((2, rows + 2 * RIM * LANES, cols), jnp.bfloat16),
            pltpu.VMEM((ext, cols), jnp.bfloat16),
        ],
        compiler_params=pltpu.CompilerParams(vmem_limit_bytes=VMEM_LIMIT),
        cost_estimate=pl.CostEstimate(
            flops=2 * groups * heads * rows * cols * (2 * QTAPS * TILE + 5 * size),
            bytes_accessed=groups * heads * cols * (4 * rows + 2 * ext) + heads * QTAPS * TILE * TILE * 2,
            transcendentals=0,
        ),
        name="attend_back",
    )(ga, p, m, q, k, v, tt, mask, head_mix)


def gather_rows(array):
    if lax.axis_size("mp") != 2:
        return lax.all_gather(array, "mp", axis=1, tiled=True)
    other = lax.ppermute(array, "mp", [(0, 1), (1, 0)])
    first = lax.axis_index("mp") == 0
    return jnp.concatenate([jnp.where(first, array, other), jnp.where(first, other, array)], axis=1)


def scatter_rows(array):
    count = lax.axis_size("mp")
    own = array.shape[1] // count
    if count != 2:
        return lax.psum_scatter(array, "mp", scatter_dimension=1, tiled=True).astype(jnp.float32)
    first = lax.axis_index("mp") == 0
    head, tail = array[:, :own], array[:, own:]
    arrived = lax.ppermute(jnp.where(first, tail, head), "mp", [(0, 1), (1, 0)])
    return jnp.where(first, head, tail).astype(jnp.float32) + arrived.astype(jnp.float32)


def sum_small(parts):
    sizes = [part.size for part in parts]
    lanes = 128
    length = -(-sum(sizes) // (8 * lanes)) * 8 * lanes
    joined = jnp.concatenate([part.reshape(-1) for part in parts])
    joined = jnp.pad(joined, (0, length - joined.size)).reshape(1, length // lanes, lanes)
    every = lax.all_gather(joined, ("dp", "seq"), axis=0, tiled=True)
    summed = jnp.sum(every, axis=0).reshape(-1)
    result, at = [], 0
    for part, size in zip(parts, sizes):
        result.append(summed[at : at + size].reshape(part.shape))
        at += size
    return result


def scatter_tokens(part):
    part = part.astype(jnp.bfloat16)
    return lax.psum_scatter(part, ("dp", "seq"), scatter_dimension=0, tiled=True)


def ring_kernel(stages, shares, *refs):
    count = len(shares)
    late_ref, share_refs, outs = refs[0], refs[1 : 1 + count], refs[1 + count : 2 + 2 * count]
    acc_ref, landing_ref, local_sem, pair_sem, add_sem, ring_sem, side_sem = refs[2 + 2 * count :]
    dp, z = lax.axis_index("dp"), lax.axis_index("seq")
    x, core = dp // 2, dp % 2
    nodes = 2 * stages
    here = z + x * (nodes - 1 - 2 * z)

    def place(r):
        rx = r // stages
        return rx, r + rx * (nodes - 1 - 2 * r)

    def peer(r):
        rx, rz = place(r % nodes)
        return {"dp": 2 * rx + core, "seq": rz}

    right, left, side = peer(here + 1), peer(here + nodes - 1), {"dp": 2 * x + 1 - core, "seq": z}

    barrier = pltpu.get_barrier_semaphore()
    for device in (left, right, side):
        pl.semaphore_signal(barrier, inc=1, device_id=device, device_id_type=pl.DeviceIdType.MESH)
    pl.semaphore_wait(barrier, 3)

    def remote(src, dst, sems, device):
        return pltpu.make_async_remote_copy(
            src_ref=src,
            dst_ref=dst,
            send_sem=sems.at[0],
            recv_sem=sems.at[1],
            device_id=device,
            device_id_type=pl.DeviceIdType.MESH,
        )

    late_out, early_outs = outs[0], outs[1:]
    shard = late_ref.shape[0] // (2 * nodes)
    half = shard // 2
    run = stages * shard

    def piece(ref, r, part):
        rx, rz = place((r + 2 * nodes) % nodes)
        size = ref.shape[0] // (2 * nodes)
        start = ((2 * rx + core) * stages + rz) * size + part * (size // 2)
        return ref.at[pl.ds(pl.multiple_of(start, size // 2), size // 2)]

    def half_of(ref, part):
        size = ref.shape[0] // 2
        return ref.at[pl.ds(part * size, size)]

    def acc_start(r, part):
        rx, rz = place((r + 2 * nodes) % nodes)
        return pl.multiple_of((rx * stages + rz) * shard + part * half, half)

    def acc_piece(r, part):
        return acc_ref.at[pl.ds(acc_start(r, part), half)]

    sends = []

    def gather_step(i, out, own, k):
        arriving = []
        for part, device, sign in ((0, right, -1), (1, left, 1)):
            src = own(part) if k == 0 else piece(out, here + sign * k, part)
            dst = piece(out, here + sign * k, part)
            across = remote(src, dst, side_sem.at[i, k, part], side)
            across.start()
            sends.append((across, True))
            if k < nodes - 1:
                copy = remote(src, dst, ring_sem.at[i, k, part], device)
                copy.start()
                sends.append((copy, False))
                arriving.append(copy)
        return arriving

    def early_step(k):
        arriving = []
        for i in range(count):
            arriving += gather_step(1 + i, early_outs[i], lambda part, i=i: half_of(share_refs[i], part), k)
        return arriving

    pairs = []
    for rx in range(2):
        theirs = pl.multiple_of((2 * rx + 1 - core) * run, run)
        copy = remote(late_ref.at[pl.ds(theirs, run)], acc_ref.at[pl.ds(rx * run, run)], pair_sem.at[rx], side)
        copy.start()
        pairs.append(copy)
    locals_ = []
    for i in range(count):
        for part in range(2):
            copy = pltpu.make_async_copy(
                half_of(share_refs[i], part), piece(early_outs[i], here, part), local_sem.at[1 + i, part]
            )
            copy.start()
            locals_.append(copy)
    waiting = early_step(0)
    for rx in range(2):
        pairs[rx].wait_recv()
        mine = (2 * rx + core) * run

        @pl.loop(0, run // half)
        def _(j):
            to = pl.ds(pl.multiple_of(rx * run + j * half, half), half)
            own = pl.ds(pl.multiple_of(mine + j * half, half), half)
            acc_ref[to, :] = (
                acc_ref[to, :].astype(jnp.float32) + late_ref[own, :].astype(jnp.float32)
            ).astype(jnp.bfloat16)

    for k in range(nodes - 1):
        adding = []
        for part, device, sign in ((0, right, -1), (1, left, 1)):
            copy = remote(
                acc_piece(here + sign * (1 + k), part), landing_ref.at[k, part], add_sem.at[k, part], device
            )
            copy.start()
            sends.append((copy, False))
            adding.append(copy)
        for part, sign in ((0, -1), (1, 1)):
            adding[part].wait_recv()
            at = pl.ds(acc_start(here + sign * (2 + k), part), half)
            acc_ref[at, :] = (
                acc_ref[at, :].astype(jnp.float32) + landing_ref[k, part].astype(jnp.float32)
            ).astype(jnp.bfloat16)
        for copy in waiting:
            copy.wait_recv()
        waiting = early_step(k + 1)

    for part in range(2):
        copy = pltpu.make_async_copy(acc_piece(here, part), piece(late_out, here, part), local_sem.at[0, part])
        copy.start()
        locals_.append(copy)
    for k in range(nodes):
        waiting = gather_step(0, late_out, lambda part: acc_piece(here, part), k)
        for copy in waiting:
            copy.wait_recv()
    for copy in pairs:
        copy.wait_send()
    for copy, both in sends:
        copy.wait_send()
        if both:
            copy.wait_recv()
    for copy in locals_:
        copy.wait()


def finish_sums(late, shares):
    stages = lax.axis_size("seq")
    nodes = 2 * stages
    count = len(shares)
    shard = late.shape[0] // (2 * nodes)
    outs = [jax.ShapeDtypeStruct(late.shape, jnp.bfloat16)] + [
        jax.ShapeDtypeStruct((2 * nodes * part.shape[0],) + part.shape[1:], jnp.bfloat16) for part in shares
    ]
    anywhere = pl.BlockSpec(memory_space=pl.ANY)
    inside = pl.BlockSpec(memory_space=pltpu.VMEM)
    dma = pltpu.SemaphoreType.DMA
    return pl.pallas_call(
        functools.partial(ring_kernel, stages, [part.shape for part in shares]),
        in_specs=[inside] + [anywhere] * count,
        out_specs=[anywhere] * (1 + count),
        out_shape=outs,
        scratch_shapes=[
            pltpu.VMEM((nodes * shard, late.shape[1]), jnp.bfloat16),
            pltpu.VMEM((nodes - 1, 2, shard // 2, late.shape[1]), jnp.bfloat16),
            dma((1 + count, 2)),
            dma((2, 2)),
            dma((nodes - 1, 2, 2)),
            dma((1 + count, nodes - 1, 2, 2)),
            dma((1 + count, nodes, 2, 2)),
        ],
        compiler_params=pltpu.CompilerParams(
            collective_id=0, has_side_effects=True, vmem_limit_bytes=VMEM_LIMIT
        ),
        name="finish_sums",
    )(late, *shares)


def sum_peers(array):
    if lax.axis_size("mp") != 2:
        return lax.psum(array, "mp")
    return array + lax.ppermute(array, "mp", [(0, 1), (1, 0)])


def matmul(spec, lhs, rhs):
    return jnp.einsum(spec, lhs, rhs, preferred_element_type=jnp.float32)


def to_heads(array, heads):
    groups, rows, width = array.shape
    return jnp.swapaxes(array.reshape(groups, rows, heads, width // heads), 1, 2)


def from_heads(array):
    groups, heads, rows, size = array.shape
    return jnp.swapaxes(array, 1, 2).reshape(groups, rows, heads * size)


def shards(
    block_input,
    segment,
    norm1_gain,
    w_qkv,
    conv_kernel,
    head_mix,
    out_gain,
    w_out,
    norm2_gain,
    w_in,
    w_down,
    grad_y,
):
    mp_count = lax.axis_size("mp")
    seq_count = lax.axis_size("seq")
    groups, own_rows, model = block_input.shape
    stretch = own_rows * mp_count
    rows = groups * stretch
    heads = conv_kernel.shape[0]
    local_width = w_qkv.shape[2]
    size = local_width // heads
    score_scale = size ** (-0.5)
    behind = min(-(-(LONGEST - 1) // stretch), seq_count - 1)
    window = (behind + 1) * stretch
    widths = tile_widths(window)
    flat = lambda array: array.reshape((rows,) + array.shape[2:])
    grouped = lambda array: array.reshape((groups, stretch) + array.shape[1:])

    seq_start = lax.axis_index("seq") * stretch
    ids = segment[:, 0]
    padded_ids = jnp.pad(ids, ((0, 0), (window - stretch, 0)), constant_values=-1)
    key_ids = lax.dynamic_slice_in_dim(padded_ids, seq_start, window, 1)
    key_pos = seq_start - (window - stretch) + jnp.arange(window, dtype=jnp.int32)
    ext_ids = jnp.pad(ids, ((0, 0), (RIM, 0)), constant_values=-2)
    ext_ids = lax.dynamic_slice_in_dim(ext_ids, seq_start, stretch + RIM, 1)
    ext_pos = seq_start - RIM + jnp.arange(stretch + RIM, dtype=jnp.int32)
    row_ids = jax.vmap(lambda v: spread_rows(v[:RIM], v[RIM:]))(ext_ids)
    row_pos = spread_rows(ext_pos[:RIM], ext_pos[RIM:])
    col_ids = spread_keys(key_ids, 1, -1)
    col_pos = spread_keys(key_pos, 0, 1 << 20)
    valid = (col_pos[None, None, :] <= row_pos[None, :, None]) & (
        row_ids[:, :, None] == col_ids[:, None, :]
    )
    own_cols = jnp.asarray(own_columns(window))
    mask = valid.astype(jnp.bfloat16)
    bias = jnp.where(valid[:, RIM * LANES :] & own_cols[None, None, :], 0.0, -jnp.inf)
    taps, taps_back = band_matrices(conv_kernel, score_scale)

    input_float = block_input.astype(jnp.float32)
    inverse_one = inverse_rms(input_float)
    normed_one = input_float * inverse_one
    share = (normed_one * norm1_gain).astype(jnp.bfloat16)
    shares = [share]
    for step in range(behind):
        shares.append(from_behind(shares[-1], "seq", 1))
    h1_blocks = [gather_rows(part) for part in shares[::-1]]
    w_q, w_k, w_v = w_qkv[:, 0], w_qkv[:, 1], w_qkv[:, 2]
    project = lambda block, weight: matmul("grd,dc->grc", block, weight).astype(jnp.bfloat16)
    h1_own = h1_blocks[-1]
    h1_ext = jnp.concatenate([h1_blocks[-2][:, stretch - LANES :], h1_own], axis=1)
    queries = project(h1_ext, w_q)
    keys_all = jnp.concatenate([project(block, w_k) for block in h1_blocks], axis=1)
    values_all = jnp.concatenate([project(block, w_v) for block in h1_blocks], axis=1)
    q_heads = to_heads(
        jax.vmap(spread_rows)(queries[:, LANES - RIM : LANES], queries[:, LANES:]), heads
    )
    k_heads = to_heads(spread_keys(keys_all, 1), heads)
    v_heads = to_heads(spread_keys(values_all, 1), heads)
    probs, maps, att = attend(q_heads, k_heads, v_heads, taps, mask, bias, head_mix, widths)
    inverse_head = inverse_rms(att)
    normed_head = att * inverse_head
    gain_heads = out_gain.reshape(1, heads, 1, size)
    mixed_out = from_heads((normed_head * gain_heads).astype(jnp.bfloat16))
    mixed_out = flat(jax.vmap(collect_plain)(mixed_out))
    branch = scatter_rows(grouped(matmul("rc,cd->rd", mixed_out, w_out).astype(jnp.bfloat16)))
    resid = input_float + branch
    inverse_two = inverse_rms(resid)
    normed_two = resid * inverse_two
    h2 = flat(gather_rows((normed_two * norm2_gain).astype(jnp.bfloat16)))
    gate_up = matmul("rd,dtf->trf", h2, w_in)
    gate, upward = gate_up[0], gate_up[1]
    sigma = jax.nn.sigmoid(gate)
    silu_gate = gate * sigma
    hidden = (silu_gate * upward).astype(jnp.bfloat16)
    mlp_out = scatter_rows(grouped(matmul("rf,fd->rd", hidden, w_down).astype(jnp.bfloat16)))
    output = (resid + mlp_out).astype(jnp.bfloat16)

    grad_float = grad_y.astype(jnp.float32)
    grad_full = flat(gather_rows(grad_y))
    share_down = scatter_tokens(matmul("rf,rd->fd", hidden, grad_full))
    grad_hidden = matmul("rd,fd->rf", grad_full, w_down)
    grad_gate = grad_hidden * upward * sigma * (1.0 + gate * (1.0 - sigma))
    grad_up = grad_hidden * silu_gate
    grad_gate_up = jnp.stack([grad_gate, grad_up]).astype(jnp.bfloat16)
    share_in = scatter_tokens(matmul("rd,rf->df", h2, jnp.concatenate([grad_gate_up[0], grad_gate_up[1]], axis=1)))
    grad_h2 = scatter_rows(grouped(matmul("trf,dtf->rd", grad_gate_up, w_in).astype(jnp.bfloat16)))
    part_gain_two = jnp.sum(grad_h2 * normed_two, axis=(0, 1))
    grad_resid = grad_float + norm_back(grad_h2, normed_two, inverse_two, norm2_gain)

    branch_grad = flat(gather_rows(grad_resid.astype(jnp.bfloat16)))
    splits = model // local_width
    part_out = matmul("rc,rsd->scd", mixed_out, branch_grad.reshape(rows, splits, model // splits)).astype(jnp.bfloat16)
    grad_mixed = grouped(matmul("rd,cd->rc", branch_grad, w_out))
    grad_mixed = to_heads(jax.vmap(spread_plain)(grad_mixed), heads)
    part_gain_out = jnp.sum(grad_mixed * normed_head, axis=(0, 2)).reshape(local_width)
    grad_att = norm_back(grad_mixed, normed_head, inverse_head, gain_heads).astype(jnp.bfloat16)
    gq, gk, gv, tap_sums, mix_sums = attend_back(
        grad_att, probs, maps, q_heads, k_heads, v_heads, taps_back, mask, head_mix, widths
    )
    bands = jnp.concatenate([tap_sums[..., TILE - HALF :], tap_sums[..., : HALF + 8]], axis=3)
    part_kernel = score_scale * sum(bands[:, :, i, i : i + KTAPS] for i in range(8))[..., ::-1]
    part_mix = mix_sums[:, :4, 0].reshape(heads, 2)
    rim_grad, grad_queries = jax.vmap(collect_rows)(from_heads(gq))
    rim_grad = jnp.pad(rim_grad, ((0, 0), (LANES - RIM, 0), (0, 0)))
    grad_q = jnp.concatenate([rim_grad, grad_queries], axis=1).astype(jnp.bfloat16)
    to_rows = lambda g: jnp.transpose(collect_keys(g, 3, window).astype(jnp.bfloat16), (0, 3, 1, 2)).reshape(
        groups, window, local_width
    )
    grad_k, grad_v = to_rows(gk), to_rows(gv)
    h1_all = jnp.concatenate(h1_blocks, axis=1)
    part_qkv = jnp.stack(
        [
            matmul("grd,grc->dc", h1_ext, grad_q),
            matmul("grd,grc->dc", h1_all, grad_k),
            matmul("grd,grc->dc", h1_all, grad_v),
        ]
    ).astype(jnp.bfloat16)
    back = lambda grad, weight: matmul("grc,dc->grd", grad, weight)
    grad_ext = back(grad_q, w_q)
    grad_h1_all = back(grad_k, w_k) + back(grad_v, w_v)
    grad_h1_all = grad_h1_all + jnp.pad(grad_ext, ((0, 0), (window - stretch - LANES, 0), (0, 0)))
    grad_blocks = grad_h1_all.astype(jnp.bfloat16).reshape(groups * (behind + 1), stretch, model)
    grad_blocks = scatter_rows(grad_blocks).reshape(groups, behind + 1, own_rows, model)
    grad_h1 = grad_blocks[:, 0]
    for step in range(1, behind + 1):
        grad_h1 = from_behind(grad_h1.astype(jnp.bfloat16), "seq", -1).astype(jnp.float32) + grad_blocks[:, step]
    part_gain_one = jnp.sum(grad_h1 * normed_one, axis=(0, 1))
    grad_input = grad_resid + norm_back(grad_h1, normed_one, inverse_one, norm1_gain)

    joined = jnp.concatenate(
        [part_qkv.reshape(3 * model, local_width), part_out.reshape(splits * local_width, model // splits)]
    )
    joined, grad_in, grad_down = finish_sums(joined, [share_in, share_down])
    grad_qkv = joined[: 3 * model].reshape(3, model, local_width)
    grad_out = joined[3 * model :].reshape(splits, local_width, model // splits)
    part_gains = sum_peers(jnp.stack([part_gain_one, part_gain_two]))
    gain_sums, grad_kernel, grad_mix, grad_gain_out = sum_small(
        [part_gains, part_kernel, part_mix, part_gain_out]
    )
    return (
        output,
        grad_input,
        gain_sums[0],
        jnp.swapaxes(grad_qkv, 0, 1).astype(jnp.float32),
        grad_kernel,
        grad_mix,
        grad_gain_out,
        jnp.swapaxes(grad_out, 0, 1).reshape(local_width, model).astype(jnp.float32),
        gain_sums[1],
        grad_in.reshape(w_in.shape).astype(jnp.float32),
        grad_down.astype(jnp.float32),
    )


def solution(mesh):
    placed = (
        P(None, ("dp", "seq", "mp"), None),
        P(None, "dp", None),
        P(),
        P(None, None, "mp"),
        P("mp", None, None),
        P("mp", None),
        P("mp"),
        P("mp", None),
        P(),
        P(None, None, "mp"),
        P("mp", None),
        P(None, ("dp", "seq", "mp"), None),
    )
    return jax.shard_map(
        shards,
        mesh=mesh,
        in_specs=placed,
        out_specs=(
            P(None, ("dp", "seq", "mp"), None),
            P(None, ("dp", "seq", "mp"), None),
            P(),
            P(None, None, "mp"),
            P("mp", None, None),
            P("mp", None),
            P("mp"),
            P("mp", None),
            P(),
            P(None, None, "mp"),
            P("mp", None),
        ),
        check_vma=False,
    )
```

```python
import functools
import math

import jax
import jax.numpy as jnp
from jax import lax
from jax.experimental import pallas as pl
from jax.experimental.pallas import tpu as pltpu
from jax.sharding import PartitionSpec as P

QTAPS = 6
KTAPS = 11
LONGEST = 512
RIM = QTAPS - 1
HALF = KTAPS // 2
TILE = 256
OWN = TILE - 2 * HALF
LANES = 16

epsilon = 1e-05
VMEM_LIMIT = 58 * 1024 * 1024


def from_behind(value, axis, steps):
    count = lax.axis_size(axis)
    first, last = (max(0, -steps), min(count, count - steps))
    return lax.ppermute(value, axis, [(source, source + steps) for source in range(first, last)])


def inverse_rms(values):
    return lax.rsqrt(jnp.mean(values * values, axis=-1, keepdims=True) + epsilon)


def norm_back(upstream, normed, inverse, gain):
    scaled = upstream * gain
    return inverse * (scaled - normed * jnp.mean(scaled * normed, axis=-1, keepdims=True))


def tile_widths(window):
    widths, left = [], window
    while left > 0:
        width = TILE
        while width > 128 and left <= width // 2 - 2 * HALF:
            width //= 2
        widths.append(width)
        left -= width - 2 * HALF
    return widths


def tile_starts(window):
    starts, at = [], 0
    for width in tile_widths(window):
        starts.append(at)
        at += width - 2 * HALF
    return starts


def spread_keys(array, axis, fill=0):
    window = array.shape[axis]
    widths, starts = tile_widths(window), tile_starts(window)
    pads = [(0, 0)] * array.ndim
    pads[axis] = (HALF, starts[-1] + widths[-1] - HALF - window)
    padded = jnp.pad(array, pads, constant_values=fill)
    return jnp.concatenate(
        [lax.slice_in_dim(padded, s, s + w, axis=axis) for s, w in zip(starts, widths)], axis=axis
    )


def own_columns(window):
    own = []
    for s, w in zip(tile_starts(window), tile_widths(window)):
        own += [HALF <= c < w - HALF and s + c - HALF < window for c in range(w)]
    return own


def spread_rows(rim, rows):
    steps = rows.shape[0] // LANES
    rest = rows.shape[1:]
    ahead = jnp.zeros((steps - RIM,) + rest, rows.dtype)
    blocks = jnp.concatenate([ahead, rim.astype(rows.dtype), rows]).reshape((LANES + 1, steps) + rest)
    ext = jnp.concatenate([blocks[:LANES, steps - RIM :], blocks[1:]], axis=1)
    return jnp.swapaxes(ext, 0, 1).reshape(((steps + RIM) * LANES,) + rest)


def taps_kernel(fwd_ref, bwd_ref, t_ref, tt_ref):
    for source, target in ((fwd_ref, t_ref), (bwd_ref, tt_ref)):
        for a in range(QTAPS):
            row = jnp.broadcast_to(source[0, a : a + 1, :], (TILE, TILE))
            turned = pltpu.roll(row, 0, 1, stride=1, stride_axis=0)
            target[0, a * TILE : (a + 1) * TILE, :] = turned.astype(jnp.bfloat16)


def band_matrices(conv_kernel, scale):
    heads = conv_kernel.shape[0]
    taps = conv_kernel * scale
    gap = jnp.zeros((heads, QTAPS, TILE - KTAPS), jnp.float32)
    fwd = jnp.concatenate([taps[:, :, HALF:], gap, taps[:, :, :HALF]], axis=2)
    flipped = taps[:, :, ::-1]
    bwd = jnp.concatenate([flipped[:, :, HALF:], gap, flipped[:, :, :HALF]], axis=2)
    big = jax.ShapeDtypeStruct((heads, QTAPS * TILE, TILE), jnp.bfloat16)
    small_spec = pl.BlockSpec((1, QTAPS, TILE), lambda h: (h, 0, 0))
    big_spec = pl.BlockSpec((1, QTAPS * TILE, TILE), lambda h: (h, 0, 0))
    return pl.pallas_call(
        taps_kernel,
        grid=(heads,),
        in_specs=[small_spec, small_spec],
        out_specs=[big_spec, big_spec],
        out_shape=[big, big],
        compiler_params=pltpu.CompilerParams(vmem_limit_bytes=VMEM_LIMIT),
        name="band_matrices",
    )(fwd, bwd)


def band(ref, h, w):
    if w == TILE:
        return ref[h]
    return jnp.concatenate([ref[h, a * TILE : a * TILE + w, :w] for a in range(QTAPS)], axis=0)


CONTRACT_LAST = (((1,), (1,)), ((), ()))
CONTRACT_FIRST = (((0,), (0,)), ((), ()))


def dot(lhs, rhs, dims=(((1,), (0,)), ((), ()))):
    return lax.dot_general(lhs, rhs, dims, preferred_element_type=jnp.float32)


def attend_kernel(
    widths, q_ref, k_ref, v_ref, t_ref, mask_ref, bias_ref, mix_ref, gain_ref, rows_ref, cols_ref, plain_ref,
    o_ref, p_ref, m_ref, att_ref, qs_ref, ks_ref, vs_ref,
    logit_ref, mixed_ref,
):
    heads, rows = p_ref.shape[0], p_ref.shape[1]
    size = q_ref.shape[1] // heads
    chunk = min(rows, 64)
    first = pl.program_id(0) * heads
    for source, pick, target in ((q_ref, rows_ref, qs_ref), (k_ref, cols_ref, ks_ref), (v_ref, cols_ref, vs_ref)):
        moved = dot(pick[...], source[...]).astype(jnp.bfloat16)
        for h in range(heads):
            target[h] = moved[:, h * size : (h + 1) * size]
    for h in range(heads):
        at = 0
        for w in widths:
            s = dot(qs_ref[h], ks_ref[h, at : at + w, :], CONTRACT_LAST)
            m_ref[h, :, at : at + w] = s.astype(jnp.bfloat16) * mask_ref[:, at : at + w]
            at += w
        at = 0
        for w in widths:
            lhs = jnp.concatenate(
                [m_ref[h, (RIM - a) * LANES : (RIM - a) * LANES + rows, at : at + w] for a in range(QTAPS)], axis=1
            )
            logit_ref[:, at : at + w] = dot(lhs, band(t_ref, h, w)) + bias_ref[:, at : at + w]
            at += w
        for r in range(0, rows, chunk):
            logits = logit_ref[r : r + chunk, :]
            powers = jnp.exp(logits - jnp.max(logits, axis=-1, keepdims=True))
            p_ref[h, r : r + chunk, :] = powers / jnp.sum(powers, axis=-1, keepdims=True)
    outs = []
    for h in range(heads):
        low = h - h % 2
        w0, w1 = mix_ref[first + h, 0], mix_ref[first + h, 1]
        for r in range(0, rows, chunk):
            mixed_ref[r : r + chunk, :] = (
                w0 * p_ref[low, r : r + chunk, :] + w1 * p_ref[low + 1, r : r + chunk, :]
            ).astype(jnp.bfloat16)
        att = dot(mixed_ref[...], vs_ref[h])
        att_ref[h] = att
        outs.append(att * inverse_rms(att))
    normed = (jnp.concatenate(outs, axis=1) * gain_ref[...]).astype(jnp.bfloat16)
    o_ref[...] = dot(plain_ref[...], normed, CONTRACT_FIRST).astype(jnp.bfloat16)


def together(heads):
    return 4 if heads % 4 == 0 else heads


def attend(q, k, v, t, mask, bias, head_mix, gain, picks, heads, widths):
    groups, tall, width = q.shape
    window = k.shape[1]
    size = width // heads
    ext, cols = mask.shape[1:]
    rows = bias.shape[1]
    some = together(heads)
    natural = lambda n: pl.BlockSpec((None, n, some * size), lambda g, n: (n, 0, g))
    per_head = lambda a, b: pl.BlockSpec((None, some, a, b), lambda g, n: (n, g, 0, 0))
    whole = lambda a, b: pl.BlockSpec((None, a, b), lambda g, n: (n, 0, 0))
    fixed = lambda array: pl.BlockSpec(array.shape, lambda g, n: (0, 0))
    stacked = lambda a, b, kind: jax.ShapeDtypeStruct((groups, heads, a, b), kind)
    return pl.pallas_call(
        functools.partial(attend_kernel, widths),
        grid=(heads // some, groups),
        in_specs=[
            natural(tall),
            natural(window),
            natural(window),
            pl.BlockSpec((some, QTAPS * TILE, TILE), lambda g, n: (g, 0, 0)),
            whole(ext, cols),
            whole(rows, cols),
            pl.BlockSpec(memory_space=pltpu.SMEM),
            pl.BlockSpec((1, some * size), lambda g, n: (0, g)),
        ]
        + [fixed(pick) for pick in picks],
        out_specs=[
            natural(rows),
            per_head(rows, cols),
            per_head(ext, cols),
            per_head(rows, size),
            per_head(ext, size),
            per_head(cols, size),
            per_head(cols, size),
        ],
        out_shape=[
            jax.ShapeDtypeStruct((groups, rows, width), jnp.bfloat16),
            stacked(rows, cols, jnp.float32),
            stacked(ext, cols, jnp.bfloat16),
            stacked(rows, size, jnp.float32),
            stacked(ext, size, jnp.bfloat16),
            stacked(cols, size, jnp.bfloat16),
            stacked(cols, size, jnp.bfloat16),
        ],
        scratch_shapes=[pltpu.VMEM((rows, cols), jnp.float32), pltpu.VMEM((rows, cols), jnp.bfloat16)],
        compiler_params=pltpu.CompilerParams(vmem_limit_bytes=VMEM_LIMIT),
        cost_estimate=pl.CostEstimate(
            flops=2 * groups * heads * rows * cols * (QTAPS * TILE + 3 * size),
            bytes_accessed=groups * heads * cols * (4 * rows + 2 * ext) + heads * QTAPS * TILE * TILE * 2,
            transcendentals=groups * heads * rows * cols,
        ),
        name="attend",
    )(q, k, v, t, mask, bias, head_mix, gain, *picks)


def attend_back_kernel(
    widths, go_ref, att_ref, p_ref, m_ref, q_ref, k_ref, v_ref, tt_ref, mask_ref, mix_ref, gain_ref,
    rows_ref, cols_ref, plain_ref,
    gq_ref, gk_ref, gv_ref, tap_ref, gmix_ref, ggain_ref,
    ga_ref, gpm_ref, mixed_ref, gc_ref, gs_ref, gqs_ref, gks_ref, gvs_ref,
):
    heads, rows, cols = p_ref.shape
    ext, size = q_ref.shape[1:]
    chunk = min(rows, 64)
    first = pl.program_id(0) * heads
    rim = RIM * LANES

    @pl.when(pl.program_id(1) == 0)
    def _():
        gmix_ref[...] = jnp.zeros(gmix_ref.shape, jnp.float32)
        tap_ref[...] = jnp.zeros(tap_ref.shape, jnp.float32)
        ggain_ref[...] = jnp.zeros(ggain_ref.shape, jnp.float32)

    upper = go_ref[...].astype(jnp.bfloat16)
    lower = (go_ref[...] - upper.astype(jnp.float32)).astype(jnp.bfloat16)
    grad_o = dot(plain_ref[...], upper) + dot(plain_ref[...], lower)
    gains = []
    for h in range(heads):
        att = att_ref[h]
        inverse = inverse_rms(att)
        normed = att * inverse
        grad = grad_o[:, h * size : (h + 1) * size]
        gains.append(jnp.sum(grad * normed, axis=0, keepdims=True))
        ga_ref[h] = norm_back(grad, normed, inverse, gain_ref[:, h * size : (h + 1) * size]).astype(jnp.bfloat16)
    ggain_ref[0:1, :] += jnp.concatenate(gains, axis=1)

    gc_ref[:, :rim, :] = jnp.zeros((2, rim, cols), jnp.bfloat16)
    gc_ref[:, rim + rows :, :] = jnp.zeros((2, rim, cols), jnp.bfloat16)
    for low in range(0, heads, 2):
        mix = [[mix_ref[first + low + o, t] for t in range(2)] for o in range(2)]
        for o in range(2):
            for r in range(0, rows, chunk):
                mixed_ref[r : r + chunk, :] = (
                    mix[o][0] * p_ref[low, r : r + chunk, :] + mix[o][1] * p_ref[low + 1, r : r + chunk, :]
                ).astype(jnp.bfloat16)
            grad = dot(ga_ref[low + o], mixed_ref[...], CONTRACT_FIRST)
            gvs_ref[(low + o) * size : (low + o + 1) * size, :] = grad.astype(jnp.bfloat16)
            gpm_ref[o] = dot(ga_ref[low + o], v_ref[low + o], CONTRACT_LAST)
        sums = [[jnp.zeros((1, 1), jnp.float32) for t in range(2)] for o in range(2)]
        for r in range(0, rows, chunk):
            for t in range(2):
                probs = p_ref[low + t, r : r + chunk, :]
                ups = [gpm_ref[o, r : r + chunk, :] for o in range(2)]
                dots = [jnp.sum(probs * up, axis=-1, keepdims=True) for up in ups]
                for o in range(2):
                    sums[o][t] = sums[o][t] + jnp.sum(dots[o], axis=0, keepdims=True)
                down = mix[0][t] * dots[0] + mix[1][t] * dots[1]
                grad = probs * (mix[0][t] * ups[0] + mix[1][t] * ups[1] - down)
                gc_ref[t, rim + r : rim + r + chunk, :] = grad.astype(jnp.bfloat16)
        for o in range(2):
            for t in range(2):
                gmix_ref[low // 2, 2 * o + t : 2 * o + t + 1, :] += jnp.broadcast_to(sums[o][t], (1, 128))
        for t in range(2):
            h = low + t
            at = 0
            for w in widths:
                lhs = jnp.concatenate(
                    [gc_ref[t, a * LANES : a * LANES + ext, at : at + w] for a in range(QTAPS)], axis=1
                )
                back = dot(lhs, band(tt_ref, h, w))
                gs_ref[:, at : at + w] = back.astype(jnp.bfloat16) * mask_ref[:, at : at + w]
                at += w
            gqs_ref[:, h * size : (h + 1) * size] = dot(gs_ref[...], k_ref[h]).astype(jnp.bfloat16)
            gks_ref[h * size : (h + 1) * size, :] = dot(q_ref[h], gs_ref[...], CONTRACT_FIRST).astype(jnp.bfloat16)
            for width in sorted(set(widths)):
                spans, at = [], 0
                for w in widths:
                    if w == width:
                        spans.append(at)
                    at += w
                turned = jnp.concatenate(
                    [gc_ref[t, rim : rim + rows, at : at + width].T for at in spans], axis=1
                )
                for a in range(QTAPS):
                    start = (RIM - a) * LANES
                    maps = jnp.concatenate(
                        [m_ref[h, start : start + rows, at : at + width] for at in spans], axis=0
                    )
                    cross = dot(turned, maps)
                    total = cross[:8]
                    for r in range(8, width, 8):
                        total = total + pltpu.roll(cross[r : r + 8], width - r, 1)
                    tap_ref[h, a, :, :128] += total[:, :128]
                    tap_ref[h, a, :, 128:] += total[:, width - 128 :]
    gq_ref[...] = dot(rows_ref[...], gqs_ref[...], CONTRACT_FIRST).astype(jnp.bfloat16)
    gk_ref[...] = dot(cols_ref[...], gks_ref[...], (((0,), (1,)), ((), ()))).astype(jnp.bfloat16)
    gv_ref[...] = dot(cols_ref[...], gvs_ref[...], (((0,), (1,)), ((), ()))).astype(jnp.bfloat16)


def attend_back(go, att, p, m, q, k, v, tt, mask, head_mix, gain, picks, tall, window, widths):
    groups, heads, ext, size = q.shape
    rows, cols = p.shape[2:]
    width = heads * size
    some = together(heads)
    natural = lambda n: pl.BlockSpec((None, n, some * size), lambda g, n: (n, 0, g))
    per_head = lambda a, b: pl.BlockSpec((None, some, a, b), lambda g, n: (n, g, 0, 0))
    fixed = lambda array: pl.BlockSpec(array.shape, lambda g, n: (0, 0))
    moved = lambda n: jax.ShapeDtypeStruct((groups, n, width), jnp.bfloat16)
    return pl.pallas_call(
        functools.partial(attend_back_kernel, widths),
        grid=(heads // some, groups),
        in_specs=[
            natural(rows),
            per_head(rows, size),
            per_head(rows, cols),
            per_head(ext, cols),
            per_head(ext, size),
            per_head(cols, size),
            per_head(cols, size),
            pl.BlockSpec((some, QTAPS * TILE, TILE), lambda g, n: (g, 0, 0)),
            pl.BlockSpec((None, ext, cols), lambda g, n: (n, 0, 0)),
            pl.BlockSpec(memory_space=pltpu.SMEM),
            pl.BlockSpec((1, some * size), lambda g, n: (0, g)),
        ]
        + [fixed(pick) for pick in picks],
        out_specs=[
            natural(tall),
            natural(window),
            natural(window),
            pl.BlockSpec((some, QTAPS, 8, TILE), lambda g, n: (g, 0, 0, 0)),
            pl.BlockSpec((some // 2, 8, 128), lambda g, n: (g, 0, 0)),
            pl.BlockSpec((8, some * size), lambda g, n: (0, g)),
        ],
        out_shape=[
            moved(tall),
            moved(window),
            moved(window),
            jax.ShapeDtypeStruct((heads, QTAPS, 8, TILE), jnp.float32),
            jax.ShapeDtypeStruct((heads // 2, 8, 128), jnp.float32),
            jax.ShapeDtypeStruct((8, width), jnp.float32),
        ],
        scratch_shapes=[
            pltpu.VMEM((some, rows, size), jnp.bfloat16),
            pltpu.VMEM((2, rows, cols), jnp.float32),
            pltpu.VMEM((rows, cols), jnp.bfloat16),
            pltpu.VMEM((2, rows + 2 * RIM * LANES, cols), jnp.bfloat16),
            pltpu.VMEM((ext, cols), jnp.bfloat16),
            pltpu.VMEM((ext, some * size), jnp.bfloat16),
            pltpu.VMEM((some * size, cols), jnp.bfloat16),
            pltpu.VMEM((some * size, cols), jnp.bfloat16),
        ],
        compiler_params=pltpu.CompilerParams(vmem_limit_bytes=VMEM_LIMIT),
        cost_estimate=pl.CostEstimate(
            flops=2 * groups * heads * rows * cols * (2 * QTAPS * TILE + 5 * size),
            bytes_accessed=groups * heads * cols * (4 * rows + 2 * ext) + heads * QTAPS * TILE * TILE * 2,
            transcendentals=0,
        ),
        name="attend_back",
    )(go, att, p, m, q, k, v, tt, mask, head_mix, gain, *picks)


def gather_rows(array):
    if lax.axis_size("mp") != 2:
        return lax.all_gather(array, "mp", axis=1, tiled=True)
    other = lax.ppermute(array, "mp", [(0, 1), (1, 0)])
    first = lax.axis_index("mp") == 0
    return jnp.concatenate([jnp.where(first, array, other), jnp.where(first, other, array)], axis=1)


def scatter_rows(array, after=None):
    count = lax.axis_size("mp")
    own = array.shape[1] // count
    if count != 2:
        return lax.psum_scatter(array, "mp", scatter_dimension=1, tiled=True).astype(jnp.float32)
    first = lax.axis_index("mp") == 0
    head, tail = array[:, :own], array[:, own:]
    arrived = lax.ppermute(jnp.where(first, tail, head), "mp", [(0, 1), (1, 0)])
    if after is not None:
        arrived, _ = lax.optimization_barrier((arrived, after))
    return jnp.where(first, head, tail).astype(jnp.float32) + arrived.astype(jnp.float32)


def join_small(parts):
    lanes, tile = 128, 16
    joined = jnp.concatenate([part.reshape(-1) for part in parts])
    rows = -(-joined.size // (tile * lanes)) * tile
    return jnp.pad(joined, (0, rows * lanes - joined.size)).reshape(rows, lanes)


def split_small(joined, parts):
    flat, result, at = joined.reshape(-1), [], 0
    for part in parts:
        result.append(flat[at : at + part.size].reshape(part.shape))
        at += part.size
    return result


def scatter_tokens(part):
    part = part.astype(jnp.bfloat16)
    return lax.psum_scatter(part, ("dp", "seq"), scatter_dimension=0, tiled=True)


def ring_kernel(stages, parts, count, *refs):
    part_refs, share_refs = refs[:parts], refs[parts : parts + count]
    outs = refs[parts + count : parts + 2 * count + 1]
    late_ref, acc_ref, landing_ref, local_sem, load_sem, pair_sem, add_sem, ring_sem, side_sem = refs[
        parts + 2 * count + 1 :
    ]
    dp, z = lax.axis_index("dp"), lax.axis_index("seq")
    x, core = dp // 2, dp % 2
    nodes = 2 * stages
    here = z + x * (nodes - 1 - 2 * z)

    def place(r):
        rx = r // stages
        return rx, r + rx * (nodes - 1 - 2 * r)

    def peer(r):
        rx, rz = place(r % nodes)
        return {"dp": 2 * rx + core, "seq": rz}

    right, left, side = peer(here + 1), peer(here + nodes - 1), {"dp": 2 * x + 1 - core, "seq": z}

    loads = []
    for i in range(parts):
        copy = pltpu.make_async_copy(part_refs[i], late_ref.at[:, i], load_sem.at[i])
        copy.start()
        loads.append(copy)

    barrier = pltpu.get_barrier_semaphore()
    for device in (left, right, side):
        pl.semaphore_signal(barrier, inc=1, device_id=device, device_id_type=pl.DeviceIdType.MESH)
    pl.semaphore_wait(barrier, 3)

    def remote(src, dst, sems, device):
        return pltpu.make_async_remote_copy(
            src_ref=src,
            dst_ref=dst,
            send_sem=sems.at[0],
            recv_sem=sems.at[1],
            device_id=device,
            device_id_type=pl.DeviceIdType.MESH,
        )

    late_out, early_outs = outs[0], outs[1:]
    half = parts // 2

    def node(r):
        rx, rz = place((r + 2 * nodes) % nodes)
        return rx * stages + rz

    def number(r):
        rx, rz = place((r + 2 * nodes) % nodes)
        return (2 * rx + core) * stages + rz

    def half_of(ref, part):
        size = ref.shape[0] // 2
        return ref.at[pl.ds(part * size, size)]

    def acc_piece(r, part):
        return acc_ref.at[node(r), pl.ds(part * half, half)]

    def early_piece(i, r, part):
        size = share_refs[i].shape[0] // 2
        return early_outs[i].at[number(r), pl.ds(part * size, size)]

    def late_piece(r, part):
        return late_out.at[pl.ds(part * half, half), number(r)]

    sends = []

    def gather_step(i, piece, own, k):
        arriving = []
        for part, device, sign in ((0, right, -1), (1, left, 1)):
            dst = piece(here + sign * k, part)
            src = own(part) if k == 0 else dst
            if k < nodes - 1:
                copy = remote(src, dst, ring_sem.at[i, k, part], device)
                copy.start()
                sends.append((copy, False))
                arriving.append(copy)
            across = remote(src, dst, side_sem.at[i, k, part], side)
            across.start()
            sends.append((across, True))
        return arriving

    def early_step(k):
        arriving = []
        for i in range(count):
            arriving += gather_step(
                1 + i, functools.partial(early_piece, i), functools.partial(half_of, share_refs[i]), k
            )
        return arriving

    for copy in loads:
        copy.wait()
    pairs = []
    for rx in range(2):
        copy = remote(
            late_ref.at[pl.ds((2 * rx + 1 - core) * stages, stages)],
            acc_ref.at[pl.ds(rx * stages, stages)],
            pair_sem.at[rx],
            side,
        )
        copy.start()
        pairs.append(copy)
    waiting = early_step(0)
    locals_ = []
    for i in range(count):
        for part in range(2):
            copy = pltpu.make_async_copy(
                half_of(share_refs[i], part), early_piece(i, here, part), local_sem.at[1 + i, part]
            )
            copy.start()
            locals_.append(copy)
    for rx in range(2):
        pairs[rx].wait_recv()

        @pl.loop(0, stages * parts)
        def _(j):
            to, own, i = rx * stages + j // parts, (2 * rx + core) * stages + j // parts, j % parts
            acc_ref[to, i] = (
                acc_ref[to, i].astype(jnp.float32) + late_ref[own, i].astype(jnp.float32)
            ).astype(jnp.bfloat16)

    for k in range(nodes - 1):
        adding = []
        for part, device, sign in ((0, right, -1), (1, left, 1)):
            copy = remote(
                acc_piece(here + sign * (1 + k), part), landing_ref.at[k, part], add_sem.at[k, part], device
            )
            copy.start()
            sends.append((copy, False))
            adding.append(copy)
        for part, sign in ((0, -1), (1, 1)):
            adding[part].wait_recv()
            to = node(here + sign * (2 + k))
            for i in range(half):
                acc_ref[to, part * half + i] = (
                    acc_ref[to, part * half + i].astype(jnp.float32) + landing_ref[k, part, i].astype(jnp.float32)
                ).astype(jnp.bfloat16)
        for copy in waiting:
            copy.wait_recv()
        waiting = early_step(k + 1)

    for part in range(2):
        copy = pltpu.make_async_copy(acc_piece(here, part), late_piece(here, part), local_sem.at[0, part])
        copy.start()
        locals_.append(copy)
    for k in range(nodes):
        waiting = gather_step(0, late_piece, lambda part: acc_piece(here, part), k)
        for copy in waiting:
            copy.wait_recv()
    for copy in pairs:
        copy.wait_send()
    for copy, both in sends:
        copy.wait_send()
        if both:
            copy.wait_recv()
    for copy in locals_:
        copy.wait()


def finish_sums(partials, shares):
    stages = lax.axis_size("seq")
    nodes = 2 * stages
    parts, count = len(partials), len(shares)
    rows, width = partials[0].shape
    shard = rows // (2 * nodes)
    outs = [jax.ShapeDtypeStruct((parts, 2 * nodes, shard, width), jnp.bfloat16)] + [
        jax.ShapeDtypeStruct((2 * nodes,) + share.shape, share.dtype) for share in shares
    ]
    anywhere = pl.BlockSpec(memory_space=pl.ANY)
    dma = pltpu.SemaphoreType.DMA
    return pl.pallas_call(
        functools.partial(ring_kernel, stages, parts, count),
        in_specs=[anywhere] * (parts + count),
        out_specs=[anywhere] * (1 + count),
        out_shape=outs,
        scratch_shapes=[
            pltpu.VMEM((2 * nodes, parts, shard, width), jnp.bfloat16),
            pltpu.VMEM((nodes, parts, shard, width), jnp.bfloat16),
            pltpu.VMEM((nodes - 1, 2, parts // 2, shard, width), jnp.bfloat16),
            dma((1 + count, 2)),
            dma((parts,)),
            dma((2, 2)),
            dma((nodes - 1, 2, 2)),
            dma((1 + count, nodes - 1, 2, 2)),
            dma((1 + count, nodes, 2, 2)),
        ],
        compiler_params=pltpu.CompilerParams(
            collective_id=0, has_side_effects=True, vmem_limit_bytes=VMEM_LIMIT
        ),
        cost_estimate=pl.CostEstimate(flops=0, bytes_accessed=600 * 1024 * 1024, transcendentals=0),
        name="finish_sums",
    )(*[part.reshape(2 * nodes, shard, width) for part in partials], *shares)


def sum_peers(array):
    if lax.axis_size("mp") != 2:
        return lax.psum(array, "mp")
    return array + lax.ppermute(array, "mp", [(0, 1), (1, 0)])


def matmul(spec, lhs, rhs):
    return jnp.einsum(spec, lhs, rhs, preferred_element_type=jnp.float32)


def shards(
    block_input,
    segment,
    norm1_gain,
    w_qkv,
    conv_kernel,
    head_mix,
    out_gain,
    w_out,
    norm2_gain,
    w_in,
    w_down,
    grad_y,
):
    mp_count = lax.axis_size("mp")
    seq_count = lax.axis_size("seq")
    groups, own_rows, model = block_input.shape
    stretch = own_rows * mp_count
    rows = groups * stretch
    heads = conv_kernel.shape[0]
    local_width = w_qkv.shape[2]
    size = local_width // heads
    ff_local = w_down.shape[0]
    score_scale = size ** (-0.5)
    behind = min(-(-(LONGEST - 1) // stretch), seq_count - 1)
    window = (behind + 1) * stretch
    widths = tile_widths(window)
    flat = lambda array: array.reshape((rows,) + array.shape[2:])
    grouped = lambda array: array.reshape((groups, stretch) + array.shape[1:])

    seq_start = lax.axis_index("seq") * stretch
    ids = segment[:, 0]
    padded_ids = jnp.pad(ids, ((0, 0), (window - stretch, 0)), constant_values=-1)
    key_ids = lax.dynamic_slice_in_dim(padded_ids, seq_start, window, 1)
    key_pos = seq_start - (window - stretch) + jnp.arange(window, dtype=jnp.int32)
    ext_ids = jnp.pad(ids, ((0, 0), (RIM, 0)), constant_values=-2)
    ext_ids = lax.dynamic_slice_in_dim(ext_ids, seq_start, stretch + RIM, 1)
    ext_pos = seq_start - RIM + jnp.arange(stretch + RIM, dtype=jnp.int32)
    row_ids = jax.vmap(lambda v: spread_rows(v[:RIM], v[RIM:]))(ext_ids)
    row_pos = spread_rows(ext_pos[:RIM], ext_pos[RIM:])
    col_ids = spread_keys(key_ids, 1, -1)
    col_pos = spread_keys(key_pos, 0, 1 << 20)
    valid = (col_pos[None, None, :] <= row_pos[None, :, None]) & (
        row_ids[:, :, None] == col_ids[:, None, :]
    )
    own_cols = jnp.asarray(own_columns(window))
    mask = valid.astype(jnp.bfloat16)
    bias = jnp.where(valid[:, RIM * LANES :] & own_cols[None, None, :], 0.0, -jnp.inf)
    taps, taps_back = band_matrices(conv_kernel, score_scale)
    tall = LANES + stretch
    spot = jnp.arange(tall, dtype=jnp.int32)
    row_order = spread_rows(spot[LANES - RIM : LANES], spot[LANES:])
    pick_rows = (row_order[:, None] == spot[None, :]).astype(jnp.bfloat16)
    pick_plain = pick_rows[RIM * LANES :, LANES:]
    key_order = spread_keys(jnp.arange(window, dtype=jnp.int32), 0, -1)
    pick_cols = (key_order[:, None] == jnp.arange(window, dtype=jnp.int32)[None, :]).astype(jnp.bfloat16)
    picks = [pick_rows, pick_cols, pick_plain]

    input_float = block_input.astype(jnp.float32)
    inverse_one = inverse_rms(input_float)
    normed_one = input_float * inverse_one
    share = (normed_one * norm1_gain).astype(jnp.bfloat16)
    shares = [share]
    for step in range(behind):
        shares.append(from_behind(shares[-1], "seq", 1))
    h1_blocks = []
    for part in shares:
        h1_blocks.append(gather_rows(part))
    grad_full = flat(gather_rows(grad_y))
    w_q, w_k, w_v = w_qkv[:, 0], w_qkv[:, 1], w_qkv[:, 2]
    h1_all = jnp.concatenate(h1_blocks[::-1], axis=1)
    h1_ext = h1_all[:, window - tall :]
    project = lambda block, weight: matmul("grd,dc->grc", block, weight).astype(jnp.bfloat16)
    queries, keys, values = project(h1_ext, w_q), project(h1_all, w_k), project(h1_all, w_v)
    queries, grad_full = lax.optimization_barrier((queries, grad_full))
    gain_row = out_gain.reshape(1, local_width)
    mixed_out, probs, maps, att, q_heads, k_heads, v_heads = attend(
        queries, keys, values, taps, mask, bias, head_mix, gain_row, picks, heads, widths
    )
    mixed_out = flat(mixed_out)
    branch = scatter_rows(grouped(matmul("rc,cd->rd", mixed_out, w_out).astype(jnp.bfloat16)))
    resid = input_float + branch
    inverse_two = inverse_rms(resid)
    normed_two = resid * inverse_two
    h2 = flat(gather_rows((normed_two * norm2_gain).astype(jnp.bfloat16)))
    gate_up = matmul("rd,dtf->trf", h2, w_in)
    gate, upward = gate_up[0], gate_up[1]
    sigma = jax.nn.sigmoid(gate)
    silu_gate = gate * sigma
    hidden = (silu_gate * upward).astype(jnp.bfloat16)
    mlp_out = scatter_rows(grouped(matmul("rf,fd->rd", hidden, w_down).astype(jnp.bfloat16)))
    output = (resid + mlp_out).astype(jnp.bfloat16)

    grad_float = grad_y.astype(jnp.float32)
    share_down = scatter_tokens(matmul("rf,rd->fd", hidden, grad_full))
    grad_hidden = matmul("rd,fd->rf", grad_full, w_down)
    grad_gate = grad_hidden * upward * sigma * (1.0 + gate * (1.0 - sigma))
    grad_up = grad_hidden * silu_gate
    grad_gate_up = jnp.stack([grad_gate, grad_up]).astype(jnp.bfloat16)
    share_in = scatter_tokens(matmul("rd,rf->df", h2, jnp.concatenate([grad_gate_up[0], grad_gate_up[1]], axis=1)))
    grad_h2 = scatter_rows(grouped(matmul("trf,dtf->rd", grad_gate_up, w_in).astype(jnp.bfloat16)))
    part_gain_two = jnp.sum(grad_h2 * normed_two, axis=(0, 1))
    grad_resid = grad_float + norm_back(grad_h2, normed_two, inverse_two, norm2_gain)

    branch_grad = flat(gather_rows(grad_resid.astype(jnp.bfloat16)))
    splits = model // local_width
    part_out = matmul("rc,rsd->scd", mixed_out, branch_grad.reshape(rows, splits, model // splits)).astype(jnp.bfloat16)
    grad_mixed = grouped(matmul("rd,cd->rc", branch_grad, w_out))
    grad_q, grad_k, grad_v, tap_sums, mix_sums, gain_sums = attend_back(
        grad_mixed, att, probs, maps, q_heads, k_heads, v_heads, taps_back, mask, head_mix, gain_row, picks,
        tall, window, widths,
    )
    part_gain_out = gain_sums[0]
    bands = jnp.concatenate([tap_sums[..., TILE - HALF :], tap_sums[..., : HALF + 8]], axis=3)
    part_kernel = score_scale * sum(bands[:, :, i, i : i + KTAPS] for i in range(8))[..., ::-1]
    part_mix = mix_sums[:, :4, 0].reshape(heads, 2)
    wide = model // local_width
    partials = [
        matmul("grd,grc->dc", h1_ext, grad_q).astype(jnp.bfloat16),
        matmul("grd,grc->dc", h1_all, grad_k).astype(jnp.bfloat16),
        matmul("grd,grc->dc", h1_all, grad_v).astype(jnp.bfloat16),
        part_out.reshape(model, local_width),
    ]
    back = lambda grad, weight: matmul("grc,dc->grd", grad, weight)
    grad_ext = back(grad_q, w_q)
    grad_h1_all = back(grad_k, w_k) + back(grad_v, w_v)
    grad_h1_all = grad_h1_all + jnp.pad(grad_ext, ((0, 0), (window - stretch - LANES, 0), (0, 0)))
    part_gain_one = jnp.sum(grad_h1_all * h1_all.astype(jnp.float32), axis=(0, 1)) / norm1_gain
    grad_blocks = grad_h1_all.astype(jnp.bfloat16).reshape(groups * (behind + 1), stretch, model)

    small = [part_gain_one, part_gain_two, part_kernel, part_mix, part_gain_out]
    share_in = share_in.reshape(-1, 2, ff_local // 128, 128)
    share_in = jnp.swapaxes(share_in, 1, 2).reshape(-1, 128)
    grad_late, grad_in, grad_down, every = finish_sums(partials, [share_in, share_down, join_small(small)])
    grad_qkv = jnp.swapaxes(grad_late[:3].reshape(3, model, local_width), 0, 1).astype(jnp.float32)
    grad_out = grad_late[3].reshape(wide, local_width, local_width)
    grad_out = jnp.swapaxes(grad_out, 0, 1).reshape(local_width, model).astype(jnp.float32)
    grad_in = grad_in.astype(jnp.float32).reshape(model, ff_local // 128, 2, 128)
    grad_in = jnp.swapaxes(grad_in, 1, 2).reshape(w_in.shape)
    grad_down = grad_down.astype(jnp.float32).reshape(w_down.shape)

    grad_blocks = scatter_rows(grad_blocks, every).reshape(groups, behind + 1, own_rows, model)
    grad_h1 = grad_blocks[:, 0]
    for step in range(1, behind + 1):
        grad_h1 = from_behind(grad_h1.astype(jnp.bfloat16), "seq", -1).astype(jnp.float32) + grad_blocks[:, step]
    grad_input = grad_resid + norm_back(grad_h1, normed_one, inverse_one, norm1_gain)

    gain_one, gain_two, grad_kernel, grad_mix, grad_gain_out = split_small(jnp.sum(every, axis=0), small)
    gain_sums = sum_peers(jnp.stack([gain_one, gain_two]))
    return (
        output,
        grad_input,
        gain_sums[0],
        grad_qkv,
        grad_kernel,
        grad_mix,
        grad_gain_out,
        grad_out,
        gain_sums[1],
        grad_in,
        grad_down,
    )


def solution(mesh):
    placed = (
        P(None, ("dp", "seq", "mp"), None),
        P(None, "dp", None),
        P(),
        P(None, None, "mp"),
        P("mp", None, None),
        P("mp", None),
        P("mp"),
        P("mp", None),
        P(),
        P(None, None, "mp"),
        P("mp", None),
        P(None, ("dp", "seq", "mp"), None),
    )
    return jax.shard_map(
        shards,
        mesh=mesh,
        in_specs=placed,
        out_specs=(
            P(None, ("dp", "seq", "mp"), None),
            P(None, ("dp", "seq", "mp"), None),
            P(),
            P(None, None, "mp"),
            P("mp", None, None),
            P("mp", None),
            P("mp"),
            P("mp", None),
            P(),
            P(None, None, "mp"),
            P("mp", None),
        ),
        check_vma=False,
    )
```

```python
import functools
import math

import jax
import jax.numpy as jnp
from jax import lax
from jax.experimental import pallas as pl
from jax.experimental.pallas import tpu as pltpu
from jax.sharding import PartitionSpec as P

QTAPS = 6
KTAPS = 11
LONGEST = 512
RIM = QTAPS - 1
HALF = KTAPS // 2
TILE = 256
OWN = TILE - 2 * HALF
LANES = 16

epsilon = 1e-05
VMEM_LIMIT = 58 * 1024 * 1024
RING_VMEM = 40 * 1024 * 1024


def from_behind(value, axis, steps):
    count = lax.axis_size(axis)
    first, last = (max(0, -steps), min(count, count - steps))
    return lax.ppermute(value, axis, [(source, source + steps) for source in range(first, last)])


def inverse_rms(values):
    return lax.rsqrt(jnp.mean(values * values, axis=-1, keepdims=True) + epsilon)


def norm_back(upstream, normed, inverse, gain):
    scaled = upstream * gain
    return inverse * (scaled - normed * jnp.mean(scaled * normed, axis=-1, keepdims=True))


def tile_widths(window):
    widths, left = [], window
    while left > 0:
        width = TILE
        while width > 128 and left <= width // 2 - 2 * HALF:
            width //= 2
        widths.append(width)
        left -= width - 2 * HALF
    return widths


def tile_starts(window):
    starts, at = [], 0
    for width in tile_widths(window):
        starts.append(at)
        at += width - 2 * HALF
    return starts


def spread_keys(array, axis, fill=0):
    window = array.shape[axis]
    widths, starts = tile_widths(window), tile_starts(window)
    pads = [(0, 0)] * array.ndim
    pads[axis] = (HALF, starts[-1] + widths[-1] - HALF - window)
    padded = jnp.pad(array, pads, constant_values=fill)
    return jnp.concatenate(
        [lax.slice_in_dim(padded, s, s + w, axis=axis) for s, w in zip(starts, widths)], axis=axis
    )


def own_columns(window):
    own = []
    for s, w in zip(tile_starts(window), tile_widths(window)):
        own += [HALF <= c < w - HALF and s + c - HALF < window for c in range(w)]
    return own


def spread_rows(rim, rows):
    steps = rows.shape[0] // LANES
    rest = rows.shape[1:]
    ahead = jnp.zeros((steps - RIM,) + rest, rows.dtype)
    blocks = jnp.concatenate([ahead, rim.astype(rows.dtype), rows]).reshape((LANES + 1, steps) + rest)
    ext = jnp.concatenate([blocks[:LANES, steps - RIM :], blocks[1:]], axis=1)
    return jnp.swapaxes(ext, 0, 1).reshape(((steps + RIM) * LANES,) + rest)


def taps_kernel(fwd_ref, bwd_ref, t_ref, tt_ref):
    for source, target in ((fwd_ref, t_ref), (bwd_ref, tt_ref)):
        for a in range(QTAPS):
            row = jnp.broadcast_to(source[0, a : a + 1, :], (TILE, TILE))
            turned = pltpu.roll(row, 0, 1, stride=1, stride_axis=0)
            target[0, a * TILE : (a + 1) * TILE, :] = turned.astype(jnp.bfloat16)


def band_matrices(conv_kernel, scale):
    heads = conv_kernel.shape[0]
    taps = conv_kernel * scale
    gap = jnp.zeros((heads, QTAPS, TILE - KTAPS), jnp.float32)
    fwd = jnp.concatenate([taps[:, :, HALF:], gap, taps[:, :, :HALF]], axis=2)
    flipped = taps[:, :, ::-1]
    bwd = jnp.concatenate([flipped[:, :, HALF:], gap, flipped[:, :, :HALF]], axis=2)
    big = jax.ShapeDtypeStruct((heads, QTAPS * TILE, TILE), jnp.bfloat16)
    small_spec = pl.BlockSpec((1, QTAPS, TILE), lambda h: (h, 0, 0))
    big_spec = pl.BlockSpec((1, QTAPS * TILE, TILE), lambda h: (h, 0, 0))
    return pl.pallas_call(
        taps_kernel,
        grid=(heads,),
        in_specs=[small_spec, small_spec],
        out_specs=[big_spec, big_spec],
        out_shape=[big, big],
        compiler_params=pltpu.CompilerParams(vmem_limit_bytes=RING_VMEM),
        name="band_matrices",
    )(fwd, bwd)


def band(ref, h, w):
    if w == TILE:
        return ref[h]
    return jnp.concatenate([ref[h, a * TILE : a * TILE + w, :w] for a in range(QTAPS)], axis=0)


CONTRACT_LAST = (((1,), (1,)), ((), ()))
CONTRACT_FIRST = (((0,), (0,)), ((), ()))


def dot(lhs, rhs, dims=(((1,), (0,)), ((), ()))):
    return lax.dot_general(lhs, rhs, dims, preferred_element_type=jnp.float32)


def attend_kernel(
    widths, q_ref, k_ref, v_ref, t_ref, mask_ref, bias_ref, mix_ref, gain_ref, rows_ref, cols_ref, plain_ref,
    o_ref, p_ref, m_ref, att_ref, qs_ref, ks_ref, vs_ref,
    logit_ref, mixed_ref,
):
    heads, rows = p_ref.shape[0], p_ref.shape[1]
    size = q_ref.shape[1] // heads
    chunk = min(rows, 64)
    first = pl.program_id(0) * heads
    for source, pick, target in ((q_ref, rows_ref, qs_ref), (k_ref, cols_ref, ks_ref), (v_ref, cols_ref, vs_ref)):
        moved = dot(pick[...], source[...]).astype(jnp.bfloat16)
        for h in range(heads):
            target[h] = moved[:, h * size : (h + 1) * size]
    for h in range(heads):
        at = 0
        for w in widths:
            s = dot(qs_ref[h], ks_ref[h, at : at + w, :], CONTRACT_LAST)
            m_ref[h, :, at : at + w] = s.astype(jnp.bfloat16) * mask_ref[:, at : at + w]
            at += w
        at = 0
        for w in widths:
            lhs = jnp.concatenate(
                [m_ref[h, (RIM - a) * LANES : (RIM - a) * LANES + rows, at : at + w] for a in range(QTAPS)], axis=1
            )
            logit_ref[:, at : at + w] = dot(lhs, band(t_ref, h, w)) + bias_ref[:, at : at + w]
            at += w
        for r in range(0, rows, chunk):
            logits = logit_ref[r : r + chunk, :]
            powers = jnp.exp(logits - jnp.max(logits, axis=-1, keepdims=True))
            p_ref[h, r : r + chunk, :] = powers / jnp.sum(powers, axis=-1, keepdims=True)
    outs = []
    for h in range(heads):
        low = h - h % 2
        w0, w1 = mix_ref[first + h, 0], mix_ref[first + h, 1]
        for r in range(0, rows, chunk):
            mixed_ref[r : r + chunk, :] = (
                w0 * p_ref[low, r : r + chunk, :] + w1 * p_ref[low + 1, r : r + chunk, :]
            ).astype(jnp.bfloat16)
        att = dot(mixed_ref[...], vs_ref[h])
        att_ref[h] = att
        outs.append(att * inverse_rms(att))
    normed = (jnp.concatenate(outs, axis=1) * gain_ref[...]).astype(jnp.bfloat16)
    o_ref[...] = dot(plain_ref[...], normed, CONTRACT_FIRST).astype(jnp.bfloat16)


def together(heads):
    return 4 if heads % 4 == 0 else heads


def attend(q, k, v, t, mask, bias, head_mix, gain, picks, heads, widths):
    groups, tall, width = q.shape
    window = k.shape[1]
    size = width // heads
    ext, cols = mask.shape[1:]
    rows = bias.shape[1]
    some = together(heads)
    natural = lambda n: pl.BlockSpec((None, n, some * size), lambda g, n: (n, 0, g))
    per_head = lambda a, b: pl.BlockSpec((None, some, a, b), lambda g, n: (n, g, 0, 0))
    whole = lambda a, b: pl.BlockSpec((None, a, b), lambda g, n: (n, 0, 0))
    fixed = lambda array: pl.BlockSpec(array.shape, lambda g, n: (0, 0))
    stacked = lambda a, b, kind: jax.ShapeDtypeStruct((groups, heads, a, b), kind)
    return pl.pallas_call(
        functools.partial(attend_kernel, widths),
        grid=(heads // some, groups),
        in_specs=[
            natural(tall),
            natural(window),
            natural(window),
            pl.BlockSpec((some, QTAPS * TILE, TILE), lambda g, n: (g, 0, 0)),
            whole(ext, cols),
            whole(rows, cols),
            pl.BlockSpec(memory_space=pltpu.SMEM),
            pl.BlockSpec((1, some * size), lambda g, n: (0, g)),
        ]
        + [fixed(pick) for pick in picks],
        out_specs=[
            natural(rows),
            per_head(rows, cols),
            per_head(ext, cols),
            per_head(rows, size),
            per_head(ext, size),
            per_head(cols, size),
            per_head(cols, size),
        ],
        out_shape=[
            jax.ShapeDtypeStruct((groups, rows, width), jnp.bfloat16),
            stacked(rows, cols, jnp.float32),
            stacked(ext, cols, jnp.bfloat16),
            stacked(rows, size, jnp.float32),
            stacked(ext, size, jnp.bfloat16),
            stacked(cols, size, jnp.bfloat16),
            stacked(cols, size, jnp.bfloat16),
        ],
        scratch_shapes=[pltpu.VMEM((rows, cols), jnp.float32), pltpu.VMEM((rows, cols), jnp.bfloat16)],
        compiler_params=pltpu.CompilerParams(vmem_limit_bytes=VMEM_LIMIT),
        cost_estimate=pl.CostEstimate(
            flops=2 * groups * heads * rows * cols * (QTAPS * TILE + 3 * size),
            bytes_accessed=groups * heads * cols * (4 * rows + 2 * ext) + heads * QTAPS * TILE * TILE * 2,
            transcendentals=groups * heads * rows * cols,
        ),
        name="attend",
    )(q, k, v, t, mask, bias, head_mix, gain, *picks)


def attend_back_kernel(
    widths, go_ref, att_ref, p_ref, m_ref, q_ref, k_ref, v_ref, tt_ref, mask_ref, mix_ref, gain_ref,
    rows_ref, cols_ref, plain_ref,
    gq_ref, gk_ref, gv_ref, tap_ref, gmix_ref, ggain_ref,
    ga_ref, gpm_ref, mixed_ref, gc_ref, gs_ref, gqs_ref, gks_ref, gvs_ref,
):
    heads, rows, cols = p_ref.shape
    ext, size = q_ref.shape[1:]
    chunk = min(rows, 64)
    first = pl.program_id(0) * heads
    rim = RIM * LANES

    @pl.when(pl.program_id(1) == 0)
    def _():
        gmix_ref[...] = jnp.zeros(gmix_ref.shape, jnp.float32)
        tap_ref[...] = jnp.zeros(tap_ref.shape, jnp.float32)
        ggain_ref[...] = jnp.zeros(ggain_ref.shape, jnp.float32)

    upper = go_ref[...].astype(jnp.bfloat16)
    lower = (go_ref[...] - upper.astype(jnp.float32)).astype(jnp.bfloat16)
    grad_o = dot(plain_ref[...], upper) + dot(plain_ref[...], lower)
    gains = []
    for h in range(heads):
        att = att_ref[h]
        inverse = inverse_rms(att)
        normed = att * inverse
        grad = grad_o[:, h * size : (h + 1) * size]
        gains.append(jnp.sum(grad * normed, axis=0, keepdims=True))
        ga_ref[h] = norm_back(grad, normed, inverse, gain_ref[:, h * size : (h + 1) * size]).astype(jnp.bfloat16)
    ggain_ref[0:1, :] += jnp.concatenate(gains, axis=1)

    gc_ref[:, :rim, :] = jnp.zeros((2, rim, cols), jnp.bfloat16)
    gc_ref[:, rim + rows :, :] = jnp.zeros((2, rim, cols), jnp.bfloat16)
    for low in range(0, heads, 2):
        mix = [[mix_ref[first + low + o, t] for t in range(2)] for o in range(2)]
        for o in range(2):
            for r in range(0, rows, chunk):
                mixed_ref[r : r + chunk, :] = (
                    mix[o][0] * p_ref[low, r : r + chunk, :] + mix[o][1] * p_ref[low + 1, r : r + chunk, :]
                ).astype(jnp.bfloat16)
            grad = dot(ga_ref[low + o], mixed_ref[...], CONTRACT_FIRST)
            gvs_ref[(low + o) * size : (low + o + 1) * size, :] = grad.astype(jnp.bfloat16)
            gpm_ref[o] = dot(ga_ref[low + o], v_ref[low + o], CONTRACT_LAST)
        sums = [[jnp.zeros((1, 1), jnp.float32) for t in range(2)] for o in range(2)]
        for r in range(0, rows, chunk):
            for t in range(2):
                probs = p_ref[low + t, r : r + chunk, :]
                ups = [gpm_ref[o, r : r + chunk, :] for o in range(2)]
                dots = [jnp.sum(probs * up, axis=-1, keepdims=True) for up in ups]
                for o in range(2):
                    sums[o][t] = sums[o][t] + jnp.sum(dots[o], axis=0, keepdims=True)
                down = mix[0][t] * dots[0] + mix[1][t] * dots[1]
                grad = probs * (mix[0][t] * ups[0] + mix[1][t] * ups[1] - down)
                gc_ref[t, rim + r : rim + r + chunk, :] = grad.astype(jnp.bfloat16)
        for o in range(2):
            for t in range(2):
                gmix_ref[low // 2, 2 * o + t : 2 * o + t + 1, :] += jnp.broadcast_to(sums[o][t], (1, 128))
        for t in range(2):
            h = low + t
            at = 0
            for w in widths:
                lhs = jnp.concatenate(
                    [gc_ref[t, a * LANES : a * LANES + ext, at : at + w] for a in range(QTAPS)], axis=1
                )
                back = dot(lhs, band(tt_ref, h, w))
                gs_ref[:, at : at + w] = back.astype(jnp.bfloat16) * mask_ref[:, at : at + w]
                at += w
            gqs_ref[:, h * size : (h + 1) * size] = dot(gs_ref[...], k_ref[h]).astype(jnp.bfloat16)
            gks_ref[h * size : (h + 1) * size, :] = dot(q_ref[h], gs_ref[...], CONTRACT_FIRST).astype(jnp.bfloat16)
            for width in sorted(set(widths)):
                spans, at = [], 0
                for w in widths:
                    if w == width:
                        spans.append(at)
                    at += w
                turned = jnp.concatenate(
                    [gc_ref[t, rim : rim + rows, at : at + width].T for at in spans], axis=1
                )
                for a in range(QTAPS):
                    start = (RIM - a) * LANES
                    maps = jnp.concatenate(
                        [m_ref[h, start : start + rows, at : at + width] for at in spans], axis=0
                    )
                    cross = dot(turned, maps)
                    total = cross[:8]
                    for r in range(8, width, 8):
                        total = total + pltpu.roll(cross[r : r + 8], width - r, 1)
                    tap_ref[h, a, :, :128] += total[:, :128]
                    tap_ref[h, a, :, 128:] += total[:, width - 128 :]
    gq_ref[...] = dot(rows_ref[...], gqs_ref[...], CONTRACT_FIRST).astype(jnp.bfloat16)
    gk_ref[...] = dot(cols_ref[...], gks_ref[...], (((0,), (1,)), ((), ()))).astype(jnp.bfloat16)
    gv_ref[...] = dot(cols_ref[...], gvs_ref[...], (((0,), (1,)), ((), ()))).astype(jnp.bfloat16)


def attend_back(go, att, p, m, q, k, v, tt, mask, head_mix, gain, picks, tall, window, widths):
    groups, heads, ext, size = q.shape
    rows, cols = p.shape[2:]
    width = heads * size
    some = together(heads)
    natural = lambda n: pl.BlockSpec((None, n, some * size), lambda g, n: (n, 0, g))
    per_head = lambda a, b: pl.BlockSpec((None, some, a, b), lambda g, n: (n, g, 0, 0))
    fixed = lambda array: pl.BlockSpec(array.shape, lambda g, n: (0, 0))
    moved = lambda n: jax.ShapeDtypeStruct((groups, n, width), jnp.bfloat16)
    return pl.pallas_call(
        functools.partial(attend_back_kernel, widths),
        grid=(heads // some, groups),
        in_specs=[
            natural(rows),
            per_head(rows, size),
            per_head(rows, cols),
            per_head(ext, cols),
            per_head(ext, size),
            per_head(cols, size),
            per_head(cols, size),
            pl.BlockSpec((some, QTAPS * TILE, TILE), lambda g, n: (g, 0, 0)),
            pl.BlockSpec((None, ext, cols), lambda g, n: (n, 0, 0)),
            pl.BlockSpec(memory_space=pltpu.SMEM),
            pl.BlockSpec((1, some * size), lambda g, n: (0, g)),
        ]
        + [fixed(pick) for pick in picks],
        out_specs=[
            natural(tall),
            natural(window),
            natural(window),
            pl.BlockSpec((some, QTAPS, 8, TILE), lambda g, n: (g, 0, 0, 0)),
            pl.BlockSpec((some // 2, 8, 128), lambda g, n: (g, 0, 0)),
            pl.BlockSpec((8, some * size), lambda g, n: (0, g)),
        ],
        out_shape=[
            moved(tall),
            moved(window),
            moved(window),
            jax.ShapeDtypeStruct((heads, QTAPS, 8, TILE), jnp.float32),
            jax.ShapeDtypeStruct((heads // 2, 8, 128), jnp.float32),
            jax.ShapeDtypeStruct((8, width), jnp.float32),
        ],
        scratch_shapes=[
            pltpu.VMEM((some, rows, size), jnp.bfloat16),
            pltpu.VMEM((2, rows, cols), jnp.float32),
            pltpu.VMEM((rows, cols), jnp.bfloat16),
            pltpu.VMEM((2, rows + 2 * RIM * LANES, cols), jnp.bfloat16),
            pltpu.VMEM((ext, cols), jnp.bfloat16),
            pltpu.VMEM((ext, some * size), jnp.bfloat16),
            pltpu.VMEM((some * size, cols), jnp.bfloat16),
            pltpu.VMEM((some * size, cols), jnp.bfloat16),
        ],
        compiler_params=pltpu.CompilerParams(vmem_limit_bytes=VMEM_LIMIT),
        cost_estimate=pl.CostEstimate(
            flops=2 * groups * heads * rows * cols * (2 * QTAPS * TILE + 5 * size),
            bytes_accessed=groups * heads * cols * (4 * rows + 2 * ext) + heads * QTAPS * TILE * TILE * 2,
            transcendentals=0,
        ),
        name="attend_back",
    )(go, att, p, m, q, k, v, tt, mask, head_mix, gain, *picks)


def gather_rows(array):
    if lax.axis_size("mp") != 2:
        return lax.all_gather(array, "mp", axis=1, tiled=True)
    other = lax.ppermute(array, "mp", [(0, 1), (1, 0)])
    first = lax.axis_index("mp") == 0
    return jnp.concatenate([jnp.where(first, array, other), jnp.where(first, other, array)], axis=1)


def scatter_rows(array, after=None):
    count = lax.axis_size("mp")
    own = array.shape[1] // count
    if count != 2:
        return lax.psum_scatter(array, "mp", scatter_dimension=1, tiled=True).astype(jnp.float32)
    first = lax.axis_index("mp") == 0
    head, tail = array[:, :own], array[:, own:]
    arrived = lax.ppermute(jnp.where(first, tail, head), "mp", [(0, 1), (1, 0)])
    if after is not None:
        arrived, _ = lax.optimization_barrier((arrived, after))
    return jnp.where(first, head, tail).astype(jnp.float32) + arrived.astype(jnp.float32)


def join_small(parts):
    lanes, tile = 128, 16
    joined = jnp.concatenate([part.reshape(-1) for part in parts])
    rows = -(-joined.size // (tile * lanes)) * tile
    return jnp.pad(joined, (0, rows * lanes - joined.size)).reshape(rows, lanes)


def split_small(joined, parts):
    flat, result, at = joined.reshape(-1), [], 0
    for part in parts:
        result.append(flat[at : at + part.size].reshape(part.shape))
        at += part.size
    return result


def scatter_tokens(part):
    part = part.astype(jnp.bfloat16)
    return lax.psum_scatter(part, ("dp", "seq"), scatter_dimension=0, tiled=True)


def ring_kernel(stages, groups, count, *refs):
    refs = list(refs)
    take = lambda n: [refs.pop(0) for _ in range(n)]
    part_refs = [take(sum(group)) for group in groups]
    share_refs = take(count)
    late_outs = [take(len(group)) for group in groups]
    early_outs = take(count)
    lates, accs, landings = take(len(groups)), take(len(groups)), take(len(groups))
    local_sem, load_sem, pair_sem, add_sem, ring_sem, side_sem = refs
    dp, z = lax.axis_index("dp"), lax.axis_index("seq")
    x, core = dp // 2, dp % 2
    nodes = 2 * stages
    here = z + x * (nodes - 1 - 2 * z)

    def place(r):
        rx = r // stages
        return rx, r + rx * (nodes - 1 - 2 * r)

    def peer(r):
        rx, rz = place(r % nodes)
        return {"dp": 2 * rx + core, "seq": rz}

    right, left, side = peer(here + 1), peer(here + nodes - 1), {"dp": 2 * x + 1 - core, "seq": z}
    ways = ((0, right, -1), (1, left, 1))

    loads = []
    for g, parts in enumerate(part_refs):
        for i, ref in enumerate(parts):
            size = ref.shape[1] // 2
            for part in range(2):
                copy = pltpu.make_async_copy(
                    ref.at[:, pl.ds(part * size, size)], lates[g].at[:, part, i], load_sem.at[len(loads)]
                )
                copy.start()
                loads.append(copy)

    barrier = pltpu.get_barrier_semaphore()
    for device in (left, right, side):
        pl.semaphore_signal(barrier, inc=1, device_id=device, device_id_type=pl.DeviceIdType.MESH)
    pl.semaphore_wait(barrier, 3)

    def remote(src, dst, sems, device):
        return pltpu.make_async_remote_copy(
            src_ref=src,
            dst_ref=dst,
            send_sem=sems.at[0],
            recv_sem=sems.at[1],
            device_id=device,
            device_id_type=pl.DeviceIdType.MESH,
        )

    def node(r):
        rx, rz = place((r + 2 * nodes) % nodes)
        return rx * stages + rz

    def number(r):
        rx, rz = place((r + 2 * nodes) % nodes)
        return (2 * rx + core) * stages + rz

    early_entries, late_entries = [], []
    for source, out in zip(share_refs, early_outs):
        size = source.shape[0] // 2
        early_entries.append(
            (
                lambda part, source=source, size=size: source.at[pl.ds(part * size, size)],
                lambda r, part, out=out, size=size: out.at[number(r), pl.ds(part * size, size)],
            )
        )
    for g, group in enumerate(groups):
        at = 0
        for n, out in zip(group, late_outs[g]):
            size = accs[g].shape[3]
            late_entries.append(
                (
                    lambda part, g=g, at=at, n=n: accs[g].at[node(here), part, pl.ds(at, n)],
                    lambda r, part, out=out, n=n, size=size: out.at[
                        pl.ds(0, n), number(r), pl.ds(part * size, size)
                    ],
                )
            )
            at += n
    sends = []

    def gather_step(i, entry, k):
        own, piece = entry
        arriving = []
        for part, device, sign in ways:
            dst = piece(here + sign * k, part)
            src = own(part) if k == 0 else dst
            if k < nodes - 1:
                copy = remote(src, dst, ring_sem.at[i, k, part], device)
                copy.start()
                sends.append((copy, False))
                arriving.append(copy)
            across = remote(src, dst, side_sem.at[i, k, part], side)
            across.start()
            sends.append((across, True))
        return arriving

    def keep_own(i, entry):
        own, piece = entry
        for part in range(2):
            copy = pltpu.make_async_copy(own(part), piece(here, part), local_sem.at[i, part])
            copy.start()
            locals_.append(copy)

    def early_step(k):
        arriving = []
        for i, entry in enumerate(early_entries):
            arriving += gather_step(i, entry, k)
        return arriving

    def add_into(total, other):
        total[...] = (total[...].astype(jnp.float32) + other[...].astype(jnp.float32)).astype(jnp.bfloat16)

    locals_ = []
    for copy in loads:
        copy.wait()
    pairs = []
    for g in range(len(groups)):
        for rx in range(2):
            copy = remote(
                lates[g].at[pl.ds((2 * rx + 1 - core) * stages, stages)],
                accs[g].at[pl.ds(rx * stages, stages)],
                pair_sem.at[g, rx],
                side,
            )
            copy.start()
            pairs.append(copy)
    waiting = early_step(0)
    for i, entry in enumerate(early_entries):
        keep_own(i, entry)
    for copy in pairs:
        copy.wait_recv()
    for g in range(len(groups)):
        members = accs[g].shape[2]

        @pl.loop(0, nodes * 2 * members)
        def _(j, g=g, members=members):
            to, part, i = j // (2 * members), (j // members) % 2, j % members
            own = (2 * (to // stages) + core) * stages + to % stages
            add_into(accs[g].at[to, part, i], lates[g].at[own, part, i])

    for k in range(nodes - 1):
        adding = []
        for g in range(len(groups)):
            for part, device, sign in ways:
                copy = remote(
                    accs[g].at[node(here + sign * (1 + k)), part], landings[g].at[k, part], add_sem.at[g, k, part], device
                )
                copy.start()
                sends.append((copy, False))
                adding.append(copy)
        for g in range(len(groups)):
            for part, _, sign in ways:
                adding[2 * g + part].wait_recv()
                to = node(here + sign * (2 + k))
                for i in range(accs[g].shape[2]):
                    add_into(accs[g].at[to, part, i], landings[g].at[k, part, i])
        for copy in waiting:
            copy.wait_recv()
        waiting = early_step(k + 1)

    for i, entry in enumerate(late_entries):
        keep_own(count + i, entry)
    for k in range(nodes):
        waiting = []
        for i, entry in enumerate(late_entries):
            waiting += gather_step(count + i, entry, k)
        for copy in waiting:
            copy.wait_recv()
    for copy in pairs:
        copy.wait_send()
    for copy, both in sends:
        copy.wait_send()
        if both:
            copy.wait_recv()
    for copy in locals_:
        copy.wait()


def finish_sums(partials, shares):
    stages = lax.axis_size("seq")
    nodes = 2 * stages
    count = len(shares)
    groups = [[len(members) for members in group] for group in partials]
    flat = [[part for members in group for part in members] for group in partials]
    shapes = [(group[0].shape[0] // (2 * nodes), group[0].shape[1]) for group in flat]
    outs = [
        jax.ShapeDtypeStruct((n, 2 * nodes) + shape, jnp.bfloat16)
        for group, shape in zip(groups, shapes)
        for n in group
    ] + [jax.ShapeDtypeStruct((2 * nodes,) + share.shape, share.dtype) for share in shares]
    anywhere = pl.BlockSpec(memory_space=pl.ANY)
    dma = pltpu.SemaphoreType.DMA
    scratch = lambda n: [
        pltpu.VMEM(n + (sum(group), rows // 2, width), jnp.bfloat16) for group, (rows, width) in zip(groups, shapes)
    ]
    arrays = [part.reshape(2 * nodes, shape[0], shape[1]) for group, shape in zip(flat, shapes) for part in group]
    total = len(outs)
    return pl.pallas_call(
        functools.partial(ring_kernel, stages, groups, count),
        in_specs=[anywhere] * (len(arrays) + count),
        out_specs=[anywhere] * total,
        out_shape=outs,
        scratch_shapes=scratch((2 * nodes, 2))
        + scratch((nodes, 2))
        + scratch((nodes - 1, 2))
        + [
            dma((total, 2)),
            dma((2 * len(arrays),)),
            dma((len(groups), 2, 2)),
            dma((len(groups), nodes - 1, 2, 2)),
            dma((total, nodes - 1, 2, 2)),
            dma((total, nodes, 2, 2)),
        ],
        compiler_params=pltpu.CompilerParams(
            collective_id=0, has_side_effects=True, vmem_limit_bytes=RING_VMEM
        ),
        cost_estimate=pl.CostEstimate(flops=0, bytes_accessed=600 * 1024 * 1024, transcendentals=0),
        name="finish_sums",
    )(*arrays, *shares)


def feed_forward_kernel(h2_ref, gy_ref, wi_ref, wd_ref, out_ref, back_ref, down_ref, in_ref, turned_ref, acc_ref, bacc_ref):
    step, steps = pl.program_id(0), pl.num_programs(0)
    block = wd_ref.shape[0]

    @pl.when(step == 0)
    def _():
        turned_ref[...] = h2_ref[...].T
        acc_ref[...] = jnp.zeros(acc_ref.shape, jnp.float32)
        bacc_ref[...] = jnp.zeros(bacc_ref.shape, jnp.float32)

    gate_up = dot(h2_ref[...], wi_ref[...])
    gate, upward = gate_up[:, :block], gate_up[:, block:]
    sigma = 1.0 / (1.0 + jnp.exp(-gate))
    silu_gate = gate * sigma
    hidden = (silu_gate * upward).astype(jnp.bfloat16)
    grad_hidden = dot(gy_ref[...], wd_ref[...], CONTRACT_LAST)
    grad_gate = grad_hidden * upward * sigma * (1.0 + gate * (1.0 - sigma))
    grads = jnp.concatenate([grad_gate, grad_hidden * silu_gate], axis=1).astype(jnp.bfloat16)
    down_ref[...] = dot(hidden, gy_ref[...], CONTRACT_FIRST).astype(jnp.bfloat16)
    in_ref[...] = dot(turned_ref[...], grads).astype(jnp.bfloat16)
    acc_ref[...] += dot(hidden, wd_ref[...])
    bacc_ref[...] += dot(grads, wi_ref[...], CONTRACT_LAST)

    @pl.when(step == steps - 1)
    def _():
        out_ref[...] = acc_ref[...].astype(jnp.bfloat16)
        back_ref[...] = bacc_ref[...].astype(jnp.bfloat16)


def feed_forward(h2, gy, w_in, w_down, block):
    rows, model = h2.shape
    hidden = w_down.shape[0]
    whole = pl.BlockSpec((rows, model), lambda j: (0, 0))
    tall = pl.BlockSpec((model, 2 * block), lambda j: (0, j))
    flat = pl.BlockSpec((block, model), lambda j: (j, 0))
    shape = lambda a, b: jax.ShapeDtypeStruct((a, b), jnp.bfloat16)
    return pl.pallas_call(
        feed_forward_kernel,
        grid=(hidden // block,),
        in_specs=[whole, whole, tall, flat],
        out_specs=[whole, whole, flat, tall],
        out_shape=[shape(rows, model), shape(rows, model), shape(hidden, model), shape(model, 2 * hidden)],
        scratch_shapes=[
            pltpu.VMEM((model, rows), jnp.bfloat16),
            pltpu.VMEM((rows, model), jnp.float32),
            pltpu.VMEM((rows, model), jnp.float32),
        ],
        compiler_params=pltpu.CompilerParams(vmem_limit_bytes=VMEM_LIMIT),
        cost_estimate=pl.CostEstimate(
            flops=18 * rows * model * hidden, bytes_accessed=12 * model * hidden, transcendentals=rows * hidden
        ),
        name="feed_forward",
    )(h2, gy, w_in, w_down)


def project_back_kernel(behind_rows, h1_ref, gq_ref, gk_ref, gv_ref, w_ref, pq_ref, pk_ref, pv_ref, gh_ref, gain_ref):
    groups, window = h1_ref.shape[:2]
    tall = gq_ref.shape[1]
    totals = None
    for g in range(groups):
        h1 = h1_ref[g]
        turned = h1.T
        parts = [
            dot(turned[:, window - tall :], gq_ref[g]),
            dot(turned, gk_ref[g]),
            dot(turned, gv_ref[g]),
        ]
        totals = parts if totals is None else [total + part for total, part in zip(totals, parts)]
        grad = dot(gk_ref[g], w_ref[1], CONTRACT_LAST) + dot(gv_ref[g], w_ref[2], CONTRACT_LAST)
        early = grad[: window - tall]
        late = grad[window - tall :] + dot(gq_ref[g], w_ref[0], CONTRACT_LAST)
        gh_ref[g, : window - tall, :] = early.astype(jnp.bfloat16)
        gh_ref[g, window - tall :, :] = late.astype(jnp.bfloat16)
        gain = jnp.sum(early * h1[: window - tall].astype(jnp.float32), axis=0, keepdims=True) + jnp.sum(
            late * h1[window - tall :].astype(jnp.float32), axis=0, keepdims=True
        )
        gain_ref[g : g + 1, :] = gain
    for ref, total in zip((pq_ref, pk_ref, pv_ref), totals):
        ref[...] = total.astype(jnp.bfloat16)


def project_back(h1, gq, gk, gv, weights, block):
    groups, window, model = h1.shape
    tall, width = gq.shape[1:]
    whole = lambda n: pl.BlockSpec((groups, n, width), lambda j: (0, 0, 0))
    cut = pl.BlockSpec((groups, window, block), lambda j: (0, 0, j))
    part = pl.BlockSpec((block, width), lambda j: (j, 0))
    return pl.pallas_call(
        functools.partial(project_back_kernel, window - tall),
        grid=(model // block,),
        in_specs=[cut, whole(tall), whole(window), whole(window), pl.BlockSpec((3, block, width), lambda j: (0, j, 0))],
        out_specs=[part, part, part, cut, pl.BlockSpec((groups, block), lambda j: (0, j))],
        out_shape=[jax.ShapeDtypeStruct((model, width), jnp.bfloat16)] * 3
        + [
            jax.ShapeDtypeStruct((groups, window, model), jnp.bfloat16),
            jax.ShapeDtypeStruct((groups, model), jnp.float32),
        ],
        compiler_params=pltpu.CompilerParams(vmem_limit_bytes=RING_VMEM),
        cost_estimate=pl.CostEstimate(
            flops=4 * groups * model * width * (2 * window + tall),
            bytes_accessed=4 * groups * window * (model + width) + 12 * model * width,
            transcendentals=0,
        ),
        name="project_back",
    )(h1, gq, gk, gv, weights)


def sum_peers(array):
    if lax.axis_size("mp") != 2:
        return lax.psum(array, "mp")
    return array + lax.ppermute(array, "mp", [(0, 1), (1, 0)])


def matmul(spec, lhs, rhs):
    return jnp.einsum(spec, lhs, rhs, preferred_element_type=jnp.float32)


def shards(
    block_input,
    segment,
    norm1_gain,
    w_qkv,
    conv_kernel,
    head_mix,
    out_gain,
    w_out,
    norm2_gain,
    w_in,
    w_down,
    grad_y,
):
    mp_count = lax.axis_size("mp")
    seq_count = lax.axis_size("seq")
    groups, own_rows, model = block_input.shape
    stretch = own_rows * mp_count
    rows = groups * stretch
    heads = conv_kernel.shape[0]
    local_width = w_qkv.shape[2]
    size = local_width // heads
    ff_local = w_down.shape[0]
    score_scale = size ** (-0.5)
    behind = min(-(-(LONGEST - 1) // stretch), seq_count - 1)
    window = (behind + 1) * stretch
    widths = tile_widths(window)
    flat = lambda array: array.reshape((rows,) + array.shape[2:])
    grouped = lambda array: array.reshape((groups, stretch) + array.shape[1:])

    seq_start = lax.axis_index("seq") * stretch
    ids = segment[:, 0]
    padded_ids = jnp.pad(ids, ((0, 0), (window - stretch, 0)), constant_values=-1)
    key_ids = lax.dynamic_slice_in_dim(padded_ids, seq_start, window, 1)
    key_pos = seq_start - (window - stretch) + jnp.arange(window, dtype=jnp.int32)
    ext_ids = jnp.pad(ids, ((0, 0), (RIM, 0)), constant_values=-2)
    ext_ids = lax.dynamic_slice_in_dim(ext_ids, seq_start, stretch + RIM, 1)
    ext_pos = seq_start - RIM + jnp.arange(stretch + RIM, dtype=jnp.int32)
    row_ids = jax.vmap(lambda v: spread_rows(v[:RIM], v[RIM:]))(ext_ids)
    row_pos = spread_rows(ext_pos[:RIM], ext_pos[RIM:])
    col_ids = spread_keys(key_ids, 1, -1)
    col_pos = spread_keys(key_pos, 0, 1 << 20)
    valid = (col_pos[None, None, :] <= row_pos[None, :, None]) & (
        row_ids[:, :, None] == col_ids[:, None, :]
    )
    own_cols = jnp.asarray(own_columns(window))
    mask = valid.astype(jnp.bfloat16)
    bias = jnp.where(valid[:, RIM * LANES :] & own_cols[None, None, :], 0.0, -jnp.inf)
    taps, taps_back = band_matrices(conv_kernel, score_scale)
    tall = LANES + stretch
    spot = jnp.arange(tall, dtype=jnp.int32)
    row_order = spread_rows(spot[LANES - RIM : LANES], spot[LANES:])
    pick_rows = (row_order[:, None] == spot[None, :]).astype(jnp.bfloat16)
    pick_plain = pick_rows[RIM * LANES :, LANES:]
    key_order = spread_keys(jnp.arange(window, dtype=jnp.int32), 0, -1)
    pick_cols = (key_order[:, None] == jnp.arange(window, dtype=jnp.int32)[None, :]).astype(jnp.bfloat16)
    picks = [pick_rows, pick_cols, pick_plain]

    input_float = block_input.astype(jnp.float32)
    inverse_one = inverse_rms(input_float)
    normed_one = input_float * inverse_one
    share = (normed_one * norm1_gain).astype(jnp.bfloat16)
    block = min(512, ff_local)
    w_in_blocks = jnp.swapaxes(w_in.reshape(model, 2, ff_local // block, block), 1, 2).reshape(model, 2 * ff_local)
    h1_blocks = [gather_rows(share)]
    for step in range(behind):
        share = from_behind(share, "seq", 1)
        h1_blocks[-1], share, w_in_blocks = lax.optimization_barrier((h1_blocks[-1], share, w_in_blocks))
        h1_blocks.append(gather_rows(share))
    h1_blocks[-1], grad_rows = lax.optimization_barrier((h1_blocks[-1], grad_y))
    grad_full = flat(gather_rows(grad_rows))
    w_q, w_k, w_v = w_qkv[:, 0], w_qkv[:, 1], w_qkv[:, 2]
    h1_all = jnp.concatenate(h1_blocks[::-1], axis=1)
    h1_ext = h1_all[:, window - tall :]
    project = lambda block, weight: matmul("grd,dc->grc", block, weight).astype(jnp.bfloat16)
    queries, keys, values = project(h1_ext, w_q), project(h1_all, w_k), project(h1_all, w_v)
    queries, grad_full = lax.optimization_barrier((queries, grad_full))
    gain_row = out_gain.reshape(1, local_width)
    mixed_out, probs, maps, att, q_heads, k_heads, v_heads = attend(
        queries, keys, values, taps, mask, bias, head_mix, gain_row, picks, heads, widths
    )
    mixed_out = flat(mixed_out)
    branch = scatter_rows(grouped(matmul("rc,cd->rd", mixed_out, w_out).astype(jnp.bfloat16)))
    resid = input_float + branch
    inverse_two = inverse_rms(resid)
    normed_two = resid * inverse_two
    h2 = flat(gather_rows((normed_two * norm2_gain).astype(jnp.bfloat16)))
    mlp_part, back_part, part_down, part_in = feed_forward(h2, grad_full, w_in_blocks, w_down, block)
    share_in = scatter_tokens(part_in)
    output = (resid + scatter_rows(grouped(mlp_part))).astype(jnp.bfloat16)

    grad_float = grad_y.astype(jnp.float32)
    grad_h2 = scatter_rows(grouped(back_part))
    part_gain_two = jnp.sum(grad_h2 * normed_two, axis=(0, 1))
    grad_resid = grad_float + norm_back(grad_h2, normed_two, inverse_two, norm2_gain)

    branch_grad = flat(gather_rows(grad_resid.astype(jnp.bfloat16)))
    splits = model // local_width
    part_out = matmul("rc,rsd->scd", mixed_out, branch_grad.reshape(rows, splits, model // splits)).astype(jnp.bfloat16)
    grad_mixed = grouped(matmul("rd,cd->rc", branch_grad, w_out))
    grad_q, grad_k, grad_v, tap_sums, mix_sums, gain_sums = attend_back(
        grad_mixed, att, probs, maps, q_heads, k_heads, v_heads, taps_back, mask, head_mix, gain_row, picks,
        tall, window, widths,
    )
    part_gain_out = gain_sums[0]
    bands = jnp.concatenate([tap_sums[..., TILE - HALF :], tap_sums[..., : HALF + 8]], axis=3)
    part_kernel = score_scale * sum(bands[:, :, i, i : i + KTAPS] for i in range(8))[..., ::-1]
    part_mix = mix_sums[:, :4, 0].reshape(heads, 2)
    wide = model // local_width
    part_q, part_k, part_v, grad_h1_all, gain_rows = project_back(
        h1_all, grad_q, grad_k, grad_v, jnp.swapaxes(w_qkv, 0, 1), math.gcd(model, 256)
    )
    partials = [part_q, part_k, part_v, part_out.reshape(model, local_width)]
    part_gain_one = jnp.sum(gain_rows, axis=0) / norm1_gain
    grad_blocks = grad_h1_all.reshape(groups * (behind + 1), stretch, model)

    small = [part_gain_one, part_gain_two, part_kernel, part_mix, part_gain_out]
    share_in = share_in.reshape(-1, ff_local // block, 2, block // 128, 128)
    share_in = jnp.swapaxes(share_in, 2, 3).reshape(-1, 128)
    grad_qkv, grad_out, grad_down, grad_in, every = finish_sums(
        [[partials[:3], partials[3:]], [[part_down]]], [share_in, join_small(small)]
    )
    grad_qkv = jnp.swapaxes(grad_qkv.reshape(3, model, local_width), 0, 1).astype(jnp.float32)
    grad_out = grad_out.reshape(wide, local_width, local_width)
    grad_out = jnp.swapaxes(grad_out, 0, 1).reshape(local_width, model).astype(jnp.float32)
    grad_in = grad_in.astype(jnp.float32).reshape(model, ff_local // 128, 2, 128)
    grad_in = jnp.swapaxes(grad_in, 1, 2).reshape(w_in.shape)
    grad_down = grad_down.astype(jnp.float32).reshape(w_down.shape)

    grad_blocks = scatter_rows(grad_blocks, every).reshape(groups, behind + 1, own_rows, model)
    grad_h1 = grad_blocks[:, 0]
    for step in range(1, behind + 1):
        grad_h1 = from_behind(grad_h1.astype(jnp.bfloat16), "seq", -1).astype(jnp.float32) + grad_blocks[:, step]
    grad_input = grad_resid + norm_back(grad_h1, normed_one, inverse_one, norm1_gain)

    gain_one, gain_two, grad_kernel, grad_mix, grad_gain_out = split_small(jnp.sum(every, axis=0), small)
    gain_sums = sum_peers(jnp.stack([gain_one, gain_two]))
    return (
        output,
        grad_input,
        gain_sums[0],
        grad_qkv,
        grad_kernel,
        grad_mix,
        grad_gain_out,
        grad_out,
        gain_sums[1],
        grad_in,
        grad_down,
    )


def solution(mesh):
    placed = (
        P(None, ("dp", "seq", "mp"), None),
        P(None, "dp", None),
        P(),
        P(None, None, "mp"),
        P("mp", None, None),
        P("mp", None),
        P("mp"),
        P("mp", None),
        P(),
        P(None, None, "mp"),
        P("mp", None),
        P(None, ("dp", "seq", "mp"), None),
    )
    return jax.shard_map(
        shards,
        mesh=mesh,
        in_specs=placed,
        out_specs=(
            P(None, ("dp", "seq", "mp"), None),
            P(None, ("dp", "seq", "mp"), None),
            P(),
            P(None, None, "mp"),
            P("mp", None, None),
            P("mp", None),
            P("mp"),
            P("mp", None),
            P(),
            P(None, None, "mp"),
            P("mp", None),
        ),
        check_vma=False,
    )
```

```python
import functools
import math

import jax
import jax.numpy as jnp
from jax import lax
from jax.experimental import pallas as pl
from jax.experimental.pallas import tpu as pltpu
from jax.sharding import PartitionSpec as P

QTAPS = 6
KTAPS = 11
LONGEST = 512
RIM = QTAPS - 1
HALF = KTAPS // 2
TILE = 256
OWN = TILE - 2 * HALF
LANES = 16

epsilon = 1e-05
VMEM_LIMIT = 58 * 1024 * 1024
RING_VMEM = 50 * 1024 * 1024


def from_behind(value, axis, steps):
    count = lax.axis_size(axis)
    first, last = (max(0, -steps), min(count, count - steps))
    return lax.ppermute(value, axis, [(source, source + steps) for source in range(first, last)])


def inverse_rms(values):
    return lax.rsqrt(jnp.mean(values * values, axis=-1, keepdims=True) + epsilon)


def norm_back(upstream, normed, inverse, gain):
    scaled = upstream * gain
    return inverse * (scaled - normed * jnp.mean(scaled * normed, axis=-1, keepdims=True))


def tile_widths(window):
    widths, left = [], window
    while left > 0:
        width = TILE
        while width > 128 and left <= width // 2 - 2 * HALF:
            width //= 2
        widths.append(width)
        left -= width - 2 * HALF
    return widths


def tile_starts(window):
    starts, at = [], 0
    for width in tile_widths(window):
        starts.append(at)
        at += width - 2 * HALF
    return starts


def spread_keys(array, axis, fill=0):
    window = array.shape[axis]
    widths, starts = tile_widths(window), tile_starts(window)
    pads = [(0, 0)] * array.ndim
    pads[axis] = (HALF, starts[-1] + widths[-1] - HALF - window)
    padded = jnp.pad(array, pads, constant_values=fill)
    return jnp.concatenate(
        [lax.slice_in_dim(padded, s, s + w, axis=axis) for s, w in zip(starts, widths)], axis=axis
    )


def own_columns(window):
    own = []
    for s, w in zip(tile_starts(window), tile_widths(window)):
        own += [HALF <= c < w - HALF and s + c - HALF < window for c in range(w)]
    return own


def spread_rows(rim, rows):
    steps = rows.shape[0] // LANES
    rest = rows.shape[1:]
    ahead = jnp.zeros((steps - RIM,) + rest, rows.dtype)
    blocks = jnp.concatenate([ahead, rim.astype(rows.dtype), rows]).reshape((LANES + 1, steps) + rest)
    ext = jnp.concatenate([blocks[:LANES, steps - RIM :], blocks[1:]], axis=1)
    return jnp.swapaxes(ext, 0, 1).reshape(((steps + RIM) * LANES,) + rest)


def taps_kernel(fwd_ref, bwd_ref, t_ref, tt_ref):
    for source, target in ((fwd_ref, t_ref), (bwd_ref, tt_ref)):
        for a in range(QTAPS):
            row = jnp.broadcast_to(source[0, a : a + 1, :], (TILE, TILE))
            turned = pltpu.roll(row, 0, 1, stride=1, stride_axis=0)
            target[0, a * TILE : (a + 1) * TILE, :] = turned.astype(jnp.bfloat16)


def band_matrices(conv_kernel, scale):
    heads = conv_kernel.shape[0]
    taps = conv_kernel * scale
    gap = jnp.zeros((heads, QTAPS, TILE - KTAPS), jnp.float32)
    fwd = jnp.concatenate([taps[:, :, HALF:], gap, taps[:, :, :HALF]], axis=2)
    flipped = taps[:, :, ::-1]
    bwd = jnp.concatenate([flipped[:, :, HALF:], gap, flipped[:, :, :HALF]], axis=2)
    big = jax.ShapeDtypeStruct((heads, QTAPS * TILE, TILE), jnp.bfloat16)
    small_spec = pl.BlockSpec((1, QTAPS, TILE), lambda h: (h, 0, 0))
    big_spec = pl.BlockSpec((1, QTAPS * TILE, TILE), lambda h: (h, 0, 0))
    return pl.pallas_call(
        taps_kernel,
        grid=(heads,),
        in_specs=[small_spec, small_spec],
        out_specs=[big_spec, big_spec],
        out_shape=[big, big],
        compiler_params=pltpu.CompilerParams(vmem_limit_bytes=RING_VMEM),
        name="band_matrices",
    )(fwd, bwd)


def band(ref, h, w):
    if w == TILE:
        return ref[h]
    return jnp.concatenate([ref[h, a * TILE : a * TILE + w, :w] for a in range(QTAPS)], axis=0)


CONTRACT_LAST = (((1,), (1,)), ((), ()))
CONTRACT_FIRST = (((0,), (0,)), ((), ()))


def dot(lhs, rhs, dims=(((1,), (0,)), ((), ()))):
    return lax.dot_general(lhs, rhs, dims, preferred_element_type=jnp.float32)


def attend_kernel(
    widths, q_ref, k_ref, v_ref, t_ref, mask_ref, bias_ref, mix_ref, gain_ref, rows_ref, cols_ref, plain_ref,
    o_ref, p_ref, m_ref, att_ref, qs_ref, ks_ref, vs_ref,
    logit_ref, mixed_ref,
):
    heads, rows = p_ref.shape[0], p_ref.shape[1]
    size = q_ref.shape[1] // heads
    chunk = min(rows, 64)
    first = pl.program_id(0) * heads
    for source, pick, target in ((q_ref, rows_ref, qs_ref), (k_ref, cols_ref, ks_ref), (v_ref, cols_ref, vs_ref)):
        moved = dot(pick[...], source[...]).astype(jnp.bfloat16)
        for h in range(heads):
            target[h] = moved[:, h * size : (h + 1) * size]
    for h in range(heads):
        at = 0
        for w in widths:
            s = dot(qs_ref[h], ks_ref[h, at : at + w, :], CONTRACT_LAST)
            m_ref[h, :, at : at + w] = s.astype(jnp.bfloat16) * mask_ref[:, at : at + w]
            at += w
        at = 0
        for w in widths:
            lhs = jnp.concatenate(
                [m_ref[h, (RIM - a) * LANES : (RIM - a) * LANES + rows, at : at + w] for a in range(QTAPS)], axis=1
            )
            logit_ref[:, at : at + w] = dot(lhs, band(t_ref, h, w)) + bias_ref[:, at : at + w]
            at += w
        for r in range(0, rows, chunk):
            logits = logit_ref[r : r + chunk, :]
            powers = jnp.exp(logits - jnp.max(logits, axis=-1, keepdims=True))
            p_ref[h, r : r + chunk, :] = powers * (1.0 / jnp.sum(powers, axis=-1, keepdims=True))
    outs = []
    for h in range(heads):
        low = h - h % 2
        w0, w1 = mix_ref[first + h, 0], mix_ref[first + h, 1]
        for r in range(0, rows, chunk):
            mixed_ref[r : r + chunk, :] = (
                w0 * p_ref[low, r : r + chunk, :] + w1 * p_ref[low + 1, r : r + chunk, :]
            ).astype(jnp.bfloat16)
        att = dot(mixed_ref[...], vs_ref[h])
        att_ref[h] = att
        outs.append(att * inverse_rms(att))
    normed = (jnp.concatenate(outs, axis=1) * gain_ref[...]).astype(jnp.bfloat16)
    o_ref[...] = dot(plain_ref[...], normed, CONTRACT_FIRST).astype(jnp.bfloat16)


def together(heads):
    return 4 if heads % 4 == 0 else heads


def attend(q, k, v, t, mask, bias, head_mix, gain, picks, heads, widths):
    groups, tall, width = q.shape
    window = k.shape[1]
    size = width // heads
    ext, cols = mask.shape[1:]
    rows = bias.shape[1]
    some = together(heads)
    natural = lambda n: pl.BlockSpec((None, n, some * size), lambda g, n: (n, 0, g))
    per_head = lambda a, b: pl.BlockSpec((None, some, a, b), lambda g, n: (n, g, 0, 0))
    whole = lambda a, b: pl.BlockSpec((None, a, b), lambda g, n: (n, 0, 0))
    fixed = lambda array: pl.BlockSpec(array.shape, lambda g, n: (0, 0))
    stacked = lambda a, b, kind: jax.ShapeDtypeStruct((groups, heads, a, b), kind)
    return pl.pallas_call(
        functools.partial(attend_kernel, widths),
        grid=(heads // some, groups),
        in_specs=[
            natural(tall),
            natural(window),
            natural(window),
            pl.BlockSpec((some, QTAPS * TILE, TILE), lambda g, n: (g, 0, 0)),
            whole(ext, cols),
            whole(rows, cols),
            pl.BlockSpec(memory_space=pltpu.SMEM),
            pl.BlockSpec((1, some * size), lambda g, n: (0, g)),
        ]
        + [fixed(pick) for pick in picks],
        out_specs=[
            natural(rows),
            per_head(rows, cols),
            per_head(ext, cols),
            per_head(rows, size),
            per_head(ext, size),
            per_head(cols, size),
            per_head(cols, size),
        ],
        out_shape=[
            jax.ShapeDtypeStruct((groups, rows, width), jnp.bfloat16),
            stacked(rows, cols, jnp.float32),
            stacked(ext, cols, jnp.bfloat16),
            stacked(rows, size, jnp.float32),
            stacked(ext, size, jnp.bfloat16),
            stacked(cols, size, jnp.bfloat16),
            stacked(cols, size, jnp.bfloat16),
        ],
        scratch_shapes=[pltpu.VMEM((rows, cols), jnp.float32), pltpu.VMEM((rows, cols), jnp.bfloat16)],
        compiler_params=pltpu.CompilerParams(vmem_limit_bytes=VMEM_LIMIT),
        cost_estimate=pl.CostEstimate(
            flops=2 * groups * heads * rows * cols * (QTAPS * TILE + 3 * size),
            bytes_accessed=groups * heads * cols * (4 * rows + 2 * ext) + heads * QTAPS * TILE * TILE * 2,
            transcendentals=groups * heads * rows * cols,
        ),
        name="attend",
    )(q, k, v, t, mask, bias, head_mix, gain, *picks)


def attend_back_kernel(
    widths, go_ref, att_ref, p_ref, m_ref, q_ref, k_ref, v_ref, tt_ref, mask_ref, mix_ref, gain_ref,
    rows_ref, cols_ref, plain_ref,
    gq_ref, gk_ref, gv_ref, tap_ref, gmix_ref, ggain_ref,
    ga_ref, gpm_ref, mixed_ref, gc_ref, gs_ref, gqs_ref, gks_ref, gvs_ref,
):
    heads, rows, cols = p_ref.shape
    ext, size = q_ref.shape[1:]
    chunk = min(rows, 64)
    first = pl.program_id(0) * heads
    rim = RIM * LANES

    @pl.when(pl.program_id(1) == 0)
    def _():
        gmix_ref[...] = jnp.zeros(gmix_ref.shape, jnp.float32)
        tap_ref[...] = jnp.zeros(tap_ref.shape, jnp.float32)
        ggain_ref[...] = jnp.zeros(ggain_ref.shape, jnp.float32)

    upper = go_ref[...].astype(jnp.bfloat16)
    lower = (go_ref[...] - upper.astype(jnp.float32)).astype(jnp.bfloat16)
    grad_o = dot(plain_ref[...], upper) + dot(plain_ref[...], lower)
    gains = []
    for h in range(heads):
        att = att_ref[h]
        inverse = inverse_rms(att)
        normed = att * inverse
        grad = grad_o[:, h * size : (h + 1) * size]
        gains.append(jnp.sum(grad * normed, axis=0, keepdims=True))
        ga_ref[h] = norm_back(grad, normed, inverse, gain_ref[:, h * size : (h + 1) * size]).astype(jnp.bfloat16)
    ggain_ref[0:1, :] += jnp.concatenate(gains, axis=1)

    gc_ref[:, :rim, :] = jnp.zeros((2, rim, cols), jnp.bfloat16)
    gc_ref[:, rim + rows :, :] = jnp.zeros((2, rim, cols), jnp.bfloat16)
    for low in range(0, heads, 2):
        mix = [[mix_ref[first + low + o, t] for t in range(2)] for o in range(2)]
        for o in range(2):
            for r in range(0, rows, chunk):
                mixed_ref[r : r + chunk, :] = (
                    mix[o][0] * p_ref[low, r : r + chunk, :] + mix[o][1] * p_ref[low + 1, r : r + chunk, :]
                ).astype(jnp.bfloat16)
            grad = dot(ga_ref[low + o], mixed_ref[...], CONTRACT_FIRST)
            gvs_ref[(low + o) * size : (low + o + 1) * size, :] = grad.astype(jnp.bfloat16)
            gpm_ref[o] = dot(ga_ref[low + o], v_ref[low + o], CONTRACT_LAST)
        sums = [[jnp.zeros((1, 1), jnp.float32) for t in range(2)] for o in range(2)]
        for r in range(0, rows, chunk):
            for t in range(2):
                probs = p_ref[low + t, r : r + chunk, :]
                ups = [gpm_ref[o, r : r + chunk, :] for o in range(2)]
                dots = [jnp.sum(probs * up, axis=-1, keepdims=True) for up in ups]
                for o in range(2):
                    sums[o][t] = sums[o][t] + jnp.sum(dots[o], axis=0, keepdims=True)
                down = mix[0][t] * dots[0] + mix[1][t] * dots[1]
                grad = probs * (mix[0][t] * ups[0] + mix[1][t] * ups[1] - down)
                gc_ref[t, rim + r : rim + r + chunk, :] = grad.astype(jnp.bfloat16)
        for o in range(2):
            for t in range(2):
                gmix_ref[low // 2, 2 * o + t : 2 * o + t + 1, :] += jnp.broadcast_to(sums[o][t], (1, 128))
        for t in range(2):
            h = low + t
            at = 0
            for w in widths:
                lhs = jnp.concatenate(
                    [gc_ref[t, a * LANES : a * LANES + ext, at : at + w] for a in range(QTAPS)], axis=1
                )
                back = dot(lhs, band(tt_ref, h, w))
                gs_ref[:, at : at + w] = back.astype(jnp.bfloat16) * mask_ref[:, at : at + w]
                at += w
            gqs_ref[:, h * size : (h + 1) * size] = dot(gs_ref[...], k_ref[h]).astype(jnp.bfloat16)
            gks_ref[h * size : (h + 1) * size, :] = dot(q_ref[h], gs_ref[...], CONTRACT_FIRST).astype(jnp.bfloat16)
            for width in sorted(set(widths)):
                spans, at = [], 0
                for w in widths:
                    if w == width:
                        spans.append(at)
                    at += w
                turned = jnp.concatenate(
                    [gc_ref[t, rim : rim + rows, at : at + width].T for at in spans], axis=1
                )
                for a in range(QTAPS):
                    start = (RIM - a) * LANES
                    maps = jnp.concatenate(
                        [m_ref[h, start : start + rows, at : at + width] for at in spans], axis=0
                    )
                    cross = dot(turned, maps)
                    total = cross[:8]
                    for r in range(8, width, 8):
                        total = total + pltpu.roll(cross[r : r + 8], width - r, 1)
                    tap_ref[h, a, :, :128] += total[:, :128]
                    tap_ref[h, a, :, 128:] += total[:, width - 128 :]
    gq_ref[...] = dot(rows_ref[...], gqs_ref[...], CONTRACT_FIRST).astype(jnp.bfloat16)
    gk_ref[...] = dot(cols_ref[...], gks_ref[...], (((0,), (1,)), ((), ()))).astype(jnp.bfloat16)
    gv_ref[...] = dot(cols_ref[...], gvs_ref[...], (((0,), (1,)), ((), ()))).astype(jnp.bfloat16)


def attend_back(go, att, p, m, q, k, v, tt, mask, head_mix, gain, picks, tall, window, widths):
    groups, heads, ext, size = q.shape
    rows, cols = p.shape[2:]
    width = heads * size
    some = together(heads)
    natural = lambda n: pl.BlockSpec((None, n, some * size), lambda g, n: (n, 0, g))
    per_head = lambda a, b: pl.BlockSpec((None, some, a, b), lambda g, n: (n, g, 0, 0))
    fixed = lambda array: pl.BlockSpec(array.shape, lambda g, n: (0, 0))
    moved = lambda n: jax.ShapeDtypeStruct((groups, n, width), jnp.bfloat16)
    return pl.pallas_call(
        functools.partial(attend_back_kernel, widths),
        grid=(heads // some, groups),
        in_specs=[
            natural(rows),
            per_head(rows, size),
            per_head(rows, cols),
            per_head(ext, cols),
            per_head(ext, size),
            per_head(cols, size),
            per_head(cols, size),
            pl.BlockSpec((some, QTAPS * TILE, TILE), lambda g, n: (g, 0, 0)),
            pl.BlockSpec((None, ext, cols), lambda g, n: (n, 0, 0)),
            pl.BlockSpec(memory_space=pltpu.SMEM),
            pl.BlockSpec((1, some * size), lambda g, n: (0, g)),
        ]
        + [fixed(pick) for pick in picks],
        out_specs=[
            natural(tall),
            natural(window),
            natural(window),
            pl.BlockSpec((some, QTAPS, 8, TILE), lambda g, n: (g, 0, 0, 0)),
            pl.BlockSpec((some // 2, 8, 128), lambda g, n: (g, 0, 0)),
            pl.BlockSpec((8, some * size), lambda g, n: (0, g)),
        ],
        out_shape=[
            moved(tall),
            moved(window),
            moved(window),
            jax.ShapeDtypeStruct((heads, QTAPS, 8, TILE), jnp.float32),
            jax.ShapeDtypeStruct((heads // 2, 8, 128), jnp.float32),
            jax.ShapeDtypeStruct((8, width), jnp.float32),
        ],
        scratch_shapes=[
            pltpu.VMEM((some, rows, size), jnp.bfloat16),
            pltpu.VMEM((2, rows, cols), jnp.float32),
            pltpu.VMEM((rows, cols), jnp.bfloat16),
            pltpu.VMEM((2, rows + 2 * RIM * LANES, cols), jnp.bfloat16),
            pltpu.VMEM((ext, cols), jnp.bfloat16),
            pltpu.VMEM((ext, some * size), jnp.bfloat16),
            pltpu.VMEM((some * size, cols), jnp.bfloat16),
            pltpu.VMEM((some * size, cols), jnp.bfloat16),
        ],
        compiler_params=pltpu.CompilerParams(vmem_limit_bytes=VMEM_LIMIT),
        cost_estimate=pl.CostEstimate(
            flops=2 * groups * heads * rows * cols * (2 * QTAPS * TILE + 5 * size),
            bytes_accessed=groups * heads * cols * (4 * rows + 2 * ext) + heads * QTAPS * TILE * TILE * 2,
            transcendentals=0,
        ),
        name="attend_back",
    )(go, att, p, m, q, k, v, tt, mask, head_mix, gain, *picks)


def gather_rows(array):
    if lax.axis_size("mp") != 2:
        return lax.all_gather(array, "mp", axis=1, tiled=True)
    other = lax.ppermute(array, "mp", [(0, 1), (1, 0)])
    first = lax.axis_index("mp") == 0
    return jnp.concatenate([jnp.where(first, array, other), jnp.where(first, other, array)], axis=1)


def scatter_rows(array, after=None):
    count = lax.axis_size("mp")
    own = array.shape[1] // count
    if count != 2:
        return lax.psum_scatter(array, "mp", scatter_dimension=1, tiled=True).astype(jnp.float32)
    first = lax.axis_index("mp") == 0
    head, tail = array[:, :own], array[:, own:]
    arrived = lax.ppermute(jnp.where(first, tail, head), "mp", [(0, 1), (1, 0)])
    if after is not None:
        arrived, _ = lax.optimization_barrier((arrived, after))
    return jnp.where(first, head, tail).astype(jnp.float32) + arrived.astype(jnp.float32)


def join_small(parts):
    lanes, tile = 128, 16
    joined = jnp.concatenate([part.reshape(-1) for part in parts])
    rows = -(-joined.size // (tile * lanes)) * tile
    return jnp.pad(joined, (0, rows * lanes - joined.size)).reshape(rows, lanes)


def split_small(joined, parts):
    flat, result, at = joined.reshape(-1), [], 0
    for part in parts:
        result.append(flat[at : at + part.size].reshape(part.shape))
        at += part.size
    return result


def scatter_tokens(part):
    part = part.astype(jnp.bfloat16)
    return lax.psum_scatter(part, ("dp", "seq"), scatter_dimension=0, tiled=True)


def ring_kernel(stages, groups, splits, count, *refs):
    refs = list(refs)
    take = lambda n: [refs.pop(0) for _ in range(n)]
    part_refs = [take(sum(group)) for group in groups]
    share_refs = take(count)
    (grads_ref,) = take(1)
    late_outs = [take(len(group)) for group in groups]
    early_outs = take(count)
    (grad_out,) = take(1)
    lates, accs, landings = take(len(groups)), take(len(groups)), take(len(groups))
    mine_ref, peers_ref, total_ref, mine_sem, peer_sem = take(5)
    local_sem, load_sem, pair_sem, add_sem, ring_sem, side_sem = refs
    dp, z = lax.axis_index("dp"), lax.axis_index("seq")
    x, core = dp // 2, dp % 2
    nodes = 2 * stages
    here = z + x * (nodes - 1 - 2 * z)

    def place(r):
        rx = r // stages
        return rx, r + rx * (nodes - 1 - 2 * r)

    def peer(r):
        rx, rz = place(r % nodes)
        return {"dp": 2 * rx + core, "seq": rz}

    right, left, side = peer(here + 1), peer(here + nodes - 1), {"dp": 2 * x + 1 - core, "seq": z}
    ways = ((0, right, -1), (1, left, 1))
    mp, mp_count = lax.axis_index("mp"), peers_ref.shape[0] + 1
    mates = [{"mp": (mp + d) % mp_count} for d in range(1, mp_count)]

    def half_index(split, shape, part):
        size = shape[split] // 2
        cut = pl.ds(part * size, size)
        return (cut, slice(None)) if split == 0 else (slice(None), cut)

    loads = []
    for g, parts in enumerate(part_refs):
        for i, ref in enumerate(parts):
            for part in range(2):
                cut = half_index(splits[g], ref.shape[1:], part)
                copy = pltpu.make_async_copy(ref.at[(slice(None),) + cut], lates[g].at[:, part, i], load_sem.at[len(loads)])
                copy.start()
                loads.append(copy)

    barrier = pltpu.get_barrier_semaphore()
    known = [left, right, side] + mates
    for device in known:
        pl.semaphore_signal(barrier, inc=1, device_id=device, device_id_type=pl.DeviceIdType.MESH)
    pl.semaphore_wait(barrier, len(known))

    def remote(src, dst, sems, device):
        return pltpu.make_async_remote_copy(
            src_ref=src,
            dst_ref=dst,
            send_sem=sems.at[0],
            recv_sem=sems.at[1],
            device_id=device,
            device_id_type=pl.DeviceIdType.MESH,
        )

    def node(r):
        rx, rz = place((r + 2 * nodes) % nodes)
        return rx * stages + rz

    def number(r):
        rx, rz = place((r + 2 * nodes) % nodes)
        return (2 * rx + core) * stages + rz

    early_entries, late_entries = [], []
    for source, out in zip(share_refs, early_outs):
        size = source.shape[0] // 2
        early_entries.append(
            (
                lambda part, source=source, size=size: source.at[pl.ds(part * size, size)],
                lambda r, part, out=out, size=size: out.at[number(r), pl.ds(part * size, size)],
            )
        )
    for g, group in enumerate(groups):
        at = 0
        for n, out in zip(group, late_outs[g]):
            late_entries.append(
                (
                    lambda part, g=g, at=at, n=n: accs[g].at[node(here), part, pl.ds(at, n)],
                    lambda r, part, out=out, n=n, g=g: out.at[
                        (pl.ds(0, n), number(r)) + half_index(splits[g], out.shape[2:], part)
                    ],
                )
            )
            at += n
    sends = []

    def gather_step(i, entry, k):
        own, piece = entry
        arriving = []
        for part, device, sign in ways:
            dst = piece(here + sign * k, part)
            src = own(part) if k == 0 else dst
            if k < nodes - 1:
                copy = remote(src, dst, ring_sem.at[i, k, part], device)
                copy.start()
                sends.append((copy, False))
                arriving.append(copy)
            across = remote(src, dst, side_sem.at[i, k, part], side)
            across.start()
            sends.append((across, True))
        return arriving

    def keep_own(i, entry):
        own, piece = entry
        for part in range(2):
            copy = pltpu.make_async_copy(own(part), piece(here, part), local_sem.at[i, part])
            copy.start()
            locals_.append(copy)

    def early_step(k):
        arriving = []
        for i, entry in enumerate(early_entries):
            arriving += gather_step(i, entry, k)
        return arriving

    def add_into(total, other):
        total[...] = (total[...].astype(jnp.float32) + other[...].astype(jnp.float32)).astype(jnp.bfloat16)

    locals_ = []
    for copy in loads:
        copy.wait()
    pairs = []
    for g in range(len(groups)):
        for rx in range(2):
            copy = remote(
                lates[g].at[pl.ds((2 * rx + 1 - core) * stages, stages)],
                accs[g].at[pl.ds(rx * stages, stages)],
                pair_sem.at[g, rx],
                side,
            )
            copy.start()
            pairs.append(copy)
    swaps = []
    for d, device in enumerate(mates):
        copy = remote(grads_ref.at[:, :, (mp + d + 1) % mp_count], peers_ref.at[d], peer_sem.at[d], device)
        copy.start()
        swaps.append(copy)
    mine = pltpu.make_async_copy(grads_ref.at[:, :, mp], mine_ref, mine_sem.at[0])
    mine.start()
    batch, reach, own_rows = mine_ref.shape[:3]
    piece_rows = math.gcd(own_rows, 32)

    def sum_grads():
        mine.wait()
        for copy in swaps:
            copy.wait_recv()

        @pl.loop(0, batch * reach)
        def _(i):
            b, step = i // reach, i % reach
            for j in range(0, own_rows, piece_rows):
                cut = pl.ds(j, piece_rows)
                total = mine_ref[b, step, cut, :].astype(jnp.float32)
                for d in range(mp_count - 1):
                    total = total + peers_ref[d, b, step, cut, :].astype(jnp.float32)
                total_ref[b, step, cut, :] = total

        copy = pltpu.make_async_copy(total_ref, grad_out, mine_sem.at[1])
        copy.start()
        locals_.append(copy)

    waiting = early_step(0)
    for i, entry in enumerate(early_entries):
        keep_own(i, entry)
    for copy in pairs:
        copy.wait_recv()
    for g in range(len(groups)):
        members = accs[g].shape[2]

        @pl.loop(0, nodes * 2 * members)
        def _(j, g=g, members=members):
            to, part, i = j // (2 * members), (j // members) % 2, j % members
            own = (2 * (to // stages) + core) * stages + to % stages
            add_into(accs[g].at[to, part, i], lates[g].at[own, part, i])

    for k in range(nodes - 1):
        adding = []
        for g in range(len(groups)):
            for part, device, sign in ways:
                copy = remote(
                    accs[g].at[node(here + sign * (1 + k)), part], landings[g].at[k, part], add_sem.at[g, k, part], device
                )
                copy.start()
                sends.append((copy, False))
                adding.append(copy)
        for g in range(len(groups)):
            for part, _, sign in ways:
                adding[2 * g + part].wait_recv()
                to = node(here + sign * (2 + k))
                for i in range(accs[g].shape[2]):
                    add_into(accs[g].at[to, part, i], landings[g].at[k, part, i])
        for copy in waiting:
            copy.wait_recv()
        waiting = early_step(k + 1)
        if k == nodes - 2:
            sum_grads()

    for i, entry in enumerate(late_entries):
        keep_own(count + i, entry)
    for k in range(nodes):
        waiting = []
        for i, entry in enumerate(late_entries):
            waiting += gather_step(count + i, entry, k)
        for copy in waiting:
            copy.wait_recv()
    for copy in pairs + swaps:
        copy.wait_send()
    for copy, both in sends:
        copy.wait_send()
        if both:
            copy.wait_recv()
    for copy in locals_:
        copy.wait()


def finish_sums(partials, splits, shares, grads):
    stages, mp_count = lax.axis_size("seq"), lax.axis_size("mp")
    nodes = 2 * stages
    count = len(shares)
    groups = [[len(members) for members in group] for group in partials]
    flat = [[part for members in group for part in members] for group in partials]
    shapes = [(group[0].shape[0] // (2 * nodes), group[0].shape[1]) for group in flat]
    batch, reach, _, own_rows, model = grads.shape
    outs = [
        jax.ShapeDtypeStruct((n, 2 * nodes) + shape, jnp.bfloat16)
        for group, shape in zip(groups, shapes)
        for n in group
    ] + [jax.ShapeDtypeStruct((2 * nodes,) + share.shape, share.dtype) for share in shares]
    total = len(outs)
    outs.append(jax.ShapeDtypeStruct((batch, reach, own_rows, model), jnp.float32))
    anywhere = pl.BlockSpec(memory_space=pl.ANY)
    dma = pltpu.SemaphoreType.DMA
    scratch = lambda n: [
        pltpu.VMEM(
            n + (sum(group), rows // (2 - split), width // (1 + split)), jnp.bfloat16
        )
        for group, split, (rows, width) in zip(groups, splits, shapes)
    ]
    arrays = [part.reshape(2 * nodes, shape[0], shape[1]) for group, shape in zip(flat, shapes) for part in group]
    held = lambda *shape: pltpu.VMEM(shape + (own_rows, model), jnp.bfloat16)
    return pl.pallas_call(
        functools.partial(ring_kernel, stages, groups, splits, count),
        in_specs=[anywhere] * (len(arrays) + count + 1),
        out_specs=[anywhere] * (total + 1),
        out_shape=outs,
        scratch_shapes=scratch((2 * nodes, 2))
        + scratch((nodes, 2))
        + scratch((nodes - 1, 2))
        + [
            held(batch, reach),
            held(mp_count - 1, batch, reach),
            pltpu.VMEM((batch, reach, own_rows, model), jnp.float32),
            dma((2,)),
            dma((mp_count - 1, 2)),
            dma((total, 2)),
            dma((2 * len(arrays),)),
            dma((len(groups), 2, 2)),
            dma((len(groups), nodes - 1, 2, 2)),
            dma((total, nodes - 1, 2, 2)),
            dma((total, nodes, 2, 2)),
        ],
        compiler_params=pltpu.CompilerParams(
            collective_id=0, has_side_effects=True, vmem_limit_bytes=RING_VMEM
        ),
        cost_estimate=pl.CostEstimate(flops=0, bytes_accessed=600 * 1024 * 1024, transcendentals=0),
        name="finish_sums",
    )(*arrays, *shares, grads)


def feed_forward_kernel(h2_ref, gy_ref, wi_ref, wd_ref, hidden_ref, back_ref, in_ref, turned_ref, acc_ref):
    step, steps = pl.program_id(0), pl.num_programs(0)
    block = wd_ref.shape[0]

    @pl.when(step == 0)
    def _():
        turned_ref[...] = h2_ref[...].T
        acc_ref[...] = jnp.zeros(acc_ref.shape, jnp.float32)

    gate_up = dot(h2_ref[...], wi_ref[...])
    gate, upward = gate_up[:, :block], gate_up[:, block:]
    sigma = 1.0 / (1.0 + jnp.exp(-gate))
    silu_gate = gate * sigma
    hidden_ref[...] = (silu_gate * upward).astype(jnp.bfloat16)
    grad_hidden = dot(gy_ref[...], wd_ref[...], CONTRACT_LAST)
    grad_gate = grad_hidden * upward * sigma * (1.0 + gate * (1.0 - sigma))
    grads = jnp.concatenate([grad_gate, grad_hidden * silu_gate], axis=1).astype(jnp.bfloat16)
    in_ref[...] = dot(turned_ref[...], grads).astype(jnp.bfloat16)
    acc_ref[...] += dot(grads, wi_ref[...], CONTRACT_LAST)

    @pl.when(step == steps - 1)
    def _():
        back_ref[...] = acc_ref[...].astype(jnp.bfloat16)


def feed_forward(h2, gy, w_in, w_down, block):
    rows, model = h2.shape
    hidden = w_down.shape[0]
    whole = pl.BlockSpec((rows, model), lambda j: (0, 0))
    tall = pl.BlockSpec((model, 2 * block), lambda j: (0, j))
    flat = pl.BlockSpec((block, model), lambda j: (j, 0))
    shape = lambda a, b: jax.ShapeDtypeStruct((a, b), jnp.bfloat16)
    return pl.pallas_call(
        feed_forward_kernel,
        grid=(hidden // block,),
        in_specs=[whole, whole, tall, flat],
        out_specs=[pl.BlockSpec((rows, block), lambda j: (0, j)), whole, tall],
        out_shape=[shape(rows, hidden), shape(rows, model), shape(model, 2 * hidden)],
        scratch_shapes=[pltpu.VMEM((model, rows), jnp.bfloat16), pltpu.VMEM((rows, model), jnp.float32)],
        compiler_params=pltpu.CompilerParams(vmem_limit_bytes=VMEM_LIMIT),
        cost_estimate=pl.CostEstimate(
            flops=14 * rows * model * hidden, bytes_accessed=10 * model * hidden, transcendentals=rows * hidden
        ),
        name="feed_forward",
    )(h2, gy, w_in, w_down)


def project_back_kernel(behind_rows, h1_ref, gq_ref, gk_ref, gv_ref, w_ref, pq_ref, pk_ref, pv_ref, gh_ref, gain_ref):
    groups, window = h1_ref.shape[:2]
    tall = gq_ref.shape[1]
    totals = None
    for g in range(groups):
        h1 = h1_ref[g]
        turned = h1.T
        parts = [
            dot(turned[:, window - tall :], gq_ref[g]),
            dot(turned, gk_ref[g]),
            dot(turned, gv_ref[g]),
        ]
        totals = parts if totals is None else [total + part for total, part in zip(totals, parts)]
        grad = dot(gk_ref[g], w_ref[1], CONTRACT_LAST) + dot(gv_ref[g], w_ref[2], CONTRACT_LAST)
        early = grad[: window - tall]
        late = grad[window - tall :] + dot(gq_ref[g], w_ref[0], CONTRACT_LAST)
        gh_ref[g, : window - tall, :] = early.astype(jnp.bfloat16)
        gh_ref[g, window - tall :, :] = late.astype(jnp.bfloat16)
        gain = jnp.sum(early * h1[: window - tall].astype(jnp.float32), axis=0, keepdims=True) + jnp.sum(
            late * h1[window - tall :].astype(jnp.float32), axis=0, keepdims=True
        )
        gain_ref[g : g + 1, :] = gain
    for ref, total in zip((pq_ref, pk_ref, pv_ref), totals):
        ref[...] = total.astype(jnp.bfloat16)


def project_back(h1, gq, gk, gv, weights, block):
    groups, window, model = h1.shape
    tall, width = gq.shape[1:]
    whole = lambda n: pl.BlockSpec((groups, n, width), lambda j: (0, 0, 0))
    cut = pl.BlockSpec((groups, window, block), lambda j: (0, 0, j))
    part = pl.BlockSpec((block, width), lambda j: (j, 0))
    return pl.pallas_call(
        functools.partial(project_back_kernel, window - tall),
        grid=(model // block,),
        in_specs=[cut, whole(tall), whole(window), whole(window), pl.BlockSpec((3, block, width), lambda j: (0, j, 0))],
        out_specs=[part, part, part, cut, pl.BlockSpec((groups, block), lambda j: (0, j))],
        out_shape=[jax.ShapeDtypeStruct((model, width), jnp.bfloat16)] * 3
        + [
            jax.ShapeDtypeStruct((groups, window, model), jnp.bfloat16),
            jax.ShapeDtypeStruct((groups, model), jnp.float32),
        ],
        compiler_params=pltpu.CompilerParams(vmem_limit_bytes=40 * 1024 * 1024),
        cost_estimate=pl.CostEstimate(
            flops=4 * groups * model * width * (2 * window + tall),
            bytes_accessed=4 * groups * window * (model + width) + 12 * model * width,
            transcendentals=0,
        ),
        name="project_back",
    )(h1, gq, gk, gv, weights)


def sum_peers(array):
    if lax.axis_size("mp") != 2:
        return lax.psum(array, "mp")
    return array + lax.ppermute(array, "mp", [(0, 1), (1, 0)])


def matmul(spec, lhs, rhs):
    return jnp.einsum(spec, lhs, rhs, preferred_element_type=jnp.float32)


def shards(
    block_input,
    segment,
    norm1_gain,
    w_qkv,
    conv_kernel,
    head_mix,
    out_gain,
    w_out,
    norm2_gain,
    w_in,
    w_down,
    grad_y,
):
    mp_count = lax.axis_size("mp")
    seq_count = lax.axis_size("seq")
    groups, own_rows, model = block_input.shape
    stretch = own_rows * mp_count
    rows = groups * stretch
    heads = conv_kernel.shape[0]
    local_width = w_qkv.shape[2]
    size = local_width // heads
    ff_local = w_down.shape[0]
    score_scale = size ** (-0.5)
    behind = min(-(-(LONGEST - 1) // stretch), seq_count - 1)
    window = (behind + 1) * stretch
    widths = tile_widths(window)
    flat = lambda array: array.reshape((rows,) + array.shape[2:])
    grouped = lambda array: array.reshape((groups, stretch) + array.shape[1:])

    seq_start = lax.axis_index("seq") * stretch
    ids = segment[:, 0]
    padded_ids = jnp.pad(ids, ((0, 0), (window - stretch, 0)), constant_values=-1)
    key_ids = lax.dynamic_slice_in_dim(padded_ids, seq_start, window, 1)
    key_pos = seq_start - (window - stretch) + jnp.arange(window, dtype=jnp.int32)
    ext_ids = jnp.pad(ids, ((0, 0), (RIM, 0)), constant_values=-2)
    ext_ids = lax.dynamic_slice_in_dim(ext_ids, seq_start, stretch + RIM, 1)
    ext_pos = seq_start - RIM + jnp.arange(stretch + RIM, dtype=jnp.int32)
    row_ids = jax.vmap(lambda v: spread_rows(v[:RIM], v[RIM:]))(ext_ids)
    row_pos = spread_rows(ext_pos[:RIM], ext_pos[RIM:])
    col_ids = spread_keys(key_ids, 1, -1)
    col_pos = spread_keys(key_pos, 0, 1 << 20)
    valid = (col_pos[None, None, :] <= row_pos[None, :, None]) & (
        row_ids[:, :, None] == col_ids[:, None, :]
    )
    own_cols = jnp.asarray(own_columns(window))
    mask = valid.astype(jnp.bfloat16)
    bias = jnp.where(valid[:, RIM * LANES :] & own_cols[None, None, :], 0.0, -jnp.inf)
    taps, taps_back = band_matrices(conv_kernel, score_scale)
    tall = LANES + stretch
    spot = jnp.arange(tall, dtype=jnp.int32)
    row_order = spread_rows(spot[LANES - RIM : LANES], spot[LANES:])
    pick_rows = (row_order[:, None] == spot[None, :]).astype(jnp.bfloat16)
    pick_plain = pick_rows[RIM * LANES :, LANES:]
    key_order = spread_keys(jnp.arange(window, dtype=jnp.int32), 0, -1)
    pick_cols = (key_order[:, None] == jnp.arange(window, dtype=jnp.int32)[None, :]).astype(jnp.bfloat16)
    picks = [pick_rows, pick_cols, pick_plain]

    input_float = block_input.astype(jnp.float32)
    inverse_one = inverse_rms(input_float)
    normed_one = input_float * inverse_one
    share = (normed_one * norm1_gain).astype(jnp.bfloat16)
    h1_blocks = [gather_rows(share)]
    for step in range(behind):
        share = from_behind(share, "seq", 1)
        h1_blocks[-1], share = lax.optimization_barrier((h1_blocks[-1], share))
        h1_blocks.append(gather_rows(share))
    h1_blocks[-1], grad_rows = lax.optimization_barrier((h1_blocks[-1], grad_y))
    grad_full = flat(gather_rows(grad_rows))
    w_q, w_k, w_v = w_qkv[:, 0], w_qkv[:, 1], w_qkv[:, 2]
    h1_all = jnp.concatenate(h1_blocks[::-1], axis=1)
    h1_ext = h1_all[:, window - tall :]
    project = lambda block, weight: matmul("grd,dc->grc", block, weight).astype(jnp.bfloat16)
    queries, keys, values = project(h1_ext, w_q), project(h1_all, w_k), project(h1_all, w_v)
    gain_row = out_gain.reshape(1, local_width)
    mixed_out, probs, maps, att, q_heads, k_heads, v_heads = attend(
        queries, keys, values, taps, mask, bias, head_mix, gain_row, picks, heads, widths
    )
    mixed_out, grad_full = lax.optimization_barrier((flat(mixed_out), grad_full))
    branch = grouped(matmul("rc,cd->rd", mixed_out, w_out).astype(jnp.bfloat16))
    branch, w_in_late = lax.optimization_barrier((branch, w_in))
    block = min(512, ff_local)
    w_in_blocks = jnp.swapaxes(w_in_late.reshape(model, 2, ff_local // block, block), 1, 2)
    w_in_blocks = w_in_blocks.reshape(model, 2 * ff_local)
    branch = scatter_rows(branch)
    resid = input_float + branch
    inverse_two = inverse_rms(resid)
    normed_two = resid * inverse_two
    h2 = flat(gather_rows((normed_two * norm2_gain).astype(jnp.bfloat16)))
    hidden, back_part, part_in = feed_forward(h2, grad_full, w_in_blocks, w_down, block)
    share_in = scatter_tokens(part_in)
    part_down = matmul("rf,rd->fd", hidden, grad_full).astype(jnp.bfloat16)
    mlp_part = matmul("rf,fd->rd", hidden, w_down).astype(jnp.bfloat16)

    grad_float = grad_y.astype(jnp.float32)
    grad_h2 = scatter_rows(grouped(back_part))
    part_gain_two = jnp.sum(grad_h2 * normed_two, axis=(0, 1))
    grad_resid = grad_float + norm_back(grad_h2, normed_two, inverse_two, norm2_gain)

    branch_grad = flat(gather_rows(grad_resid.astype(jnp.bfloat16)))
    part_out = matmul("rc,rd->cd", mixed_out, branch_grad).astype(jnp.bfloat16)
    grad_mixed = grouped(matmul("rd,cd->rc", branch_grad, w_out))
    grad_mixed, part_down, mlp_part = lax.optimization_barrier((grad_mixed, part_down, mlp_part))
    output = (resid + scatter_rows(grouped(mlp_part))).astype(jnp.bfloat16)
    grad_q, grad_k, grad_v, tap_sums, mix_sums, gain_sums = attend_back(
        grad_mixed, att, probs, maps, q_heads, k_heads, v_heads, taps_back, mask, head_mix, gain_row, picks,
        tall, window, widths,
    )
    part_gain_out = gain_sums[0]
    bands = jnp.concatenate([tap_sums[..., TILE - HALF :], tap_sums[..., : HALF + 8]], axis=3)
    part_kernel = score_scale * sum(bands[:, :, i, i : i + KTAPS] for i in range(8))[..., ::-1]
    part_mix = mix_sums[:, :4, 0].reshape(heads, 2)
    part_q, part_k, part_v, grad_h1_all, gain_rows = project_back(
        h1_all, grad_q, grad_k, grad_v, jnp.swapaxes(w_qkv, 0, 1), math.gcd(model, 256)
    )
    part_gain_one = jnp.sum(gain_rows, axis=0) / norm1_gain
    grad_blocks = grad_h1_all.reshape(groups, behind + 1, mp_count, own_rows, model)

    small = [part_gain_one, part_gain_two, part_kernel, part_mix, part_gain_out]
    share_in = share_in.reshape(-1, ff_local // block, 2, block // 128, 128)
    share_in = jnp.swapaxes(share_in, 2, 3).reshape(-1, 128)
    grad_qkv, grad_out, grad_down, grad_in, every, grad_blocks = finish_sums(
        [[[part_q, part_k, part_v]], [[part_out]], [[part_down]]], [0, 1, 0], [share_in, join_small(small)], grad_blocks
    )
    grad_qkv = jnp.swapaxes(grad_qkv.reshape(3, model, local_width), 0, 1).astype(jnp.float32)
    grad_out = grad_out.astype(jnp.float32).reshape(w_out.shape)
    grad_in = grad_in.astype(jnp.float32).reshape(model, ff_local // 128, 2, 128)
    grad_in = jnp.swapaxes(grad_in, 1, 2).reshape(w_in.shape)
    grad_down = grad_down.astype(jnp.float32).reshape(w_down.shape)
    grad_h1 = grad_blocks[:, 0]
    for step in range(1, behind + 1):
        grad_h1 = from_behind(grad_h1.astype(jnp.bfloat16), "seq", -1).astype(jnp.float32) + grad_blocks[:, step]
    grad_input = grad_resid + norm_back(grad_h1, normed_one, inverse_one, norm1_gain)

    gain_one, gain_two, grad_kernel, grad_mix, grad_gain_out = split_small(jnp.sum(every, axis=0), small)
    gain_sums = sum_peers(jnp.stack([gain_one, gain_two]))
    return (
        output,
        grad_input,
        gain_sums[0],
        grad_qkv,
        grad_kernel,
        grad_mix,
        grad_gain_out,
        grad_out,
        gain_sums[1],
        grad_in,
        grad_down,
    )


def solution(mesh):
    placed = (
        P(None, ("dp", "seq", "mp"), None),
        P(None, "dp", None),
        P(),
        P(None, None, "mp"),
        P("mp", None, None),
        P("mp", None),
        P("mp"),
        P("mp", None),
        P(),
        P(None, None, "mp"),
        P("mp", None),
        P(None, ("dp", "seq", "mp"), None),
    )
    return jax.shard_map(
        shards,
        mesh=mesh,
        in_specs=placed,
        out_specs=(
            P(None, ("dp", "seq", "mp"), None),
            P(None, ("dp", "seq", "mp"), None),
            P(),
            P(None, None, "mp"),
            P("mp", None, None),
            P("mp", None),
            P("mp"),
            P("mp", None),
            P(),
            P(None, None, "mp"),
            P("mp", None),
        ),
        check_vma=False,
    )
```

```python
import functools
import math

import jax
import jax.numpy as jnp
from jax import lax
from jax.experimental import pallas as pl
from jax.experimental.pallas import tpu as pltpu
from jax.sharding import PartitionSpec as P

QTAPS = 6
KTAPS = 11
LONGEST = 512
RIM = QTAPS - 1
HALF = KTAPS // 2
TILE = 256
OWN = TILE - 2 * HALF
LANES = 16

epsilon = 1e-05
VMEM_LIMIT = 58 * 1024 * 1024
RING_VMEM = 50 * 1024 * 1024


def from_behind(value, axis, steps):
    count = lax.axis_size(axis)
    first, last = (max(0, -steps), min(count, count - steps))
    return lax.ppermute(value, axis, [(source, source + steps) for source in range(first, last)])


def inverse_rms(values):
    return lax.rsqrt(jnp.mean(values * values, axis=-1, keepdims=True) + epsilon)


def norm_back(upstream, normed, inverse, gain):
    scaled = upstream * gain
    return inverse * (scaled - normed * jnp.mean(scaled * normed, axis=-1, keepdims=True))


def tile_widths(window):
    widths, left = [], window
    while left > 0:
        width = TILE
        while width > 128 and left <= width // 2 - 2 * HALF:
            width //= 2
        widths.append(width)
        left -= width - 2 * HALF
    return widths


def tile_starts(window):
    starts, at = [], 0
    for width in tile_widths(window):
        starts.append(at)
        at += width - 2 * HALF
    return starts


def spread_keys(array, axis, fill=0):
    window = array.shape[axis]
    widths, starts = tile_widths(window), tile_starts(window)
    pads = [(0, 0)] * array.ndim
    pads[axis] = (HALF, starts[-1] + widths[-1] - HALF - window)
    padded = jnp.pad(array, pads, constant_values=fill)
    return jnp.concatenate(
        [lax.slice_in_dim(padded, s, s + w, axis=axis) for s, w in zip(starts, widths)], axis=axis
    )


def own_columns(window):
    own = []
    for s, w in zip(tile_starts(window), tile_widths(window)):
        own += [HALF <= c < w - HALF and s + c - HALF < window for c in range(w)]
    return own


def spread_rows(rim, rows):
    steps = rows.shape[0] // LANES
    rest = rows.shape[1:]
    ahead = jnp.zeros((steps - RIM,) + rest, rows.dtype)
    blocks = jnp.concatenate([ahead, rim.astype(rows.dtype), rows]).reshape((LANES + 1, steps) + rest)
    ext = jnp.concatenate([blocks[:LANES, steps - RIM :], blocks[1:]], axis=1)
    return jnp.swapaxes(ext, 0, 1).reshape(((steps + RIM) * LANES,) + rest)


def taps_kernel(fwd_ref, bwd_ref, t_ref, tt_ref):
    for source, target in ((fwd_ref, t_ref), (bwd_ref, tt_ref)):
        for a in range(QTAPS):
            row = jnp.broadcast_to(source[0, a : a + 1, :], (TILE, TILE))
            turned = pltpu.roll(row, 0, 1, stride=1, stride_axis=0)
            target[0, a * TILE : (a + 1) * TILE, :] = turned.astype(jnp.bfloat16)


def band_matrices(conv_kernel, scale):
    heads = conv_kernel.shape[0]
    taps = conv_kernel * scale
    gap = jnp.zeros((heads, QTAPS, TILE - KTAPS), jnp.float32)
    fwd = jnp.concatenate([taps[:, :, HALF:], gap, taps[:, :, :HALF]], axis=2)
    flipped = taps[:, :, ::-1]
    bwd = jnp.concatenate([flipped[:, :, HALF:], gap, flipped[:, :, :HALF]], axis=2)
    big = jax.ShapeDtypeStruct((heads, QTAPS * TILE, TILE), jnp.bfloat16)
    small_spec = pl.BlockSpec((1, QTAPS, TILE), lambda h: (h, 0, 0))
    big_spec = pl.BlockSpec((1, QTAPS * TILE, TILE), lambda h: (h, 0, 0))
    return pl.pallas_call(
        taps_kernel,
        grid=(heads,),
        in_specs=[small_spec, small_spec],
        out_specs=[big_spec, big_spec],
        out_shape=[big, big],
        compiler_params=pltpu.CompilerParams(vmem_limit_bytes=RING_VMEM),
        name="band_matrices",
    )(fwd, bwd)


def band(ref, h, w):
    if w == TILE:
        return ref[h]
    return jnp.concatenate([ref[h, a * TILE : a * TILE + w, :w] for a in range(QTAPS)], axis=0)


CONTRACT_LAST = (((1,), (1,)), ((), ()))
CONTRACT_FIRST = (((0,), (0,)), ((), ()))


def dot(lhs, rhs, dims=(((1,), (0,)), ((), ()))):
    return lax.dot_general(lhs, rhs, dims, preferred_element_type=jnp.float32)


def attend_kernel(
    widths, q_ref, k_ref, v_ref, t_ref, mask_ref, bias_ref, mix_ref, gain_ref, rows_ref, cols_ref, plain_ref,
    o_ref, p_ref, m_ref, att_ref, qs_ref, ks_ref, vs_ref,
    logit_ref, mixed_ref,
):
    heads, rows = p_ref.shape[0], p_ref.shape[1]
    size = q_ref.shape[1] // heads
    chunk = min(rows, 64)
    first = pl.program_id(0) * heads
    for source, pick, target in ((q_ref, rows_ref, qs_ref), (k_ref, cols_ref, ks_ref), (v_ref, cols_ref, vs_ref)):
        moved = dot(pick[...], source[...]).astype(jnp.bfloat16)
        for h in range(heads):
            target[h] = moved[:, h * size : (h + 1) * size]
    for h in range(heads):
        at = 0
        for w in widths:
            s = dot(qs_ref[h], ks_ref[h, at : at + w, :], CONTRACT_LAST)
            m_ref[h, :, at : at + w] = s.astype(jnp.bfloat16) * mask_ref[:, at : at + w]
            at += w
        at = 0
        for w in widths:
            lhs = jnp.concatenate(
                [m_ref[h, (RIM - a) * LANES : (RIM - a) * LANES + rows, at : at + w] for a in range(QTAPS)], axis=1
            )
            logit_ref[:, at : at + w] = dot(lhs, band(t_ref, h, w)) + bias_ref[:, at : at + w]
            at += w
        for r in range(0, rows, chunk):
            logits = logit_ref[r : r + chunk, :]
            powers = jnp.exp(logits - jnp.max(logits, axis=-1, keepdims=True))
            p_ref[h, r : r + chunk, :] = powers * (1.0 / jnp.sum(powers, axis=-1, keepdims=True))
    outs = []
    for h in range(heads):
        low = h - h % 2
        w0, w1 = mix_ref[first + h, 0], mix_ref[first + h, 1]
        for r in range(0, rows, chunk):
            mixed_ref[r : r + chunk, :] = (
                w0 * p_ref[low, r : r + chunk, :] + w1 * p_ref[low + 1, r : r + chunk, :]
            ).astype(jnp.bfloat16)
        att = dot(mixed_ref[...], vs_ref[h])
        att_ref[h] = att
        outs.append(att * inverse_rms(att))
    normed = (jnp.concatenate(outs, axis=1) * gain_ref[...]).astype(jnp.bfloat16)
    o_ref[...] = dot(plain_ref[...], normed, CONTRACT_FIRST).astype(jnp.bfloat16)


def together(heads):
    return 4 if heads % 4 == 0 else heads


def attend(q, k, v, t, mask, bias, head_mix, gain, picks, heads, widths):
    groups, tall, width = q.shape
    window = k.shape[1]
    size = width // heads
    ext, cols = mask.shape[1:]
    rows = bias.shape[1]
    some = together(heads)
    natural = lambda n: pl.BlockSpec((None, n, some * size), lambda g, n: (n, 0, g))
    per_head = lambda a, b: pl.BlockSpec((None, some, a, b), lambda g, n: (n, g, 0, 0))
    whole = lambda a, b: pl.BlockSpec((None, a, b), lambda g, n: (n, 0, 0))
    fixed = lambda array: pl.BlockSpec(array.shape, lambda g, n: (0, 0))
    stacked = lambda a, b, kind: jax.ShapeDtypeStruct((groups, heads, a, b), kind)
    return pl.pallas_call(
        functools.partial(attend_kernel, widths),
        grid=(heads // some, groups),
        in_specs=[
            natural(tall),
            natural(window),
            natural(window),
            pl.BlockSpec((some, QTAPS * TILE, TILE), lambda g, n: (g, 0, 0)),
            whole(ext, cols),
            whole(rows, cols),
            pl.BlockSpec(memory_space=pltpu.SMEM),
            pl.BlockSpec((1, some * size), lambda g, n: (0, g)),
        ]
        + [fixed(pick) for pick in picks],
        out_specs=[
            natural(rows),
            per_head(rows, cols),
            per_head(ext, cols),
            per_head(rows, size),
            per_head(ext, size),
            per_head(cols, size),
            per_head(cols, size),
        ],
        out_shape=[
            jax.ShapeDtypeStruct((groups, rows, width), jnp.bfloat16),
            stacked(rows, cols, jnp.float32),
            stacked(ext, cols, jnp.bfloat16),
            stacked(rows, size, jnp.float32),
            stacked(ext, size, jnp.bfloat16),
            stacked(cols, size, jnp.bfloat16),
            stacked(cols, size, jnp.bfloat16),
        ],
        scratch_shapes=[pltpu.VMEM((rows, cols), jnp.float32), pltpu.VMEM((rows, cols), jnp.bfloat16)],
        compiler_params=pltpu.CompilerParams(vmem_limit_bytes=VMEM_LIMIT),
        cost_estimate=pl.CostEstimate(
            flops=2 * groups * heads * rows * cols * (QTAPS * TILE + 3 * size),
            bytes_accessed=groups * heads * cols * (4 * rows + 2 * ext) + heads * QTAPS * TILE * TILE * 2,
            transcendentals=groups * heads * rows * cols,
        ),
        name="attend",
    )(q, k, v, t, mask, bias, head_mix, gain, *picks)


def attend_back_kernel(
    widths, go_ref, att_ref, p_ref, m_ref, q_ref, k_ref, v_ref, tt_ref, mask_ref, mix_ref, gain_ref,
    rows_ref, cols_ref, plain_ref,
    gq_ref, gk_ref, gv_ref, tap_ref, gmix_ref, ggain_ref,
    ga_ref, gpm_ref, mixed_ref, gc_ref, gs_ref, gqs_ref, gks_ref, gvs_ref,
):
    heads, rows, cols = p_ref.shape
    ext, size = q_ref.shape[1:]
    chunk = min(rows, 64)
    first = pl.program_id(0) * heads
    rim = RIM * LANES

    @pl.when(pl.program_id(1) == 0)
    def _():
        gmix_ref[...] = jnp.zeros(gmix_ref.shape, jnp.float32)
        tap_ref[...] = jnp.zeros(tap_ref.shape, jnp.float32)
        ggain_ref[...] = jnp.zeros(ggain_ref.shape, jnp.float32)

    upper = go_ref[...].astype(jnp.bfloat16)
    lower = (go_ref[...] - upper.astype(jnp.float32)).astype(jnp.bfloat16)
    grad_o = dot(plain_ref[...], upper) + dot(plain_ref[...], lower)
    gains = []
    for h in range(heads):
        att = att_ref[h]
        inverse = inverse_rms(att)
        normed = att * inverse
        grad = grad_o[:, h * size : (h + 1) * size]
        gains.append(jnp.sum(grad * normed, axis=0, keepdims=True))
        ga_ref[h] = norm_back(grad, normed, inverse, gain_ref[:, h * size : (h + 1) * size]).astype(jnp.bfloat16)
    ggain_ref[0:1, :] += jnp.concatenate(gains, axis=1)

    gc_ref[:, :rim, :] = jnp.zeros((2, rim, cols), jnp.bfloat16)
    gc_ref[:, rim + rows :, :] = jnp.zeros((2, rim, cols), jnp.bfloat16)
    for low in range(0, heads, 2):
        mix = [[mix_ref[first + low + o, t] for t in range(2)] for o in range(2)]
        for o in range(2):
            for r in range(0, rows, chunk):
                mixed_ref[r : r + chunk, :] = (
                    mix[o][0] * p_ref[low, r : r + chunk, :] + mix[o][1] * p_ref[low + 1, r : r + chunk, :]
                ).astype(jnp.bfloat16)
            grad = dot(ga_ref[low + o], mixed_ref[...], CONTRACT_FIRST)
            gvs_ref[(low + o) * size : (low + o + 1) * size, :] = grad.astype(jnp.bfloat16)
            gpm_ref[o] = dot(ga_ref[low + o], v_ref[low + o], CONTRACT_LAST)
        sums = [[jnp.zeros((1, 1), jnp.float32) for t in range(2)] for o in range(2)]
        for r in range(0, rows, chunk):
            for t in range(2):
                probs = p_ref[low + t, r : r + chunk, :]
                ups = [gpm_ref[o, r : r + chunk, :] for o in range(2)]
                dots = [jnp.sum(probs * up, axis=-1, keepdims=True) for up in ups]
                for o in range(2):
                    sums[o][t] = sums[o][t] + jnp.sum(dots[o], axis=0, keepdims=True)
                down = mix[0][t] * dots[0] + mix[1][t] * dots[1]
                grad = probs * (mix[0][t] * ups[0] + mix[1][t] * ups[1] - down)
                gc_ref[t, rim + r : rim + r + chunk, :] = grad.astype(jnp.bfloat16)
        for o in range(2):
            for t in range(2):
                gmix_ref[low // 2, 2 * o + t : 2 * o + t + 1, :] += jnp.broadcast_to(sums[o][t], (1, 128))
        for t in range(2):
            h = low + t
            at = 0
            for w in widths:
                lhs = jnp.concatenate(
                    [gc_ref[t, a * LANES : a * LANES + ext, at : at + w] for a in range(QTAPS)], axis=1
                )
                back = dot(lhs, band(tt_ref, h, w))
                gs_ref[:, at : at + w] = back.astype(jnp.bfloat16) * mask_ref[:, at : at + w]
                at += w
            gqs_ref[:, h * size : (h + 1) * size] = dot(gs_ref[...], k_ref[h]).astype(jnp.bfloat16)
            gks_ref[h * size : (h + 1) * size, :] = dot(q_ref[h], gs_ref[...], CONTRACT_FIRST).astype(jnp.bfloat16)
            for width in sorted(set(widths)):
                spans, at = [], 0
                for w in widths:
                    if w == width:
                        spans.append(at)
                    at += w
                turned = jnp.concatenate(
                    [gc_ref[t, rim : rim + rows, at : at + width].T for at in spans], axis=1
                )
                for a in range(QTAPS):
                    start = (RIM - a) * LANES
                    maps = jnp.concatenate(
                        [m_ref[h, start : start + rows, at : at + width] for at in spans], axis=0
                    )
                    cross = dot(turned, maps)
                    total = cross[:8]
                    for r in range(8, width, 8):
                        total = total + pltpu.roll(cross[r : r + 8], width - r, 1)
                    tap_ref[h, a, :, :128] += total[:, :128]
                    tap_ref[h, a, :, 128:] += total[:, width - 128 :]
    gq_ref[...] = dot(rows_ref[...], gqs_ref[...], CONTRACT_FIRST).astype(jnp.bfloat16)
    gk_ref[...] = dot(cols_ref[...], gks_ref[...], (((0,), (1,)), ((), ()))).astype(jnp.bfloat16)
    gv_ref[...] = dot(cols_ref[...], gvs_ref[...], (((0,), (1,)), ((), ()))).astype(jnp.bfloat16)


def attend_back(go, att, p, m, q, k, v, tt, mask, head_mix, gain, picks, tall, window, widths):
    groups, heads, ext, size = q.shape
    rows, cols = p.shape[2:]
    width = heads * size
    some = together(heads)
    natural = lambda n: pl.BlockSpec((None, n, some * size), lambda g, n: (n, 0, g))
    per_head = lambda a, b: pl.BlockSpec((None, some, a, b), lambda g, n: (n, g, 0, 0))
    fixed = lambda array: pl.BlockSpec(array.shape, lambda g, n: (0, 0))
    moved = lambda n: jax.ShapeDtypeStruct((groups, n, width), jnp.bfloat16)
    return pl.pallas_call(
        functools.partial(attend_back_kernel, widths),
        grid=(heads // some, groups),
        in_specs=[
            natural(rows),
            per_head(rows, size),
            per_head(rows, cols),
            per_head(ext, cols),
            per_head(ext, size),
            per_head(cols, size),
            per_head(cols, size),
            pl.BlockSpec((some, QTAPS * TILE, TILE), lambda g, n: (g, 0, 0)),
            pl.BlockSpec((None, ext, cols), lambda g, n: (n, 0, 0)),
            pl.BlockSpec(memory_space=pltpu.SMEM),
            pl.BlockSpec((1, some * size), lambda g, n: (0, g)),
        ]
        + [fixed(pick) for pick in picks],
        out_specs=[
            natural(tall),
            natural(window),
            natural(window),
            pl.BlockSpec((some, QTAPS, 8, TILE), lambda g, n: (g, 0, 0, 0)),
            pl.BlockSpec((some // 2, 8, 128), lambda g, n: (g, 0, 0)),
            pl.BlockSpec((8, some * size), lambda g, n: (0, g)),
        ],
        out_shape=[
            moved(tall),
            moved(window),
            moved(window),
            jax.ShapeDtypeStruct((heads, QTAPS, 8, TILE), jnp.float32),
            jax.ShapeDtypeStruct((heads // 2, 8, 128), jnp.float32),
            jax.ShapeDtypeStruct((8, width), jnp.float32),
        ],
        scratch_shapes=[
            pltpu.VMEM((some, rows, size), jnp.bfloat16),
            pltpu.VMEM((2, rows, cols), jnp.float32),
            pltpu.VMEM((rows, cols), jnp.bfloat16),
            pltpu.VMEM((2, rows + 2 * RIM * LANES, cols), jnp.bfloat16),
            pltpu.VMEM((ext, cols), jnp.bfloat16),
            pltpu.VMEM((ext, some * size), jnp.bfloat16),
            pltpu.VMEM((some * size, cols), jnp.bfloat16),
            pltpu.VMEM((some * size, cols), jnp.bfloat16),
        ],
        compiler_params=pltpu.CompilerParams(vmem_limit_bytes=VMEM_LIMIT),
        cost_estimate=pl.CostEstimate(
            flops=2 * groups * heads * rows * cols * (2 * QTAPS * TILE + 5 * size),
            bytes_accessed=groups * heads * cols * (4 * rows + 2 * ext) + heads * QTAPS * TILE * TILE * 2,
            transcendentals=0,
        ),
        name="attend_back",
    )(go, att, p, m, q, k, v, tt, mask, head_mix, gain, *picks)


def gather_rows(array):
    if lax.axis_size("mp") != 2:
        return lax.all_gather(array, "mp", axis=1, tiled=True)
    other = lax.ppermute(array, "mp", [(0, 1), (1, 0)])
    first = lax.axis_index("mp") == 0
    return jnp.concatenate([jnp.where(first, array, other), jnp.where(first, other, array)], axis=1)


def scatter_rows(array, after=None):
    count = lax.axis_size("mp")
    own = array.shape[1] // count
    if count != 2:
        return lax.psum_scatter(array, "mp", scatter_dimension=1, tiled=True).astype(jnp.float32)
    first = lax.axis_index("mp") == 0
    head, tail = array[:, :own], array[:, own:]
    arrived = lax.ppermute(jnp.where(first, tail, head), "mp", [(0, 1), (1, 0)])
    if after is not None:
        arrived, _ = lax.optimization_barrier((arrived, after))
    return jnp.where(first, head, tail).astype(jnp.float32) + arrived.astype(jnp.float32)


def join_small(parts):
    lanes, tile = 128, 16
    joined = jnp.concatenate([part.reshape(-1) for part in parts])
    rows = -(-joined.size // (tile * lanes)) * tile
    return jnp.pad(joined, (0, rows * lanes - joined.size)).reshape(rows, lanes)


def split_small(joined, parts):
    flat, result, at = joined.reshape(-1), [], 0
    for part in parts:
        result.append(flat[at : at + part.size].reshape(part.shape))
        at += part.size
    return result


def scatter_tokens(part):
    part = part.astype(jnp.bfloat16)
    return lax.psum_scatter(part, ("dp", "seq"), scatter_dimension=0, tiled=True)


def ring_kernel(stages, groups, splits, count, *refs):
    refs = list(refs)
    take = lambda n: [refs.pop(0) for _ in range(n)]
    part_refs = [take(sum(group)) for group in groups]
    share_refs = take(count)
    (grads_ref,) = take(1)
    late_outs = [take(len(group)) for group in groups]
    early_outs = take(count)
    (grad_out,) = take(1)
    lates, accs, landings = take(len(groups)), take(len(groups)), take(len(groups))
    mine_ref, peers_ref, total_ref, mine_sem, peer_sem = take(5)
    local_sem, load_sem, pair_sem, add_sem, ring_sem, side_sem = refs
    dp, z = lax.axis_index("dp"), lax.axis_index("seq")
    x, core = dp // 2, dp % 2
    nodes = 2 * stages
    here = z + x * (nodes - 1 - 2 * z)

    def place(r):
        rx = r // stages
        return rx, r + rx * (nodes - 1 - 2 * r)

    def peer(r):
        rx, rz = place(r % nodes)
        return {"dp": 2 * rx + core, "seq": rz}

    right, left, side = peer(here + 1), peer(here + nodes - 1), {"dp": 2 * x + 1 - core, "seq": z}
    ways = ((0, right, -1), (1, left, 1))
    mp, mp_count = lax.axis_index("mp"), peers_ref.shape[0] + 1
    mates = [{"mp": (mp + d) % mp_count} for d in range(1, mp_count)]

    def half_index(split, shape, part):
        size = shape[split] // 2
        cut = pl.ds(part * size, size)
        return (cut, slice(None)) if split == 0 else (slice(None), cut)

    loads = []
    for g, parts in enumerate(part_refs):
        for i, ref in enumerate(parts):
            for part in range(2):
                cut = half_index(splits[g], ref.shape[1:], part)
                copy = pltpu.make_async_copy(ref.at[(slice(None),) + cut], lates[g].at[:, part, i], load_sem.at[len(loads)])
                copy.start()
                loads.append(copy)

    barrier = pltpu.get_barrier_semaphore()
    known = [left, right, side] + mates
    for device in known:
        pl.semaphore_signal(barrier, inc=1, device_id=device, device_id_type=pl.DeviceIdType.MESH)
    pl.semaphore_wait(barrier, len(known))

    def remote(src, dst, sems, device):
        return pltpu.make_async_remote_copy(
            src_ref=src,
            dst_ref=dst,
            send_sem=sems.at[0],
            recv_sem=sems.at[1],
            device_id=device,
            device_id_type=pl.DeviceIdType.MESH,
        )

    def node(r):
        rx, rz = place((r + 2 * nodes) % nodes)
        return rx * stages + rz

    def number(r):
        rx, rz = place((r + 2 * nodes) % nodes)
        return (2 * rx + core) * stages + rz

    early_entries, late_entries = [], []
    for source, out in zip(share_refs, early_outs):
        size = source.shape[0] // 2
        early_entries.append(
            (
                lambda part, source=source, size=size: source.at[pl.ds(part * size, size)],
                lambda r, part, out=out, size=size: out.at[number(r), pl.ds(part * size, size)],
            )
        )
    for g, group in enumerate(groups):
        at = 0
        for n, out in zip(group, late_outs[g]):
            late_entries.append(
                (
                    lambda part, g=g, at=at, n=n: accs[g].at[node(here), part, pl.ds(at, n)],
                    lambda r, part, out=out, n=n, g=g: out.at[
                        (pl.ds(0, n), number(r)) + half_index(splits[g], out.shape[2:], part)
                    ],
                )
            )
            at += n
    sends = []

    def gather_step(i, entry, k):
        own, piece = entry
        arriving = []
        for part, device, sign in ways:
            dst = piece(here + sign * k, part)
            src = own(part) if k == 0 else dst
            if k < nodes - 1:
                copy = remote(src, dst, ring_sem.at[i, k, part], device)
                copy.start()
                sends.append((copy, False))
                arriving.append(copy)
            across = remote(src, dst, side_sem.at[i, k, part], side)
            across.start()
            sends.append((across, True))
        return arriving

    def keep_own(i, entry):
        own, piece = entry
        for part in range(2):
            copy = pltpu.make_async_copy(own(part), piece(here, part), local_sem.at[i, part])
            copy.start()
            locals_.append(copy)

    def early_step(k):
        arriving = []
        for i, entry in enumerate(early_entries):
            arriving += gather_step(i, entry, k)
        return arriving

    def add_into(total, other):
        total[...] = (total[...].astype(jnp.float32) + other[...].astype(jnp.float32)).astype(jnp.bfloat16)

    locals_ = []
    for copy in loads:
        copy.wait()
    pairs = []
    for g in range(len(groups)):
        for rx in range(2):
            copy = remote(
                lates[g].at[pl.ds((2 * rx + 1 - core) * stages, stages)],
                accs[g].at[pl.ds(rx * stages, stages)],
                pair_sem.at[g, rx],
                side,
            )
            copy.start()
            pairs.append(copy)
    swaps = []
    for d, device in enumerate(mates):
        copy = remote(grads_ref.at[:, :, (mp + d + 1) % mp_count], peers_ref.at[d], peer_sem.at[d], device)
        copy.start()
        swaps.append(copy)
    mine = pltpu.make_async_copy(grads_ref.at[:, :, mp], mine_ref, mine_sem.at[0])
    mine.start()
    batch, reach, own_rows = mine_ref.shape[:3]
    piece_rows = math.gcd(own_rows, 32)

    def sum_grads():
        mine.wait()
        for copy in swaps:
            copy.wait_recv()

        @pl.loop(0, batch * reach)
        def _(i):
            b, step = i // reach, i % reach
            for j in range(0, own_rows, piece_rows):
                cut = pl.ds(j, piece_rows)
                total = mine_ref[b, step, cut, :].astype(jnp.float32)
                for d in range(mp_count - 1):
                    total = total + peers_ref[d, b, step, cut, :].astype(jnp.float32)
                total_ref[b, step, cut, :] = total

        copy = pltpu.make_async_copy(total_ref, grad_out, mine_sem.at[1])
        copy.start()
        locals_.append(copy)

    waiting = early_step(0)
    for i, entry in enumerate(early_entries):
        keep_own(i, entry)
    for copy in pairs:
        copy.wait_recv()
    for g in range(len(groups)):
        members = accs[g].shape[2]

        @pl.loop(0, nodes * 2 * members)
        def _(j, g=g, members=members):
            to, part, i = j // (2 * members), (j // members) % 2, j % members
            own = (2 * (to // stages) + core) * stages + to % stages
            add_into(accs[g].at[to, part, i], lates[g].at[own, part, i])

    for k in range(nodes - 1):
        adding = []
        for g in range(len(groups)):
            for part, device, sign in ways:
                copy = remote(
                    accs[g].at[node(here + sign * (1 + k)), part], landings[g].at[k, part], add_sem.at[g, k, part], device
                )
                copy.start()
                sends.append((copy, False))
                adding.append(copy)
        for g in range(len(groups)):
            for part, _, sign in ways:
                adding[2 * g + part].wait_recv()
                to = node(here + sign * (2 + k))
                for i in range(accs[g].shape[2]):
                    add_into(accs[g].at[to, part, i], landings[g].at[k, part, i])
        for copy in waiting:
            copy.wait_recv()
        waiting = early_step(k + 1)
        if k == nodes - 2:
            sum_grads()

    for i, entry in enumerate(late_entries):
        keep_own(count + i, entry)
    for k in range(nodes):
        waiting = []
        for i, entry in enumerate(late_entries):
            waiting += gather_step(count + i, entry, k)
        for copy in waiting:
            copy.wait_recv()
    for copy in pairs + swaps:
        copy.wait_send()
    for copy, both in sends:
        copy.wait_send()
        if both:
            copy.wait_recv()
    for copy in locals_:
        copy.wait()


def finish_sums(partials, splits, shares, grads):
    stages, mp_count = lax.axis_size("seq"), lax.axis_size("mp")
    nodes = 2 * stages
    count = len(shares)
    groups = [[len(members) for members in group] for group in partials]
    flat = [[part for members in group for part in members] for group in partials]
    shapes = [(group[0].shape[0] // (2 * nodes), group[0].shape[1]) for group in flat]
    batch, reach, _, own_rows, model = grads.shape
    outs = [
        jax.ShapeDtypeStruct((n, 2 * nodes) + shape, jnp.bfloat16)
        for group, shape in zip(groups, shapes)
        for n in group
    ] + [jax.ShapeDtypeStruct((2 * nodes,) + share.shape, share.dtype) for share in shares]
    total = len(outs)
    outs.append(jax.ShapeDtypeStruct((batch, reach, own_rows, model), jnp.float32))
    anywhere = pl.BlockSpec(memory_space=pl.ANY)
    dma = pltpu.SemaphoreType.DMA
    scratch = lambda n: [
        pltpu.VMEM(
            n + (sum(group), rows // (2 - split), width // (1 + split)), jnp.bfloat16
        )
        for group, split, (rows, width) in zip(groups, splits, shapes)
    ]
    arrays = [part.reshape(2 * nodes, shape[0], shape[1]) for group, shape in zip(flat, shapes) for part in group]
    held = lambda *shape: pltpu.VMEM(shape + (own_rows, model), jnp.bfloat16)
    return pl.pallas_call(
        functools.partial(ring_kernel, stages, groups, splits, count),
        in_specs=[anywhere] * (len(arrays) + count + 1),
        out_specs=[anywhere] * (total + 1),
        out_shape=outs,
        scratch_shapes=scratch((2 * nodes, 2))
        + scratch((nodes, 2))
        + scratch((nodes - 1, 2))
        + [
            held(batch, reach),
            held(mp_count - 1, batch, reach),
            pltpu.VMEM((batch, reach, own_rows, model), jnp.float32),
            dma((2,)),
            dma((mp_count - 1, 2)),
            dma((total, 2)),
            dma((2 * len(arrays),)),
            dma((len(groups), 2, 2)),
            dma((len(groups), nodes - 1, 2, 2)),
            dma((total, nodes - 1, 2, 2)),
            dma((total, nodes, 2, 2)),
        ],
        compiler_params=pltpu.CompilerParams(
            collective_id=0, has_side_effects=True, vmem_limit_bytes=RING_VMEM
        ),
        cost_estimate=pl.CostEstimate(flops=0, bytes_accessed=600 * 1024 * 1024, transcendentals=0),
        name="finish_sums",
    )(*arrays, *shares, grads)


def relay_kernel(block, in_ref, out_ref):
    hidden = in_ref.shape[2]
    for t in range(2):
        values = in_ref[:, t, :]
        for j in range(hidden // block):
            out_ref[:, (2 * j + t) * block : (2 * j + t + 1) * block] = values[:, j * block : (j + 1) * block]


def relay_rows(w_in, block, part):
    model, _, hidden = w_in.shape
    rows = math.gcd(model // 2, 128)
    steps = model // 2 // rows
    return pl.pallas_call(
        functools.partial(relay_kernel, block),
        grid=(steps,),
        in_specs=[pl.BlockSpec((rows, 2, hidden), lambda i: (part * steps + i, 0, 0))],
        out_specs=pl.BlockSpec((rows, 2 * hidden), lambda i: (i, 0)),
        out_shape=jax.ShapeDtypeStruct((model // 2, 2 * hidden), jnp.bfloat16),
        compiler_params=pltpu.CompilerParams(vmem_limit_bytes=24 * 1024 * 1024),
        cost_estimate=pl.CostEstimate(flops=0, bytes_accessed=4 * model * hidden, transcendentals=0),
        name="relay_rows",
    )(w_in)


def feed_forward_kernel(h2_ref, gy_ref, upper_ref, lower_ref, wd_ref, hidden_ref, back_ref, in_ref, turned_ref, acc_ref):
    step, steps = pl.program_id(0), pl.num_programs(0)
    block = wd_ref.shape[0]
    half = upper_ref.shape[0]

    @pl.when(step == 0)
    def _():
        turned_ref[...] = h2_ref[...].T
        acc_ref[...] = jnp.zeros(acc_ref.shape, jnp.float32)

    gate_up = dot(h2_ref[:, :half], upper_ref[...]) + dot(h2_ref[:, half:], lower_ref[...])
    gate, upward = gate_up[:, :block], gate_up[:, block:]
    sigma = 1.0 / (1.0 + jnp.exp(-gate))
    silu_gate = gate * sigma
    hidden_ref[...] = (silu_gate * upward).astype(jnp.bfloat16)
    grad_hidden = dot(gy_ref[...], wd_ref[...], CONTRACT_LAST)
    grad_gate = grad_hidden * upward * sigma * (1.0 + gate * (1.0 - sigma))
    grads = jnp.concatenate([grad_gate, grad_hidden * silu_gate], axis=1).astype(jnp.bfloat16)
    in_ref[...] = dot(turned_ref[...], grads).astype(jnp.bfloat16)
    acc_ref[:, :half] += dot(grads, upper_ref[...], CONTRACT_LAST)
    acc_ref[:, half:] += dot(grads, lower_ref[...], CONTRACT_LAST)

    @pl.when(step == steps - 1)
    def _():
        back_ref[...] = acc_ref[...].astype(jnp.bfloat16)


def feed_forward(h2, gy, w_in, w_down, block):
    rows, model = h2.shape
    hidden = w_down.shape[0]
    whole = pl.BlockSpec((rows, model), lambda j: (0, 0))
    tall = pl.BlockSpec((model, 2 * block), lambda j: (0, j))
    part = pl.BlockSpec((model // 2, 2 * block), lambda j: (0, j))
    flat = pl.BlockSpec((block, model), lambda j: (j, 0))
    shape = lambda a, b: jax.ShapeDtypeStruct((a, b), jnp.bfloat16)
    return pl.pallas_call(
        feed_forward_kernel,
        grid=(hidden // block,),
        in_specs=[whole, whole, part, part, flat],
        out_specs=[pl.BlockSpec((rows, block), lambda j: (0, j)), whole, tall],
        out_shape=[shape(rows, hidden), shape(rows, model), shape(model, 2 * hidden)],
        scratch_shapes=[pltpu.VMEM((model, rows), jnp.bfloat16), pltpu.VMEM((rows, model), jnp.float32)],
        compiler_params=pltpu.CompilerParams(vmem_limit_bytes=VMEM_LIMIT),
        cost_estimate=pl.CostEstimate(
            flops=14 * rows * model * hidden, bytes_accessed=10 * model * hidden, transcendentals=rows * hidden
        ),
        name="feed_forward",
    )(h2, gy, *w_in, w_down)


def project_back_kernel(behind_rows, h1_ref, gq_ref, gk_ref, gv_ref, w_ref, pq_ref, pk_ref, pv_ref, gh_ref, gain_ref):
    groups, window = h1_ref.shape[:2]
    tall = gq_ref.shape[1]
    totals = None
    for g in range(groups):
        h1 = h1_ref[g]
        turned = h1.T
        parts = [
            dot(turned[:, window - tall :], gq_ref[g]),
            dot(turned, gk_ref[g]),
            dot(turned, gv_ref[g]),
        ]
        totals = parts if totals is None else [total + part for total, part in zip(totals, parts)]
        grad = dot(gk_ref[g], w_ref[1], CONTRACT_LAST) + dot(gv_ref[g], w_ref[2], CONTRACT_LAST)
        early = grad[: window - tall]
        late = grad[window - tall :] + dot(gq_ref[g], w_ref[0], CONTRACT_LAST)
        gh_ref[g, : window - tall, :] = early.astype(jnp.bfloat16)
        gh_ref[g, window - tall :, :] = late.astype(jnp.bfloat16)
        gain = jnp.sum(early * h1[: window - tall].astype(jnp.float32), axis=0, keepdims=True) + jnp.sum(
            late * h1[window - tall :].astype(jnp.float32), axis=0, keepdims=True
        )
        gain_ref[g : g + 1, :] = gain
    for ref, total in zip((pq_ref, pk_ref, pv_ref), totals):
        ref[...] = total.astype(jnp.bfloat16)


def project_back(h1, gq, gk, gv, weights, block):
    groups, window, model = h1.shape
    tall, width = gq.shape[1:]
    whole = lambda n: pl.BlockSpec((groups, n, width), lambda j: (0, 0, 0))
    cut = pl.BlockSpec((groups, window, block), lambda j: (0, 0, j))
    part = pl.BlockSpec((block, width), lambda j: (j, 0))
    return pl.pallas_call(
        functools.partial(project_back_kernel, window - tall),
        grid=(model // block,),
        in_specs=[cut, whole(tall), whole(window), whole(window), pl.BlockSpec((3, block, width), lambda j: (0, j, 0))],
        out_specs=[part, part, part, cut, pl.BlockSpec((groups, block), lambda j: (0, j))],
        out_shape=[jax.ShapeDtypeStruct((model, width), jnp.bfloat16)] * 3
        + [
            jax.ShapeDtypeStruct((groups, window, model), jnp.bfloat16),
            jax.ShapeDtypeStruct((groups, model), jnp.float32),
        ],
        compiler_params=pltpu.CompilerParams(vmem_limit_bytes=40 * 1024 * 1024),
        cost_estimate=pl.CostEstimate(
            flops=4 * groups * model * width * (2 * window + tall),
            bytes_accessed=4 * groups * window * (model + width) + 12 * model * width,
            transcendentals=0,
        ),
        name="project_back",
    )(h1, gq, gk, gv, weights)


def sum_peers(array):
    if lax.axis_size("mp") != 2:
        return lax.psum(array, "mp")
    return array + lax.ppermute(array, "mp", [(0, 1), (1, 0)])


def matmul(spec, lhs, rhs):
    return jnp.einsum(spec, lhs, rhs, preferred_element_type=jnp.float32)


def shards(
    block_input,
    segment,
    norm1_gain,
    w_qkv,
    conv_kernel,
    head_mix,
    out_gain,
    w_out,
    norm2_gain,
    w_in,
    w_down,
    grad_y,
):
    mp_count = lax.axis_size("mp")
    seq_count = lax.axis_size("seq")
    groups, own_rows, model = block_input.shape
    stretch = own_rows * mp_count
    rows = groups * stretch
    heads = conv_kernel.shape[0]
    local_width = w_qkv.shape[2]
    size = local_width // heads
    ff_local = w_down.shape[0]
    score_scale = size ** (-0.5)
    behind = min(-(-(LONGEST - 1) // stretch), seq_count - 1)
    window = (behind + 1) * stretch
    widths = tile_widths(window)
    flat = lambda array: array.reshape((rows,) + array.shape[2:])
    grouped = lambda array: array.reshape((groups, stretch) + array.shape[1:])

    seq_start = lax.axis_index("seq") * stretch
    ids = segment[:, 0]
    padded_ids = jnp.pad(ids, ((0, 0), (window - stretch, 0)), constant_values=-1)
    key_ids = lax.dynamic_slice_in_dim(padded_ids, seq_start, window, 1)
    key_pos = seq_start - (window - stretch) + jnp.arange(window, dtype=jnp.int32)
    ext_ids = jnp.pad(ids, ((0, 0), (RIM, 0)), constant_values=-2)
    ext_ids = lax.dynamic_slice_in_dim(ext_ids, seq_start, stretch + RIM, 1)
    ext_pos = seq_start - RIM + jnp.arange(stretch + RIM, dtype=jnp.int32)
    row_ids = jax.vmap(lambda v: spread_rows(v[:RIM], v[RIM:]))(ext_ids)
    row_pos = spread_rows(ext_pos[:RIM], ext_pos[RIM:])
    col_ids = spread_keys(key_ids, 1, -1)
    col_pos = spread_keys(key_pos, 0, 1 << 20)
    valid = (col_pos[None, None, :] <= row_pos[None, :, None]) & (
        row_ids[:, :, None] == col_ids[:, None, :]
    )
    own_cols = jnp.asarray(own_columns(window))
    mask = valid.astype(jnp.bfloat16)
    bias = jnp.where(valid[:, RIM * LANES :] & own_cols[None, None, :], 0.0, -jnp.inf)
    taps, taps_back = band_matrices(conv_kernel, score_scale)
    tall = LANES + stretch
    spot = jnp.arange(tall, dtype=jnp.int32)
    row_order = spread_rows(spot[LANES - RIM : LANES], spot[LANES:])
    pick_rows = (row_order[:, None] == spot[None, :]).astype(jnp.bfloat16)
    pick_plain = pick_rows[RIM * LANES :, LANES:]
    key_order = spread_keys(jnp.arange(window, dtype=jnp.int32), 0, -1)
    pick_cols = (key_order[:, None] == jnp.arange(window, dtype=jnp.int32)[None, :]).astype(jnp.bfloat16)
    picks = [pick_rows, pick_cols, pick_plain]

    input_float = block_input.astype(jnp.float32)
    inverse_one = inverse_rms(input_float)
    normed_one = input_float * inverse_one
    share = (normed_one * norm1_gain).astype(jnp.bfloat16)
    h1_blocks = [gather_rows(share)]
    for step in range(behind):
        share = from_behind(share, "seq", 1)
        if step:
            h1_blocks[-1], share = lax.optimization_barrier((h1_blocks[-1], share))
        h1_blocks.append(gather_rows(share))
    h1_blocks[-1], grad_rows = lax.optimization_barrier((h1_blocks[-1], grad_y))
    grad_full = flat(gather_rows(grad_rows))
    w_q, w_k, w_v = w_qkv[:, 0], w_qkv[:, 1], w_qkv[:, 2]
    h1_all = jnp.concatenate(h1_blocks[::-1], axis=1)
    h1_ext = h1_all[:, window - tall :]
    project = lambda block, weight: matmul("grd,dc->grc", block, weight).astype(jnp.bfloat16)
    queries, keys, values = project(h1_ext, w_q), project(h1_all, w_k), project(h1_all, w_v)
    gain_row = out_gain.reshape(1, local_width)
    mixed_out, probs, maps, att, q_heads, k_heads, v_heads = attend(
        queries, keys, values, taps, mask, bias, head_mix, gain_row, picks, heads, widths
    )
    mixed_out, grad_full = lax.optimization_barrier((flat(mixed_out), grad_full))
    branch = grouped(matmul("rc,cd->rd", mixed_out, w_out).astype(jnp.bfloat16))
    block = min(512, ff_local)
    branch, w_in_late = lax.optimization_barrier((branch, w_in))
    w_in_parts = [relay_rows(w_in_late, block, 0)]
    branch = scatter_rows(branch)
    branch, w_in_parts[0], w_in_late = lax.optimization_barrier((branch, w_in_parts[0], w_in_late))
    w_in_parts.append(relay_rows(w_in_late, block, 1))
    resid = input_float + branch
    inverse_two = inverse_rms(resid)
    normed_two = resid * inverse_two
    h2 = flat(gather_rows((normed_two * norm2_gain).astype(jnp.bfloat16)))
    hidden, back_part, part_in = feed_forward(h2, grad_full, w_in_parts, w_down, block)
    share_in = scatter_tokens(part_in)
    part_down = matmul("rf,rd->fd", hidden, grad_full).astype(jnp.bfloat16)
    mlp_part = matmul("rf,fd->rd", hidden, w_down).astype(jnp.bfloat16)

    grad_float = grad_y.astype(jnp.float32)
    grad_h2 = scatter_rows(grouped(back_part))
    part_gain_two = jnp.sum(grad_h2 * normed_two, axis=(0, 1))
    grad_resid = grad_float + norm_back(grad_h2, normed_two, inverse_two, norm2_gain)

    branch_grad = flat(gather_rows(grad_resid.astype(jnp.bfloat16)))
    part_out = matmul("rc,rd->cd", mixed_out, branch_grad).astype(jnp.bfloat16)
    grad_mixed = grouped(matmul("rd,cd->rc", branch_grad, w_out))
    grad_mixed, part_down, mlp_part = lax.optimization_barrier((grad_mixed, part_down, mlp_part))
    output = (resid + scatter_rows(grouped(mlp_part))).astype(jnp.bfloat16)
    grad_q, grad_k, grad_v, tap_sums, mix_sums, gain_sums = attend_back(
        grad_mixed, att, probs, maps, q_heads, k_heads, v_heads, taps_back, mask, head_mix, gain_row, picks,
        tall, window, widths,
    )
    part_gain_out = gain_sums[0]
    bands = jnp.concatenate([tap_sums[..., TILE - HALF :], tap_sums[..., : HALF + 8]], axis=3)
    part_kernel = score_scale * sum(bands[:, :, i, i : i + KTAPS] for i in range(8))[..., ::-1]
    part_mix = mix_sums[:, :4, 0].reshape(heads, 2)
    part_q, part_k, part_v, grad_h1_all, gain_rows = project_back(
        h1_all, grad_q, grad_k, grad_v, jnp.swapaxes(w_qkv, 0, 1), math.gcd(model, 256)
    )
    part_gain_one = jnp.sum(gain_rows, axis=0) / norm1_gain
    grad_blocks = grad_h1_all.reshape(groups, behind + 1, mp_count, own_rows, model)

    small = [part_gain_one, part_gain_two, part_kernel, part_mix, part_gain_out]
    share_in = share_in.reshape(-1, ff_local // block, 2, block // 128, 128)
    share_in = jnp.swapaxes(share_in, 2, 3).reshape(-1, 128)
    grad_qkv, grad_out, grad_down, grad_in, every, grad_blocks = finish_sums(
        [[[part_q, part_k, part_v]], [[part_out]], [[part_down]]], [0, 1, 0], [share_in, join_small(small)], grad_blocks
    )
    grad_qkv = jnp.swapaxes(grad_qkv.reshape(3, model, local_width), 0, 1).astype(jnp.float32)
    grad_out = grad_out.astype(jnp.float32).reshape(w_out.shape)
    grad_in = grad_in.astype(jnp.float32).reshape(model, ff_local // 128, 2, 128)
    grad_in = jnp.swapaxes(grad_in, 1, 2).reshape(w_in.shape)
    grad_down = grad_down.astype(jnp.float32).reshape(w_down.shape)
    grad_h1 = grad_blocks[:, 0]
    for step in range(1, behind + 1):
        grad_h1 = from_behind(grad_h1.astype(jnp.bfloat16), "seq", -1).astype(jnp.float32) + grad_blocks[:, step]
    grad_input = grad_resid + norm_back(grad_h1, normed_one, inverse_one, norm1_gain)

    gain_one, gain_two, grad_kernel, grad_mix, grad_gain_out = split_small(jnp.sum(every, axis=0), small)
    gain_sums = sum_peers(jnp.stack([gain_one, gain_two]))
    return (
        output,
        grad_input,
        gain_sums[0],
        grad_qkv,
        grad_kernel,
        grad_mix,
        grad_gain_out,
        grad_out,
        gain_sums[1],
        grad_in,
        grad_down,
    )


def solution(mesh):
    placed = (
        P(None, ("dp", "seq", "mp"), None),
        P(None, "dp", None),
        P(),
        P(None, None, "mp"),
        P("mp", None, None),
        P("mp", None),
        P("mp"),
        P("mp", None),
        P(),
        P(None, None, "mp"),
        P("mp", None),
        P(None, ("dp", "seq", "mp"), None),
    )
    return jax.shard_map(
        shards,
        mesh=mesh,
        in_specs=placed,
        out_specs=(
            P(None, ("dp", "seq", "mp"), None),
            P(None, ("dp", "seq", "mp"), None),
            P(),
            P(None, None, "mp"),
            P("mp", None, None),
            P("mp", None),
            P("mp"),
            P("mp", None),
            P(),
            P(None, None, "mp"),
            P("mp", None),
        ),
        check_vma=False,
    )
```

```python
import functools
import math

import jax
import jax.numpy as jnp
from jax import lax
from jax.experimental import pallas as pl
from jax.experimental.pallas import tpu as pltpu
from jax.sharding import PartitionSpec as P

QTAPS = 6
KTAPS = 11
LONGEST = 512
RIM = QTAPS - 1
HALF = KTAPS // 2
TILE = 256
OWN = TILE - 2 * HALF
LANES = 16

epsilon = 1e-05
VMEM_LIMIT = 58 * 1024 * 1024
RING_VMEM = 50 * 1024 * 1024


def from_behind(value, axis, steps):
    count = lax.axis_size(axis)
    first, last = (max(0, -steps), min(count, count - steps))
    return lax.ppermute(value, axis, [(source, source + steps) for source in range(first, last)])


def inverse_rms(values):
    return lax.rsqrt(jnp.mean(values * values, axis=-1, keepdims=True) + epsilon)


def norm_back(upstream, normed, inverse, gain):
    scaled = upstream * gain
    return inverse * (scaled - normed * jnp.mean(scaled * normed, axis=-1, keepdims=True))


def tile_widths(window):
    widths, left = [], window
    while left > 0:
        width = TILE
        while width > 128 and left <= width // 2 - 2 * HALF:
            width //= 2
        widths.append(width)
        left -= width - 2 * HALF
    return widths


def tile_starts(window):
    starts, at = [], 0
    for width in tile_widths(window):
        starts.append(at)
        at += width - 2 * HALF
    return starts


def spread_keys(array, axis, fill=0):
    window = array.shape[axis]
    widths, starts = tile_widths(window), tile_starts(window)
    pads = [(0, 0)] * array.ndim
    pads[axis] = (HALF, starts[-1] + widths[-1] - HALF - window)
    padded = jnp.pad(array, pads, constant_values=fill)
    return jnp.concatenate(
        [lax.slice_in_dim(padded, s, s + w, axis=axis) for s, w in zip(starts, widths)], axis=axis
    )


def own_columns(window):
    own = []
    for s, w in zip(tile_starts(window), tile_widths(window)):
        own += [HALF <= c < w - HALF and s + c - HALF < window for c in range(w)]
    return own


def spread_rows(rim, rows):
    steps = rows.shape[0] // LANES
    rest = rows.shape[1:]
    ahead = jnp.zeros((steps - RIM,) + rest, rows.dtype)
    blocks = jnp.concatenate([ahead, rim.astype(rows.dtype), rows]).reshape((LANES + 1, steps) + rest)
    ext = jnp.concatenate([blocks[:LANES, steps - RIM :], blocks[1:]], axis=1)
    return jnp.swapaxes(ext, 0, 1).reshape(((steps + RIM) * LANES,) + rest)


def taps_kernel(fwd_ref, bwd_ref, t_ref, tt_ref):
    for source, target in ((fwd_ref, t_ref), (bwd_ref, tt_ref)):
        for a in range(QTAPS):
            row = jnp.broadcast_to(source[0, a : a + 1, :], (TILE, TILE))
            turned = pltpu.roll(row, 0, 1, stride=1, stride_axis=0)
            target[0, a * TILE : (a + 1) * TILE, :] = turned.astype(jnp.bfloat16)


def band_matrices(conv_kernel, scale):
    heads = conv_kernel.shape[0]
    taps = conv_kernel * scale
    gap = jnp.zeros((heads, QTAPS, TILE - KTAPS), jnp.float32)
    fwd = jnp.concatenate([taps[:, :, HALF:], gap, taps[:, :, :HALF]], axis=2)
    flipped = taps[:, :, ::-1]
    bwd = jnp.concatenate([flipped[:, :, HALF:], gap, flipped[:, :, :HALF]], axis=2)
    big = jax.ShapeDtypeStruct((heads, QTAPS * TILE, TILE), jnp.bfloat16)
    small_spec = pl.BlockSpec((1, QTAPS, TILE), lambda h: (h, 0, 0))
    big_spec = pl.BlockSpec((1, QTAPS * TILE, TILE), lambda h: (h, 0, 0))
    return pl.pallas_call(
        taps_kernel,
        grid=(heads,),
        in_specs=[small_spec, small_spec],
        out_specs=[big_spec, big_spec],
        out_shape=[big, big],
        compiler_params=pltpu.CompilerParams(vmem_limit_bytes=RING_VMEM),
        name="band_matrices",
    )(fwd, bwd)


def band(ref, h, w):
    if w == TILE:
        return ref[h]
    return jnp.concatenate([ref[h, a * TILE : a * TILE + w, :w] for a in range(QTAPS)], axis=0)


CONTRACT_LAST = (((1,), (1,)), ((), ()))
CONTRACT_FIRST = (((0,), (0,)), ((), ()))


def dot(lhs, rhs, dims=(((1,), (0,)), ((), ()))):
    return lax.dot_general(lhs, rhs, dims, preferred_element_type=jnp.float32)


def attend_kernel(
    widths, q_ref, k_ref, v_ref, t_ref, mask_ref, bias_ref, mix_ref, gain_ref, rows_ref, cols_ref, plain_ref,
    o_ref, p_ref, m_ref, att_ref, qs_ref, ks_ref, vs_ref,
    logit_ref, mixed_ref,
):
    heads, rows = p_ref.shape[0], p_ref.shape[1]
    size = q_ref.shape[1] // heads
    chunk = min(rows, 64)
    first = pl.program_id(0) * heads
    for source, pick, target in ((q_ref, rows_ref, qs_ref), (k_ref, cols_ref, ks_ref), (v_ref, cols_ref, vs_ref)):
        moved = dot(pick[...], source[...]).astype(jnp.bfloat16)
        for h in range(heads):
            target[h] = moved[:, h * size : (h + 1) * size]
    for h in range(heads):
        at = 0
        for w in widths:
            s = dot(qs_ref[h], ks_ref[h, at : at + w, :], CONTRACT_LAST)
            m_ref[h, :, at : at + w] = s.astype(jnp.bfloat16) * mask_ref[:, at : at + w]
            at += w
        at = 0
        for w in widths:
            lhs = jnp.concatenate(
                [m_ref[h, (RIM - a) * LANES : (RIM - a) * LANES + rows, at : at + w] for a in range(QTAPS)], axis=1
            )
            logit_ref[:, at : at + w] = dot(lhs, band(t_ref, h, w)) + bias_ref[:, at : at + w]
            at += w
        for r in range(0, rows, chunk):
            logits = logit_ref[r : r + chunk, :]
            powers = jnp.exp(logits - jnp.max(logits, axis=-1, keepdims=True))
            p_ref[h, r : r + chunk, :] = powers * (1.0 / jnp.sum(powers, axis=-1, keepdims=True))
    outs = []
    for h in range(heads):
        low = h - h % 2
        w0, w1 = mix_ref[first + h, 0], mix_ref[first + h, 1]
        for r in range(0, rows, chunk):
            mixed_ref[r : r + chunk, :] = (
                w0 * p_ref[low, r : r + chunk, :] + w1 * p_ref[low + 1, r : r + chunk, :]
            ).astype(jnp.bfloat16)
        att = dot(mixed_ref[...], vs_ref[h])
        att_ref[h] = att
        outs.append(att * inverse_rms(att))
    normed = (jnp.concatenate(outs, axis=1) * gain_ref[...]).astype(jnp.bfloat16)
    o_ref[...] = dot(plain_ref[...], normed, CONTRACT_FIRST).astype(jnp.bfloat16)


def together(heads):
    return 4 if heads % 4 == 0 else heads


def attend(q, k, v, t, mask, bias, head_mix, gain, picks, heads, widths):
    groups, tall, width = q.shape
    window = k.shape[1]
    size = width // heads
    ext, cols = mask.shape[1:]
    rows = bias.shape[1]
    some = together(heads)
    natural = lambda n: pl.BlockSpec((None, n, some * size), lambda g, n: (n, 0, g))
    per_head = lambda a, b: pl.BlockSpec((None, some, a, b), lambda g, n: (n, g, 0, 0))
    whole = lambda a, b: pl.BlockSpec((None, a, b), lambda g, n: (n, 0, 0))
    fixed = lambda array: pl.BlockSpec(array.shape, lambda g, n: (0, 0))
    stacked = lambda a, b, kind: jax.ShapeDtypeStruct((groups, heads, a, b), kind)
    return pl.pallas_call(
        functools.partial(attend_kernel, widths),
        grid=(heads // some, groups),
        in_specs=[
            natural(tall),
            natural(window),
            natural(window),
            pl.BlockSpec((some, QTAPS * TILE, TILE), lambda g, n: (g, 0, 0)),
            whole(ext, cols),
            whole(rows, cols),
            pl.BlockSpec(memory_space=pltpu.SMEM),
            pl.BlockSpec((1, some * size), lambda g, n: (0, g)),
        ]
        + [fixed(pick) for pick in picks],
        out_specs=[
            natural(rows),
            per_head(rows, cols),
            per_head(ext, cols),
            per_head(rows, size),
            per_head(ext, size),
            per_head(cols, size),
            per_head(cols, size),
        ],
        out_shape=[
            jax.ShapeDtypeStruct((groups, rows, width), jnp.bfloat16),
            stacked(rows, cols, jnp.float32),
            stacked(ext, cols, jnp.bfloat16),
            stacked(rows, size, jnp.float32),
            stacked(ext, size, jnp.bfloat16),
            stacked(cols, size, jnp.bfloat16),
            stacked(cols, size, jnp.bfloat16),
        ],
        scratch_shapes=[pltpu.VMEM((rows, cols), jnp.float32), pltpu.VMEM((rows, cols), jnp.bfloat16)],
        compiler_params=pltpu.CompilerParams(vmem_limit_bytes=VMEM_LIMIT),
        cost_estimate=pl.CostEstimate(
            flops=2 * groups * heads * rows * cols * (QTAPS * TILE + 3 * size),
            bytes_accessed=groups * heads * cols * (4 * rows + 2 * ext) + heads * QTAPS * TILE * TILE * 2,
            transcendentals=groups * heads * rows * cols,
        ),
        name="attend",
    )(q, k, v, t, mask, bias, head_mix, gain, *picks)


def attend_back_kernel(
    widths, go_ref, att_ref, p_ref, m_ref, q_ref, k_ref, v_ref, tt_ref, mask_ref, mix_ref, gain_ref,
    rows_ref, cols_ref, plain_ref,
    gq_ref, gk_ref, gv_ref, tap_ref, gmix_ref, ggain_ref,
    ga_ref, gpm_ref, mixed_ref, gc_ref, gs_ref, gqs_ref, gks_ref, gvs_ref,
):
    heads, rows, cols = p_ref.shape
    ext, size = q_ref.shape[1:]
    chunk = min(rows, 64)
    first = pl.program_id(0) * heads
    rim = RIM * LANES

    @pl.when(pl.program_id(1) == 0)
    def _():
        gmix_ref[...] = jnp.zeros(gmix_ref.shape, jnp.float32)
        tap_ref[...] = jnp.zeros(tap_ref.shape, jnp.float32)
        ggain_ref[...] = jnp.zeros(ggain_ref.shape, jnp.float32)

    upper = go_ref[...].astype(jnp.bfloat16)
    lower = (go_ref[...] - upper.astype(jnp.float32)).astype(jnp.bfloat16)
    grad_o = dot(plain_ref[...], upper) + dot(plain_ref[...], lower)
    gains = []
    for h in range(heads):
        att = att_ref[h]
        inverse = inverse_rms(att)
        normed = att * inverse
        grad = grad_o[:, h * size : (h + 1) * size]
        gains.append(jnp.sum(grad * normed, axis=0, keepdims=True))
        ga_ref[h] = norm_back(grad, normed, inverse, gain_ref[:, h * size : (h + 1) * size]).astype(jnp.bfloat16)
    ggain_ref[0:1, :] += jnp.concatenate(gains, axis=1)

    gc_ref[:, :rim, :] = jnp.zeros((2, rim, cols), jnp.bfloat16)
    gc_ref[:, rim + rows :, :] = jnp.zeros((2, rim, cols), jnp.bfloat16)
    for low in range(0, heads, 2):
        mix = [[mix_ref[first + low + o, t] for t in range(2)] for o in range(2)]
        for o in range(2):
            for r in range(0, rows, chunk):
                mixed_ref[r : r + chunk, :] = (
                    mix[o][0] * p_ref[low, r : r + chunk, :] + mix[o][1] * p_ref[low + 1, r : r + chunk, :]
                ).astype(jnp.bfloat16)
            grad = dot(ga_ref[low + o], mixed_ref[...], CONTRACT_FIRST)
            gvs_ref[(low + o) * size : (low + o + 1) * size, :] = grad.astype(jnp.bfloat16)
            gpm_ref[o] = dot(ga_ref[low + o], v_ref[low + o], CONTRACT_LAST)
        sums = [[jnp.zeros((1, 1), jnp.float32) for t in range(2)] for o in range(2)]
        for r in range(0, rows, chunk):
            for t in range(2):
                probs = p_ref[low + t, r : r + chunk, :]
                ups = [gpm_ref[o, r : r + chunk, :] for o in range(2)]
                dots = [jnp.sum(probs * up, axis=-1, keepdims=True) for up in ups]
                for o in range(2):
                    sums[o][t] = sums[o][t] + jnp.sum(dots[o], axis=0, keepdims=True)
                down = mix[0][t] * dots[0] + mix[1][t] * dots[1]
                grad = probs * (mix[0][t] * ups[0] + mix[1][t] * ups[1] - down)
                gc_ref[t, rim + r : rim + r + chunk, :] = grad.astype(jnp.bfloat16)
        for o in range(2):
            for t in range(2):
                gmix_ref[low // 2, 2 * o + t : 2 * o + t + 1, :] += jnp.broadcast_to(sums[o][t], (1, 128))
        for t in range(2):
            h = low + t
            at = 0
            for w in widths:
                lhs = jnp.concatenate(
                    [gc_ref[t, a * LANES : a * LANES + ext, at : at + w] for a in range(QTAPS)], axis=1
                )
                back = dot(lhs, band(tt_ref, h, w))
                gs_ref[:, at : at + w] = back.astype(jnp.bfloat16) * mask_ref[:, at : at + w]
                at += w
            gqs_ref[:, h * size : (h + 1) * size] = dot(gs_ref[...], k_ref[h]).astype(jnp.bfloat16)
            gks_ref[h * size : (h + 1) * size, :] = dot(q_ref[h], gs_ref[...], CONTRACT_FIRST).astype(jnp.bfloat16)
            for width in sorted(set(widths)):
                spans, at = [], 0
                for w in widths:
                    if w == width:
                        spans.append(at)
                    at += w
                turned = jnp.concatenate(
                    [gc_ref[t, rim : rim + rows, at : at + width].T for at in spans], axis=1
                )
                for a in range(QTAPS):
                    start = (RIM - a) * LANES
                    maps = jnp.concatenate(
                        [m_ref[h, start : start + rows, at : at + width] for at in spans], axis=0
                    )
                    cross = dot(turned, maps)
                    total = cross[:8]
                    for r in range(8, width, 8):
                        total = total + pltpu.roll(cross[r : r + 8], width - r, 1)
                    tap_ref[h, a, :, :128] += total[:, :128]
                    tap_ref[h, a, :, 128:] += total[:, width - 128 :]
    gq_ref[...] = dot(rows_ref[...], gqs_ref[...], CONTRACT_FIRST).astype(jnp.bfloat16)
    gk_ref[...] = dot(cols_ref[...], gks_ref[...], (((0,), (1,)), ((), ()))).astype(jnp.bfloat16)
    gv_ref[...] = dot(cols_ref[...], gvs_ref[...], (((0,), (1,)), ((), ()))).astype(jnp.bfloat16)


def attend_back(go, att, p, m, q, k, v, tt, mask, head_mix, gain, picks, tall, window, widths):
    groups, heads, ext, size = q.shape
    rows, cols = p.shape[2:]
    width = heads * size
    some = together(heads)
    natural = lambda n: pl.BlockSpec((None, n, some * size), lambda g, n: (n, 0, g))
    per_head = lambda a, b: pl.BlockSpec((None, some, a, b), lambda g, n: (n, g, 0, 0))
    fixed = lambda array: pl.BlockSpec(array.shape, lambda g, n: (0, 0))
    moved = lambda n: jax.ShapeDtypeStruct((groups, n, width), jnp.bfloat16)
    return pl.pallas_call(
        functools.partial(attend_back_kernel, widths),
        grid=(heads // some, groups),
        in_specs=[
            natural(rows),
            per_head(rows, size),
            per_head(rows, cols),
            per_head(ext, cols),
            per_head(ext, size),
            per_head(cols, size),
            per_head(cols, size),
            pl.BlockSpec((some, QTAPS * TILE, TILE), lambda g, n: (g, 0, 0)),
            pl.BlockSpec((None, ext, cols), lambda g, n: (n, 0, 0)),
            pl.BlockSpec(memory_space=pltpu.SMEM),
            pl.BlockSpec((1, some * size), lambda g, n: (0, g)),
        ]
        + [fixed(pick) for pick in picks],
        out_specs=[
            natural(tall),
            natural(window),
            natural(window),
            pl.BlockSpec((some, QTAPS, 8, TILE), lambda g, n: (g, 0, 0, 0)),
            pl.BlockSpec((some // 2, 8, 128), lambda g, n: (g, 0, 0)),
            pl.BlockSpec((8, some * size), lambda g, n: (0, g)),
        ],
        out_shape=[
            moved(tall),
            moved(window),
            moved(window),
            jax.ShapeDtypeStruct((heads, QTAPS, 8, TILE), jnp.float32),
            jax.ShapeDtypeStruct((heads // 2, 8, 128), jnp.float32),
            jax.ShapeDtypeStruct((8, width), jnp.float32),
        ],
        scratch_shapes=[
            pltpu.VMEM((some, rows, size), jnp.bfloat16),
            pltpu.VMEM((2, rows, cols), jnp.float32),
            pltpu.VMEM((rows, cols), jnp.bfloat16),
            pltpu.VMEM((2, rows + 2 * RIM * LANES, cols), jnp.bfloat16),
            pltpu.VMEM((ext, cols), jnp.bfloat16),
            pltpu.VMEM((ext, some * size), jnp.bfloat16),
            pltpu.VMEM((some * size, cols), jnp.bfloat16),
            pltpu.VMEM((some * size, cols), jnp.bfloat16),
        ],
        compiler_params=pltpu.CompilerParams(vmem_limit_bytes=VMEM_LIMIT),
        cost_estimate=pl.CostEstimate(
            flops=2 * groups * heads * rows * cols * (2 * QTAPS * TILE + 5 * size),
            bytes_accessed=groups * heads * cols * (4 * rows + 2 * ext) + heads * QTAPS * TILE * TILE * 2,
            transcendentals=0,
        ),
        name="attend_back",
    )(go, att, p, m, q, k, v, tt, mask, head_mix, gain, *picks)


def gather_rows(array):
    if lax.axis_size("mp") != 2:
        return lax.all_gather(array, "mp", axis=1, tiled=True)
    other = lax.ppermute(array, "mp", [(0, 1), (1, 0)])
    first = lax.axis_index("mp") == 0
    return jnp.concatenate([jnp.where(first, array, other), jnp.where(first, other, array)], axis=1)


def scatter_rows(array, after=None):
    count = lax.axis_size("mp")
    own = array.shape[1] // count
    if count != 2:
        return lax.psum_scatter(array, "mp", scatter_dimension=1, tiled=True).astype(jnp.float32)
    first = lax.axis_index("mp") == 0
    head, tail = array[:, :own], array[:, own:]
    arrived = lax.ppermute(jnp.where(first, tail, head), "mp", [(0, 1), (1, 0)])
    if after is not None:
        arrived, _ = lax.optimization_barrier((arrived, after))
    return jnp.where(first, head, tail).astype(jnp.float32) + arrived.astype(jnp.float32)


def join_small(parts):
    lanes, tile = 128, 16
    joined = jnp.concatenate([part.reshape(-1) for part in parts])
    rows = -(-joined.size // (tile * lanes)) * tile
    return jnp.pad(joined, (0, rows * lanes - joined.size)).reshape(rows, lanes)


def split_small(joined, parts):
    flat, result, at = joined.reshape(-1), [], 0
    for part in parts:
        result.append(flat[at : at + part.size].reshape(part.shape))
        at += part.size
    return result


def scatter_tokens(part):
    part = part.astype(jnp.bfloat16)
    return lax.psum_scatter(part, ("dp", "seq"), scatter_dimension=0, tiled=True)


def ring_kernel(stages, groups, splits, count, *refs):
    refs = list(refs)
    take = lambda n: [refs.pop(0) for _ in range(n)]
    part_refs = [take(sum(group)) for group in groups]
    share_refs = take(count)
    (grads_ref,) = take(1)
    late_outs = [take(len(group)) for group in groups]
    early_outs = take(count)
    (grad_out,) = take(1)
    lates, accs, landings = take(len(groups)), take(len(groups)), take(len(groups))
    mine_ref, peers_ref, total_ref, mine_sem, peer_sem = take(5)
    local_sem, load_sem, pair_sem, add_sem, ring_sem, side_sem = refs
    dp, z = lax.axis_index("dp"), lax.axis_index("seq")
    x, core = dp // 2, dp % 2
    nodes = 2 * stages
    here = z + x * (nodes - 1 - 2 * z)

    def place(r):
        rx = r // stages
        return rx, r + rx * (nodes - 1 - 2 * r)

    def peer(r):
        rx, rz = place(r % nodes)
        return {"dp": 2 * rx + core, "seq": rz}

    right, left, side = peer(here + 1), peer(here + nodes - 1), {"dp": 2 * x + 1 - core, "seq": z}
    ways = ((0, right, -1), (1, left, 1))
    mp, mp_count = lax.axis_index("mp"), peers_ref.shape[0] + 1
    mates = [{"mp": (mp + d) % mp_count} for d in range(1, mp_count)]

    def half_index(split, shape, part):
        size = shape[split] // 2
        cut = pl.ds(part * size, size)
        return (cut, slice(None)) if split == 0 else (slice(None), cut)

    loads = []
    for g, parts in enumerate(part_refs):
        for i, ref in enumerate(parts):
            for part in range(2):
                cut = half_index(splits[g], ref.shape[1:], part)
                copy = pltpu.make_async_copy(ref.at[(slice(None),) + cut], lates[g].at[:, part, i], load_sem.at[len(loads)])
                copy.start()
                loads.append(copy)

    barrier = pltpu.get_barrier_semaphore()
    known = [left, right, side] + mates
    for device in known:
        pl.semaphore_signal(barrier, inc=1, device_id=device, device_id_type=pl.DeviceIdType.MESH)
    pl.semaphore_wait(barrier, len(known))

    def remote(src, dst, sems, device):
        return pltpu.make_async_remote_copy(
            src_ref=src,
            dst_ref=dst,
            send_sem=sems.at[0],
            recv_sem=sems.at[1],
            device_id=device,
            device_id_type=pl.DeviceIdType.MESH,
        )

    def node(r):
        rx, rz = place((r + 2 * nodes) % nodes)
        return rx * stages + rz

    def number(r):
        rx, rz = place((r + 2 * nodes) % nodes)
        return (2 * rx + core) * stages + rz

    early_entries, late_entries = [], []
    for source, out in zip(share_refs, early_outs):
        size = source.shape[0] // 2
        early_entries.append(
            (
                lambda part, source=source, size=size: source.at[pl.ds(part * size, size)],
                lambda r, part, out=out, size=size: out.at[number(r), pl.ds(part * size, size)],
            )
        )
    for g, group in enumerate(groups):
        at = 0
        for n, out in zip(group, late_outs[g]):
            late_entries.append(
                (
                    lambda part, g=g, at=at, n=n: accs[g].at[node(here), part, pl.ds(at, n)],
                    lambda r, part, out=out, n=n, g=g: out.at[
                        (pl.ds(0, n), number(r)) + half_index(splits[g], out.shape[2:], part)
                    ],
                )
            )
            at += n
    sends = []

    def gather_step(i, entry, k):
        own, piece = entry
        arriving = []
        for part, device, sign in ways:
            dst = piece(here + sign * k, part)
            src = own(part) if k == 0 else dst
            if k < nodes - 1:
                copy = remote(src, dst, ring_sem.at[i, k, part], device)
                copy.start()
                sends.append((copy, False))
                arriving.append(copy)
            across = remote(src, dst, side_sem.at[i, k, part], side)
            across.start()
            sends.append((across, True))
        return arriving

    def keep_own(i, entry):
        own, piece = entry
        for part in range(2):
            copy = pltpu.make_async_copy(own(part), piece(here, part), local_sem.at[i, part])
            copy.start()
            locals_.append(copy)

    def early_step(k):
        arriving = []
        for i, entry in enumerate(early_entries):
            arriving += gather_step(i, entry, k)
        return arriving

    def add_into(total, other):
        total[...] = (total[...].astype(jnp.float32) + other[...].astype(jnp.float32)).astype(jnp.bfloat16)

    locals_ = []
    for copy in loads:
        copy.wait()
    pairs = []
    for g in range(len(groups)):
        for rx in range(2):
            copy = remote(
                lates[g].at[pl.ds((2 * rx + 1 - core) * stages, stages)],
                accs[g].at[pl.ds(rx * stages, stages)],
                pair_sem.at[g, rx],
                side,
            )
            copy.start()
            pairs.append(copy)
    swaps = []
    for d, device in enumerate(mates):
        copy = remote(grads_ref.at[:, :, (mp + d + 1) % mp_count], peers_ref.at[d], peer_sem.at[d], device)
        copy.start()
        swaps.append(copy)
    mine = pltpu.make_async_copy(grads_ref.at[:, :, mp], mine_ref, mine_sem.at[0])
    mine.start()
    batch, reach, own_rows = mine_ref.shape[:3]
    piece_rows = math.gcd(own_rows, 32)

    def sum_grads():
        mine.wait()
        for copy in swaps:
            copy.wait_recv()

        @pl.loop(0, batch * reach)
        def _(i):
            b, step = i // reach, i % reach
            for j in range(0, own_rows, piece_rows):
                cut = pl.ds(j, piece_rows)
                total = mine_ref[b, step, cut, :].astype(jnp.float32)
                for d in range(mp_count - 1):
                    total = total + peers_ref[d, b, step, cut, :].astype(jnp.float32)
                total_ref[b, step, cut, :] = total

        copy = pltpu.make_async_copy(total_ref, grad_out, mine_sem.at[1])
        copy.start()
        locals_.append(copy)

    waiting = early_step(0)
    for i, entry in enumerate(early_entries):
        keep_own(i, entry)
    for copy in pairs:
        copy.wait_recv()
    for g in range(len(groups)):
        members = accs[g].shape[2]

        @pl.loop(0, nodes * 2 * members)
        def _(j, g=g, members=members):
            to, part, i = j // (2 * members), (j // members) % 2, j % members
            own = (2 * (to // stages) + core) * stages + to % stages
            add_into(accs[g].at[to, part, i], lates[g].at[own, part, i])

    for k in range(nodes - 1):
        adding = []
        for g in range(len(groups)):
            for part, device, sign in ways:
                copy = remote(
                    accs[g].at[node(here + sign * (1 + k)), part], landings[g].at[k, part], add_sem.at[g, k, part], device
                )
                copy.start()
                sends.append((copy, False))
                adding.append(copy)
        for g in range(len(groups)):
            for part, _, sign in ways:
                adding[2 * g + part].wait_recv()
                to = node(here + sign * (2 + k))
                for i in range(accs[g].shape[2]):
                    add_into(accs[g].at[to, part, i], landings[g].at[k, part, i])
        for copy in waiting:
            copy.wait_recv()
        waiting = early_step(k + 1)
        if k == nodes - 2:
            sum_grads()

    for i, entry in enumerate(late_entries):
        keep_own(count + i, entry)
    for k in range(nodes):
        waiting = []
        for i, entry in enumerate(late_entries):
            waiting += gather_step(count + i, entry, k)
        for copy in waiting:
            copy.wait_recv()
    for copy in pairs + swaps:
        copy.wait_send()
    for copy, both in sends:
        copy.wait_send()
        if both:
            copy.wait_recv()
    for copy in locals_:
        copy.wait()


def finish_sums(partials, splits, shares, grads):
    stages, mp_count = lax.axis_size("seq"), lax.axis_size("mp")
    nodes = 2 * stages
    count = len(shares)
    groups = [[len(members) for members in group] for group in partials]
    flat = [[part for members in group for part in members] for group in partials]
    shapes = [(group[0].shape[0] // (2 * nodes), group[0].shape[1]) for group in flat]
    batch, reach, _, own_rows, model = grads.shape
    outs = [
        jax.ShapeDtypeStruct((n, 2 * nodes) + shape, jnp.bfloat16)
        for group, shape in zip(groups, shapes)
        for n in group
    ] + [jax.ShapeDtypeStruct((2 * nodes,) + share.shape, share.dtype) for share in shares]
    total = len(outs)
    outs.append(jax.ShapeDtypeStruct((batch, reach, own_rows, model), jnp.float32))
    anywhere = pl.BlockSpec(memory_space=pl.ANY)
    dma = pltpu.SemaphoreType.DMA
    scratch = lambda n: [
        pltpu.VMEM(
            n + (sum(group), rows // (2 - split), width // (1 + split)), jnp.bfloat16
        )
        for group, split, (rows, width) in zip(groups, splits, shapes)
    ]
    arrays = [part.reshape(2 * nodes, shape[0], shape[1]) for group, shape in zip(flat, shapes) for part in group]
    held = lambda *shape: pltpu.VMEM(shape + (own_rows, model), jnp.bfloat16)
    return pl.pallas_call(
        functools.partial(ring_kernel, stages, groups, splits, count),
        in_specs=[anywhere] * (len(arrays) + count + 1),
        out_specs=[anywhere] * (total + 1),
        out_shape=outs,
        scratch_shapes=scratch((2 * nodes, 2))
        + scratch((nodes, 2))
        + scratch((nodes - 1, 2))
        + [
            held(batch, reach),
            held(mp_count - 1, batch, reach),
            pltpu.VMEM((batch, reach, own_rows, model), jnp.float32),
            dma((2,)),
            dma((mp_count - 1, 2)),
            dma((total, 2)),
            dma((2 * len(arrays),)),
            dma((len(groups), 2, 2)),
            dma((len(groups), nodes - 1, 2, 2)),
            dma((total, nodes - 1, 2, 2)),
            dma((total, nodes, 2, 2)),
        ],
        compiler_params=pltpu.CompilerParams(
            collective_id=0, has_side_effects=True, vmem_limit_bytes=RING_VMEM
        ),
        cost_estimate=pl.CostEstimate(flops=0, bytes_accessed=600 * 1024 * 1024, transcendentals=0),
        name="finish_sums",
    )(*arrays, *shares, grads)


def relay_kernel(block, in_ref, out_ref):
    hidden = in_ref.shape[2]
    for t in range(2):
        values = in_ref[:, t, :]
        for j in range(hidden // block):
            out_ref[:, (2 * j + t) * block : (2 * j + t + 1) * block] = values[:, j * block : (j + 1) * block]


def relay_rows(w_in, block, part):
    model, _, hidden = w_in.shape
    rows = math.gcd(model // 2, 128)
    steps = model // 2 // rows
    return pl.pallas_call(
        functools.partial(relay_kernel, block),
        grid=(steps,),
        in_specs=[pl.BlockSpec((rows, 2, hidden), lambda i: (part * steps + i, 0, 0))],
        out_specs=pl.BlockSpec((rows, 2 * hidden), lambda i: (i, 0)),
        out_shape=jax.ShapeDtypeStruct((model // 2, 2 * hidden), jnp.bfloat16),
        compiler_params=pltpu.CompilerParams(vmem_limit_bytes=10 * 1024 * 1024),
        cost_estimate=pl.CostEstimate(flops=0, bytes_accessed=4 * model * hidden, transcendentals=0),
        name="relay_rows",
    )(w_in)


def feed_forward_kernel(h2_ref, gy_ref, upper_ref, lower_ref, wd_ref, hidden_ref, back_ref, in_ref, turned_ref, acc_ref):
    step, steps = pl.program_id(0), pl.num_programs(0)
    block = wd_ref.shape[0]
    half = upper_ref.shape[0]

    @pl.when(step == 0)
    def _():
        turned_ref[...] = h2_ref[...].T
        acc_ref[...] = jnp.zeros(acc_ref.shape, jnp.float32)

    gate_up = dot(h2_ref[:, :half], upper_ref[...]) + dot(h2_ref[:, half:], lower_ref[...])
    gate, upward = gate_up[:, :block], gate_up[:, block:]
    sigma = 1.0 / (1.0 + jnp.exp(-gate))
    silu_gate = gate * sigma
    hidden_ref[...] = (silu_gate * upward).astype(jnp.bfloat16)
    grad_hidden = dot(gy_ref[...], wd_ref[...], CONTRACT_LAST)
    grad_gate = grad_hidden * upward * sigma * (1.0 + gate * (1.0 - sigma))
    grads = jnp.concatenate([grad_gate, grad_hidden * silu_gate], axis=1).astype(jnp.bfloat16)
    in_ref[...] = dot(turned_ref[...], grads).astype(jnp.bfloat16)
    acc_ref[:, :half] += dot(grads, upper_ref[...], CONTRACT_LAST)
    acc_ref[:, half:] += dot(grads, lower_ref[...], CONTRACT_LAST)

    @pl.when(step == steps - 1)
    def _():
        back_ref[...] = acc_ref[...].astype(jnp.bfloat16)


def feed_forward(h2, gy, w_in, w_down, block):
    rows, model = h2.shape
    hidden = w_down.shape[0]
    whole = pl.BlockSpec((rows, model), lambda j: (0, 0))
    tall = pl.BlockSpec((model, 2 * block), lambda j: (0, j))
    part = pl.BlockSpec((model // 2, 2 * block), lambda j: (0, j))
    flat = pl.BlockSpec((block, model), lambda j: (j, 0))
    shape = lambda a, b: jax.ShapeDtypeStruct((a, b), jnp.bfloat16)
    return pl.pallas_call(
        feed_forward_kernel,
        grid=(hidden // block,),
        in_specs=[whole, whole, part, part, flat],
        out_specs=[pl.BlockSpec((rows, block), lambda j: (0, j)), whole, tall],
        out_shape=[shape(rows, hidden), shape(rows, model), shape(model, 2 * hidden)],
        scratch_shapes=[pltpu.VMEM((model, rows), jnp.bfloat16), pltpu.VMEM((rows, model), jnp.float32)],
        compiler_params=pltpu.CompilerParams(vmem_limit_bytes=48 * 1024 * 1024),
        cost_estimate=pl.CostEstimate(
            flops=14 * rows * model * hidden, bytes_accessed=10 * model * hidden, transcendentals=rows * hidden
        ),
        name="feed_forward",
    )(h2, gy, *w_in, w_down)


def project_back_kernel(behind_rows, h1_ref, gq_ref, gk_ref, gv_ref, w_ref, pq_ref, pk_ref, pv_ref, gh_ref, gain_ref):
    groups, window = h1_ref.shape[:2]
    tall = gq_ref.shape[1]
    totals = None
    for g in range(groups):
        h1 = h1_ref[g]
        turned = h1.T
        parts = [
            dot(turned[:, window - tall :], gq_ref[g]),
            dot(turned, gk_ref[g]),
            dot(turned, gv_ref[g]),
        ]
        totals = parts if totals is None else [total + part for total, part in zip(totals, parts)]
        grad = dot(gk_ref[g], w_ref[1], CONTRACT_LAST) + dot(gv_ref[g], w_ref[2], CONTRACT_LAST)
        early = grad[: window - tall]
        late = grad[window - tall :] + dot(gq_ref[g], w_ref[0], CONTRACT_LAST)
        gh_ref[g, : window - tall, :] = early.astype(jnp.bfloat16)
        gh_ref[g, window - tall :, :] = late.astype(jnp.bfloat16)
        gain = jnp.sum(early * h1[: window - tall].astype(jnp.float32), axis=0, keepdims=True) + jnp.sum(
            late * h1[window - tall :].astype(jnp.float32), axis=0, keepdims=True
        )
        gain_ref[g : g + 1, :] = gain
    for ref, total in zip((pq_ref, pk_ref, pv_ref), totals):
        ref[...] = total.astype(jnp.bfloat16)


def project_back(h1, gq, gk, gv, weights, block):
    groups, window, model = h1.shape
    tall, width = gq.shape[1:]
    whole = lambda n: pl.BlockSpec((groups, n, width), lambda j: (0, 0, 0))
    cut = pl.BlockSpec((groups, window, block), lambda j: (0, 0, j))
    part = pl.BlockSpec((block, width), lambda j: (j, 0))
    return pl.pallas_call(
        functools.partial(project_back_kernel, window - tall),
        grid=(model // block,),
        in_specs=[cut, whole(tall), whole(window), whole(window), pl.BlockSpec((3, block, width), lambda j: (0, j, 0))],
        out_specs=[part, part, part, cut, pl.BlockSpec((groups, block), lambda j: (0, j))],
        out_shape=[jax.ShapeDtypeStruct((model, width), jnp.bfloat16)] * 3
        + [
            jax.ShapeDtypeStruct((groups, window, model), jnp.bfloat16),
            jax.ShapeDtypeStruct((groups, model), jnp.float32),
        ],
        compiler_params=pltpu.CompilerParams(vmem_limit_bytes=40 * 1024 * 1024),
        cost_estimate=pl.CostEstimate(
            flops=4 * groups * model * width * (2 * window + tall),
            bytes_accessed=4 * groups * window * (model + width) + 12 * model * width,
            transcendentals=0,
        ),
        name="project_back",
    )(h1, gq, gk, gv, weights)


def sum_peers(array):
    if lax.axis_size("mp") != 2:
        return lax.psum(array, "mp")
    return array + lax.ppermute(array, "mp", [(0, 1), (1, 0)])


def matmul(spec, lhs, rhs):
    return jnp.einsum(spec, lhs, rhs, preferred_element_type=jnp.float32)


def shards(
    block_input,
    segment,
    norm1_gain,
    w_qkv,
    conv_kernel,
    head_mix,
    out_gain,
    w_out,
    norm2_gain,
    w_in,
    w_down,
    grad_y,
):
    mp_count = lax.axis_size("mp")
    seq_count = lax.axis_size("seq")
    groups, own_rows, model = block_input.shape
    stretch = own_rows * mp_count
    rows = groups * stretch
    heads = conv_kernel.shape[0]
    local_width = w_qkv.shape[2]
    size = local_width // heads
    ff_local = w_down.shape[0]
    score_scale = size ** (-0.5)
    behind = min(-(-(LONGEST - 1) // stretch), seq_count - 1)
    window = (behind + 1) * stretch
    widths = tile_widths(window)
    flat = lambda array: array.reshape((rows,) + array.shape[2:])
    grouped = lambda array: array.reshape((groups, stretch) + array.shape[1:])

    seq_start = lax.axis_index("seq") * stretch
    ids = segment[:, 0]
    padded_ids = jnp.pad(ids, ((0, 0), (window - stretch, 0)), constant_values=-1)
    key_ids = lax.dynamic_slice_in_dim(padded_ids, seq_start, window, 1)
    key_pos = seq_start - (window - stretch) + jnp.arange(window, dtype=jnp.int32)
    ext_ids = jnp.pad(ids, ((0, 0), (RIM, 0)), constant_values=-2)
    ext_ids = lax.dynamic_slice_in_dim(ext_ids, seq_start, stretch + RIM, 1)
    ext_pos = seq_start - RIM + jnp.arange(stretch + RIM, dtype=jnp.int32)
    row_ids = jax.vmap(lambda v: spread_rows(v[:RIM], v[RIM:]))(ext_ids)
    row_pos = spread_rows(ext_pos[:RIM], ext_pos[RIM:])
    col_ids = spread_keys(key_ids, 1, -1)
    col_pos = spread_keys(key_pos, 0, 1 << 20)
    valid = (col_pos[None, None, :] <= row_pos[None, :, None]) & (
        row_ids[:, :, None] == col_ids[:, None, :]
    )
    own_cols = jnp.asarray(own_columns(window))
    mask = valid.astype(jnp.bfloat16)
    bias = jnp.where(valid[:, RIM * LANES :] & own_cols[None, None, :], 0.0, -jnp.inf)
    taps, taps_back = band_matrices(conv_kernel, score_scale)
    tall = LANES + stretch
    spot = jnp.arange(tall, dtype=jnp.int32)
    row_order = spread_rows(spot[LANES - RIM : LANES], spot[LANES:])
    pick_rows = (row_order[:, None] == spot[None, :]).astype(jnp.bfloat16)
    pick_plain = pick_rows[RIM * LANES :, LANES:]
    key_order = spread_keys(jnp.arange(window, dtype=jnp.int32), 0, -1)
    pick_cols = (key_order[:, None] == jnp.arange(window, dtype=jnp.int32)[None, :]).astype(jnp.bfloat16)
    picks = [pick_rows, pick_cols, pick_plain]

    input_float = block_input.astype(jnp.float32)
    inverse_one = inverse_rms(input_float)
    normed_one = input_float * inverse_one
    share = (normed_one * norm1_gain).astype(jnp.bfloat16)
    h1_blocks = [gather_rows(share)]
    for step in range(behind):
        share = from_behind(share, "seq", 1)
        if step:
            h1_blocks[-1], share = lax.optimization_barrier((h1_blocks[-1], share))
        h1_blocks.append(gather_rows(share))
    h1_blocks[-1], grad_rows = lax.optimization_barrier((h1_blocks[-1], grad_y))
    grad_full = flat(gather_rows(grad_rows))
    w_q, w_k, w_v = w_qkv[:, 0], w_qkv[:, 1], w_qkv[:, 2]
    h1_all = jnp.concatenate(h1_blocks[::-1], axis=1)
    h1_ext = h1_all[:, window - tall :]
    project = lambda block, weight: matmul("grd,dc->grc", block, weight).astype(jnp.bfloat16)
    queries, keys, values = project(h1_ext, w_q), project(h1_all, w_k), project(h1_all, w_v)
    gain_row = out_gain.reshape(1, local_width)
    mixed_out, probs, maps, att, q_heads, k_heads, v_heads = attend(
        queries, keys, values, taps, mask, bias, head_mix, gain_row, picks, heads, widths
    )
    mixed_out, grad_full = lax.optimization_barrier((flat(mixed_out), grad_full))
    branch = grouped(matmul("rc,cd->rd", mixed_out, w_out).astype(jnp.bfloat16))
    block = min(512, ff_local)
    branch, w_in_late = lax.optimization_barrier((branch, w_in))
    w_in_parts = [relay_rows(w_in_late, block, 0)]
    branch = scatter_rows(branch)
    branch, w_in_parts[0], w_in_late = lax.optimization_barrier((branch, w_in_parts[0], w_in_late))
    w_in_parts.append(relay_rows(w_in_late, block, 1))
    resid = input_float + branch
    inverse_two = inverse_rms(resid)
    normed_two = resid * inverse_two
    h2 = flat(gather_rows((normed_two * norm2_gain).astype(jnp.bfloat16)))
    hidden, back_part, part_in = feed_forward(h2, grad_full, w_in_parts, w_down, block)
    share_in = scatter_tokens(part_in)
    part_down = matmul("rf,rd->fd", hidden, grad_full).astype(jnp.bfloat16)
    mlp_part = matmul("rf,fd->rd", hidden, w_down).astype(jnp.bfloat16)

    grad_float = grad_y.astype(jnp.float32)
    grad_h2 = scatter_rows(grouped(back_part))
    part_gain_two = jnp.sum(grad_h2 * normed_two, axis=(0, 1))
    grad_resid = grad_float + norm_back(grad_h2, normed_two, inverse_two, norm2_gain)

    branch_grad = flat(gather_rows(grad_resid.astype(jnp.bfloat16)))
    part_out = matmul("rc,rd->cd", mixed_out, branch_grad).astype(jnp.bfloat16)
    grad_mixed = grouped(matmul("rd,cd->rc", branch_grad, w_out))
    grad_mixed, part_down, mlp_part = lax.optimization_barrier((grad_mixed, part_down, mlp_part))
    output = (resid + scatter_rows(grouped(mlp_part))).astype(jnp.bfloat16)
    grad_q, grad_k, grad_v, tap_sums, mix_sums, gain_sums = attend_back(
        grad_mixed, att, probs, maps, q_heads, k_heads, v_heads, taps_back, mask, head_mix, gain_row, picks,
        tall, window, widths,
    )
    part_gain_out = gain_sums[0]
    bands = jnp.concatenate([tap_sums[..., TILE - HALF :], tap_sums[..., : HALF + 8]], axis=3)
    part_kernel = score_scale * sum(bands[:, :, i, i : i + KTAPS] for i in range(8))[..., ::-1]
    part_mix = mix_sums[:, :4, 0].reshape(heads, 2)
    part_q, part_k, part_v, grad_h1_all, gain_rows = project_back(
        h1_all, grad_q, grad_k, grad_v, jnp.swapaxes(w_qkv, 0, 1), math.gcd(model, 256)
    )
    part_gain_one = jnp.sum(gain_rows, axis=0) / norm1_gain
    grad_blocks = grad_h1_all.reshape(groups, behind + 1, mp_count, own_rows, model)

    small = [part_gain_one, part_gain_two, part_kernel, part_mix, part_gain_out]
    share_in = share_in.reshape(-1, ff_local // block, 2, block // 128, 128)
    share_in = jnp.swapaxes(share_in, 2, 3).reshape(-1, 128)
    grad_qkv, grad_out, grad_down, grad_in, every, grad_blocks = finish_sums(
        [[[part_q, part_k, part_v]], [[part_out]], [[part_down]]], [0, 1, 0], [share_in, join_small(small)], grad_blocks
    )
    grad_qkv = jnp.swapaxes(grad_qkv.reshape(3, model, local_width), 0, 1).astype(jnp.float32)
    grad_out = grad_out.astype(jnp.float32).reshape(w_out.shape)
    grad_in = grad_in.astype(jnp.float32).reshape(model, ff_local // 128, 2, 128)
    grad_in = jnp.swapaxes(grad_in, 1, 2).reshape(w_in.shape)
    grad_down = grad_down.astype(jnp.float32).reshape(w_down.shape)
    grad_h1 = grad_blocks[:, 0]
    for step in range(1, behind + 1):
        grad_h1 = from_behind(grad_h1.astype(jnp.bfloat16), "seq", -1).astype(jnp.float32) + grad_blocks[:, step]
    grad_input = grad_resid + norm_back(grad_h1, normed_one, inverse_one, norm1_gain)

    gain_one, gain_two, grad_kernel, grad_mix, grad_gain_out = split_small(jnp.sum(every, axis=0), small)
    gain_sums = sum_peers(jnp.stack([gain_one, gain_two]))
    return (
        output,
        grad_input,
        gain_sums[0],
        grad_qkv,
        grad_kernel,
        grad_mix,
        grad_gain_out,
        grad_out,
        gain_sums[1],
        grad_in,
        grad_down,
    )


def solution(mesh):
    placed = (
        P(None, ("dp", "seq", "mp"), None),
        P(None, "dp", None),
        P(),
        P(None, None, "mp"),
        P("mp", None, None),
        P("mp", None),
        P("mp"),
        P("mp", None),
        P(),
        P(None, None, "mp"),
        P("mp", None),
        P(None, ("dp", "seq", "mp"), None),
    )
    return jax.shard_map(
        shards,
        mesh=mesh,
        in_specs=placed,
        out_specs=(
            P(None, ("dp", "seq", "mp"), None),
            P(None, ("dp", "seq", "mp"), None),
            P(),
            P(None, None, "mp"),
            P("mp", None, None),
            P("mp", None),
            P("mp"),
            P("mp", None),
            P(),
            P(None, None, "mp"),
            P("mp", None),
        ),
        check_vma=False,
    )
```
